256 devices in a mesh: seq: 32 (over x, z), head: 8 (over y, core).
Axes of the slice: x: 4, y: 4, z: 8, core: 2. Of those that a mesh axis runs over, the one named last changes fastest.
Arguments:
- tokens: bfloat16 [16384, 2048], P('seq', 'head'), may hold values from -6 to 6
- weight_x: bfloat16 [2048, 4096], P(None, 'head'), may hold values from -0.125 to 0.125
- weight_z: bfloat16 [2048, 4096], P(None, 'head'), may hold values from -0.125 to 0.125
- weight_bc: bfloat16 [2048, 256], replicated, may hold values from -0.125 to 0.125
- weight_dt: bfloat16 [64, 2048], P('head'), may hold values from -0.125 to 0.125
- conv_x_weight: float32 [4, 4096], P(None, 'head'), may hold values from -3 to 3
- conv_x_bias: float32 [4096], P('head'), may hold values from -3 to 3
- conv_bc_weight: float32 [4, 256], replicated, may hold values from -3 to 3
- conv_bc_bias: float32 [256], replicated, may hold values from -3 to 3
- step_bias: float32 [64], P('head'), may hold values from -4.5 to -2.5
- decay_log: float32 [64], P('head')
- skip_gain: float32 [64], P('head'), may hold values from 0.5 to 1.5
- norm_gain: float32 [4096], P('head'), may hold values from 0.1 to 1.9
- lengths: int32 [8], replicated, may hold values from 1 to 8192, 16384 in all
- page_table: int32 [8], replicated, may hold values from 0 to 31, as said below
Outputs:
- normed: bfloat16 [16384, 4096], P('seq', 'head')
- ssm_pages: float32 [32, 64, 64, 128], P('seq', 'head')
- conv_x_pages: float32 [32, 3, 4096], P('seq', None, 'head')
- conv_bc_pages: float32 [32, 3, 256], P('seq')
The draws below stay inside these ranges and needn't reach their ends.
Inputs may be any that keep to these rules, and one draw needn't show every extreme that they name: The lengths sum to 16384, and the longest is exactly 8192. `page_table`: the pages of different prompts differ; the last prompt's page is 30.
All inputs are finite; a program needn't handle non-finite values.
Results may differ from the reference program's by a relative error of at most 0.015.
Values may be sent and summed in bfloat16 or wider, within the bound.
A program may use at most 64 MiB of HBM per device.

```python
import math
import jax
import jax.numpy as jnp
import numpy as np
from jax import lax

D = 2048
HEADS = 64
HEADDIM = 64
STATE = 128
CONV = 4
GROUP = 256
REQS = 8
INNER = 4096
TOKENS = 16384
MAXLEN = 8192
PAGES = 32


def draw_decay_log(key, part):
    key_kind, key_slow, key_fast = jax.random.split(jax.random.fold_in(key, 11), 3)
    slow_share = 0.5
    slow_heads = jax.random.bernoulli(key_kind, slow_share, (HEADS,))
    slow_rate = jnp.exp(jax.random.uniform(key_slow, (HEADS,), jnp.float32, jnp.log(0.3), jnp.log(2.0))) / (0.05 * MAXLEN)
    fast_rate = jnp.exp(jax.random.uniform(key_fast, (HEADS,), jnp.float32, jnp.log(1.0 / 50.0), jnp.log(1.0 / 30.0))) / 0.05
    return jnp.log(jnp.where(slow_heads, slow_rate, fast_rate)).astype(jnp.float32)


def draw_page_table(key, part):
    shuffled = jax.random.permutation(jax.random.fold_in(key, 23), PAGES).astype(jnp.int32)
    chosen = shuffled[:REQS]
    last_page = chosen[REQS - 1]
    target = jnp.int32(PAGES - 2)
    chosen = jnp.where(chosen == target, last_page, chosen)
    chosen = chosen.at[REQS - 1].set(target)
    return chosen.astype(jnp.int32)


def block_levels(stream_key, dims, cuts, low, largest):
    def one(axis_at, parts):
        heights = jax.random.uniform(jax.random.fold_in(jax.random.fold_in(stream_key, 6), axis_at), (parts,), jnp.float32, low / len(cuts), largest / len(cuts))
        return jnp.repeat(jnp.exp(heights), dims[axis_at] // parts).reshape((-1,) + (1,) * (len(dims) - axis_at - 1))

    gain = one(*cuts[0])
    for cut in cuts[1:]:
        gain = gain * one(*cut)
    return gain


def profile(count, total, reach, skew):
    weights = [(1 << 20) // math.isqrt(rank ** skew) + 1 for rank in range(2, count + 1)]
    surplus, given = total - reach - (count - 1), [1] * (count - 1)
    while surplus > 0:
        free = [i for i in range(count - 1) if given[i] < reach]
        mass, remaining = sum([weights[i] for i in free]), surplus
        for i in free:
            more = min(reach - given[i], max(1, remaining * weights[i] // mass), surplus)
            given[i] = given[i] + more
            surplus = surplus - more
    return np.array([reach] + given)


def ragged_sizes(own_key, count, total, bound, lean):
    if count == 2:
        one = jax.random.randint(own_key, (), max(1, total - bound), min(bound, total - 1) + 1)
        return jnp.stack([one, total - one])
    tallies = jnp.asarray(profile(count, total, bound, lean), jnp.int32)
    couples = (count - 1) // 2
    giver, receiver = tallies[1:1 + 2 * couples:2], tallies[2:2 + 2 * couples:2]
    margin = jnp.minimum(giver - 1, bound - receiver)
    moved = jax.random.randint(jax.random.fold_in(own_key, 1), (couples,), 0, 1 << 20) % (margin + 1)
    tallies = tallies.at[1:1 + 2 * couples:2].set(giver - moved).at[2:2 + 2 * couples:2].set(receiver + moved)
    return tallies[jax.random.permutation(jax.random.fold_in(own_key, 2), count)]


def normal_values(own_key, shape, deviation, most, pieces=(), held_as=jnp.bfloat16):
    drawn = deviation * jax.random.normal(own_key, shape, jnp.float32)
    if pieces:
        drawn = drawn * block_levels(own_key, shape, pieces, -0.22, 0.18)
    return jnp.clip(drawn, -most, most).astype(held_as)


def setup_inputs(seed: int = 0) -> dict:
    seeds = jax.random.split(jax.random.key(seed), 16)
    return {
        "tokens": normal_values(seeds[0], (TOKENS, D), 1.0, 6.0, ((0, 32), (1, 8))),
        "weight_x": normal_values(seeds[1], (D, INNER), D ** -0.5, 0.125, ((1, 8),)),
        "weight_z": normal_values(seeds[2], (D, INNER), D ** -0.5, 0.125, ((1, 8),)),
        "weight_bc": normal_values(seeds[3], (D, 2 * STATE), D ** -0.5, 0.125),
        "weight_dt": normal_values(seeds[4], (HEADS, D), D ** -0.5, 0.125, ((0, 8),)),
        "conv_x_weight": normal_values(seeds[5], (CONV, INNER), CONV ** -0.5, 3.0, ((1, 8),), jnp.float32),
        "conv_x_bias": normal_values(seeds[6], (INNER,), 0.5, 3.0, ((0, 8),), jnp.float32),
        "conv_bc_weight": normal_values(seeds[7], (CONV, 2 * STATE), CONV ** -0.5, 3.0, (), jnp.float32),
        "conv_bc_bias": normal_values(seeds[8], (2 * STATE,), 0.5, 3.0, (), jnp.float32),
        "step_bias": jnp.clip(-4.5 + 2.0 * jax.random.uniform(seeds[9], (HEADS,), jnp.float32) ** block_levels(seeds[9], (HEADS,), ((0, 8),), -0.2, 0.2), -4.5, -2.5),
        "decay_log": draw_decay_log(jax.random.fold_in(seeds[15], 71), 0),
        "skip_gain": jnp.clip(0.5 + 1.0 * jax.random.uniform(seeds[11], (HEADS,), jnp.float32) ** block_levels(seeds[11], (HEADS,), ((0, 8),), -0.2, 0.2), 0.5, 1.5),
        "norm_gain": jnp.clip(1.0 + 0.18 * jax.random.normal(seeds[12], (INNER,), jnp.float32), 0.1, 1.9),
        "lengths": ragged_sizes(seeds[13], REQS, TOKENS, MAXLEN, 2).astype(jnp.int32),
        "page_table": draw_page_table(jax.random.fold_in(seeds[15], 71), 0),
    }


norm_epsilon = 1e-05

def segment_of(starts, positions):
    return lax.optimization_barrier(jnp.sum((starts[None, :] <= positions[:, None]).astype(jnp.int32), axis=1)) - 1

def causal_conv(extended, conv_weight, conv_bias, segments_ext, count):
    tap_count = conv_weight.shape[0]
    own_segment = segments_ext[tap_count - 1:tap_count - 1 + count]
    running = jnp.zeros((count, extended.shape[1]), jnp.float32) + conv_bias[None, :]
    for tap_index in range(tap_count):
        same_prompt = (segments_ext[tap_index:tap_index + count] == own_segment)[:, None]
        running = running + jnp.where(same_prompt, extended[tap_index:tap_index + count].astype(jnp.float32) * conv_weight[tap_index][None, :], 0.0)
    return jax.nn.silu(running).astype(jnp.bfloat16)

def group_local(x_group, b_group, c_group, dt_group, la_group, seg_group, reset_group):
    length = x_group.shape[0]
    cumulative = jnp.cumsum(la_group, axis=1)
    position_index = jnp.arange(length)
    keep_mask = (position_index[:, None] >= position_index[None, :]) & (seg_group[:, None] == seg_group[None, :])
    gaps = jnp.where(keep_mask[None], cumulative[:, :, None] - cumulative[:, None, :], 0.0)
    decay_mask = jnp.where(keep_mask[None], jnp.exp(gaps), 0.0)
    scores = jnp.dot(c_group, b_group.T, preferred_element_type=jnp.float32)
    weights = (scores[None] * decay_mask).astype(jnp.bfloat16)
    x_values = x_group.astype(jnp.float32)
    x_scaled = (dt_group.T[:, :, None] * x_values).astype(jnp.bfloat16)
    within = jnp.einsum('hij,jhp->ihp', weights.astype(jnp.float32), x_scaled.astype(jnp.float32))
    keep_last = seg_group == seg_group[length - 1]
    to_last = jnp.where(keep_last[None], jnp.exp(jnp.where(keep_last[None], cumulative[:, length - 1:] - cumulative, 0.0)), 0.0)
    x_weighted = ((to_last * dt_group).T[:, :, None] * x_values).astype(jnp.bfloat16)
    state_now = jnp.einsum('jhp,jn->hpn', x_weighted.astype(jnp.float32), b_group.astype(jnp.float32))
    unbroken = jnp.cumsum(reset_group.astype(jnp.int32)) == 0
    decay_rate = jnp.where(unbroken[length - 1], jnp.exp(cumulative[:, length - 1]), 0.0)
    inflow = jnp.where(unbroken[None, :], jnp.exp(cumulative), 0.0)
    return (within, state_now, decay_rate, inflow)

def final_state(x_group, b_group, dt_group, la_group, seg_group, reset_group, spot_index, entering):
    length = x_group.shape[0]
    cumulative = jnp.cumsum(la_group, axis=1)
    position_index = jnp.arange(length)
    keep_mask = (position_index <= spot_index) & (seg_group == seg_group[spot_index])
    cum_spot = cumulative[:, spot_index]
    to_spot = jnp.where(keep_mask[None], jnp.exp(jnp.where(keep_mask[None], cum_spot[:, None] - cumulative, 0.0)), 0.0)
    x_weighted = ((to_spot * dt_group).T[:, :, None] * x_group.astype(jnp.float32)).astype(jnp.bfloat16)
    from_group = jnp.einsum('jhp,jn->hpn', x_weighted.astype(jnp.float32), b_group.astype(jnp.float32))
    unbroken = jnp.cumsum(reset_group.astype(jnp.int32))[spot_index] == 0
    inflow_spot = jnp.where(unbroken, jnp.exp(cum_spot), 0.0)
    return from_group + inflow_spot[:, None, None] * entering

def reference(tokens, weight_x, weight_z, weight_bc, weight_dt, conv_x_weight, conv_x_bias, conv_bc_weight, conv_bc_bias, step_bias, decay_log, skip_gain, norm_gain, lengths, page_table):
    x_in = jnp.dot(tokens, weight_x, preferred_element_type=jnp.float32).astype(jnp.bfloat16)
    z_in = jnp.dot(tokens, weight_z, preferred_element_type=jnp.float32).astype(jnp.bfloat16)
    bc_in = jnp.dot(tokens, weight_bc, preferred_element_type=jnp.float32).astype(jnp.bfloat16)
    dt_raw = lax.dot_general(weight_dt, tokens, (((1,), (1,)), ((), ())), preferred_element_type=jnp.float32)
    starts = (jnp.cumsum(lengths) - lengths).astype(jnp.int32)
    prompt_ends = (starts + lengths - 1).astype(jnp.int32)
    positions = jnp.arange(TOKENS, dtype=jnp.int32)
    segments = segment_of(starts, positions)
    resets = jnp.any(starts[None, :] == positions[:, None], axis=1)
    ext_positions = jnp.arange(-(CONV - 1), TOKENS, dtype=jnp.int32)
    segments_ext = segment_of(starts, ext_positions)
    extended = jnp.concatenate([jnp.zeros((CONV - 1, INNER + 2 * STATE), jnp.bfloat16), jnp.concatenate([x_in, bc_in], axis=1)], axis=0)
    conv_weight = jnp.concatenate([conv_x_weight, conv_bc_weight], axis=1)
    conv_bias = jnp.concatenate([conv_x_bias, conv_bc_bias], axis=0)
    conv_out = causal_conv(extended, conv_weight, conv_bias, segments_ext, TOKENS)
    x_conv = conv_out[:, :INNER]
    b_conv = conv_out[:, INNER:INNER + STATE]
    c_conv = conv_out[:, INNER + STATE:]
    step_size = jax.nn.softplus(dt_raw + step_bias[:, None])
    log_decay = -step_size * jnp.exp(decay_log)[:, None]
    group_count = TOKENS // GROUP
    x_all = x_conv.reshape(group_count, GROUP, HEADS, HEADDIM)
    b_all = b_conv.reshape(group_count, GROUP, STATE)
    c_all = c_conv.reshape(group_count, GROUP, STATE)
    dt_all = step_size.reshape(HEADS, group_count, GROUP).transpose(1, 0, 2)
    la_all = log_decay.reshape(HEADS, group_count, GROUP).transpose(1, 0, 2)
    seg_all = segments.reshape(group_count, GROUP)
    reset_all = resets.reshape(group_count, GROUP)
    end_group = (prompt_ends // GROUP).astype(jnp.int32)
    spots = (prompt_ends % GROUP).astype(jnp.int32)

    def advance(carried, inputs):
        entering, chosen = carried
        x_group, b_group, c_group, dt_group, la_group, seg_group, reset_group, number = inputs
        within, state_now, decay_rate, inflow = group_local(x_group, b_group, c_group, dt_group, la_group, seg_group, reset_group)
        entering_low = lax.optimization_barrier(entering.astype(jnp.bfloat16)).astype(jnp.float32)
        across = jnp.einsum('in,hpn->ihp', c_group.astype(jnp.float32), entering_low) * inflow.T[:, :, None]
        ssd_out = (within + across + skip_gain[None, :, None] * x_group.astype(jnp.float32)).astype(jnp.bfloat16)
        chosen = jnp.where((end_group == number)[:, None, None, None], entering[None], chosen)
        return ((decay_rate[:, None, None] * entering + state_now, chosen), ssd_out)
    start_carry = (jnp.zeros((HEADS, HEADDIM, STATE), jnp.float32), jnp.zeros((REQS, HEADS, HEADDIM, STATE), jnp.float32))
    numbers = jnp.arange(group_count, dtype=jnp.int32)
    (_, chosen), outputs = lax.scan(advance, start_carry, (x_all, b_all, c_all, dt_all, la_all, seg_all, reset_all, numbers))
    ssd_flat = outputs.reshape(TOKENS, INNER)
    gated_out = ssd_flat.astype(jnp.float32) * jax.nn.silu(z_in.astype(jnp.float32))
    mean_square = lax.optimization_barrier(jnp.mean(gated_out * gated_out, axis=1, keepdims=True))
    normed = (gated_out * lax.rsqrt(mean_square + norm_epsilon) * norm_gain[None, :]).astype(jnp.bfloat16)
    finals = jax.vmap(final_state)(x_all[end_group], b_all[end_group], dt_all[end_group], la_all[end_group], seg_all[end_group], reset_all[end_group], spots, chosen)

    def conv_rows(end_here, owner):
        picked = lax.dynamic_slice_in_dim(extended, end_here + 1, CONV - 1, 0)
        picked_seg = lax.dynamic_slice_in_dim(segments_ext, end_here + 1, CONV - 1, 0)
        return jnp.where((picked_seg == owner)[:, None], picked.astype(jnp.float32), 0.0)
    kept_rows = jax.vmap(conv_rows)(prompt_ends, jnp.arange(REQS, dtype=jnp.int32))
    ssm_pages = jnp.zeros((PAGES, HEADS, HEADDIM, STATE), jnp.float32).at[page_table].set(finals)
    conv_x_pages = jnp.zeros((PAGES, CONV - 1, INNER), jnp.float32).at[page_table].set(kept_rows[:, :, :INNER])
    conv_bc_pages = jnp.zeros((PAGES, CONV - 1, 2 * STATE), jnp.float32).at[page_table].set(kept_rows[:, :, INNER:])
    return (normed, ssm_pages, conv_x_pages, conv_bc_pages)
```

```python
import functools

import jax
import jax.numpy as jnp
from jax import lax
from jax.experimental import pallas as pl
from jax.experimental.pallas import tpu as pltpu
from jax.sharding import PartitionSpec as P

MESH = pl.DeviceIdType.MESH
F32 = jnp.float32
BF16 = jnp.bfloat16
EPS = 1e-05
HALO = 16
LOG2E = 1.4426950408889634


def vmem():
    return pl.BlockSpec(memory_space=pltpu.VMEM)


def hbm():
    return pl.BlockSpec(memory_space=pl.ANY)


def smem():
    return pl.BlockSpec(memory_space=pltpu.SMEM)


def project_kernel(
    nseq, nhead,
    tok, wx, wz, wbc, wdt,
    u_out, z_out, dt_out,
    tokbuf, w, wdtp, acc, accdt,
    lsem, ssem, rsem, hs_sem, hr_sem,
):
    ny = nhead // 2
    seq = lax.axis_index("seq")
    head = lax.axis_index("head")
    y = head // 2
    core = head % 2
    rows, feat = tok.shape
    half = rows // 2
    inner = wx.shape[1]
    wide = wbc.shape[1]
    heads = wdt.shape[0]
    yp, ym = (y + 1) % ny, (y + ny - 1) % ny
    y2 = (y + 2) % ny
    up, down = yp * 2 + core, ym * 2 + core
    other = y * 2 + (1 - core)
    nxt, prv = (seq + 1) % nseq, (seq + nseq - 1) % nseq
    lanes = pl.ds(pl.multiple_of(core * feat, feat), feat)
    other_lanes = pl.ds(pl.multiple_of((1 - core) * feat, feat), feat)
    first, second = pl.ds(HALO, half), pl.ds(HALO + half, half)
    both = pl.ds(HALO, rows)
    edge = pl.ds(0, HALO)

    loads = [
        pltpu.make_async_copy(tok, tokbuf.at[y, both, lanes], lsem.at[0]),
        pltpu.make_async_copy(wx, w.at[:, pl.ds(0, inner)], lsem.at[1]),
        pltpu.make_async_copy(wbc, w.at[:, pl.ds(2 * inner, wide)], lsem.at[2]),
        pltpu.make_async_copy(wz, w.at[:, pl.ds(inner, inner)], lsem.at[3]),
        pltpu.make_async_copy(wdt, wdtp.at[pl.ds(0, heads)], lsem.at[4]),
    ]

    barrier = pltpu.get_barrier_semaphore()
    for k in range(1, nhead):
        pl.semaphore_signal(
            barrier, inc=1, device_id={"head": (head + k) % nhead}, device_id_type=MESH
        )
    pl.semaphore_signal(barrier, inc=1, device_id={"seq": nxt}, device_id_type=MESH)
    pl.semaphore_signal(barrier, inc=1, device_id={"seq": prv}, device_id_type=MESH)
    wdtp[pl.ds(heads, 128 - heads), :] = jnp.zeros((128 - heads, wdtp.shape[1]), BF16)
    for one in loads:
        one.start()
    pl.semaphore_wait(barrier, nhead + 1)

    sent = []

    def send(src, dst, number, to):
        copy = pltpu.make_async_remote_copy(
            src_ref=src, dst_ref=dst, send_sem=ssem.at[number], recv_sem=rsem.at[number],
            device_id=to, device_id_type=MESH,
        )
        copy.start()
        sent.append(copy)

    def arrive(region, number):
        pltpu.make_async_remote_copy(
            src_ref=region, dst_ref=region, send_sem=ssem.at[number], recv_sem=rsem.at[number],
            device_id={"head": other}, device_id_type=MESH,
        ).wait_recv()

    to_up, to_down, to_other = {"head": up}, {"head": down}, {"head": other}
    mine = tokbuf.at[y]
    send(tok.at[pl.ds(rows - HALO, HALO)], mine.at[edge, lanes], 13, {"seq": nxt})
    send(tok.at[pl.ds(0, half)], mine.at[first, lanes], 1, to_up)
    send(tok.at[pl.ds(half, half)], mine.at[second, lanes], 3, to_down)
    send(tok, mine.at[both, lanes], 0, to_other)
    send(tok.at[pl.ds(half, half)], mine.at[second, lanes], 2, to_up)
    send(tok.at[pl.ds(0, half)], mine.at[first, lanes], 4, to_down)

    def halo_piece(owner):
        return tokbuf.at[
            owner // 2, edge, pl.ds(pl.multiple_of((owner % 2) * feat, feat), feat)
        ]

    arrive(halo_piece(head), 13)
    halo_sends = []
    for k in range(1, nhead):
        copy = pltpu.make_async_remote_copy(
            src_ref=halo_piece(head), dst_ref=halo_piece(head),
            send_sem=hs_sem.at[k], recv_sem=hr_sem.at[head],
            device_id={"head": (head + k) % nhead}, device_id_type=MESH,
        )
        copy.start()
        halo_sends.append(copy)

    def halo_arrive(owner):
        pltpu.make_async_remote_copy(
            src_ref=halo_piece(owner), dst_ref=halo_piece(owner),
            send_sem=hs_sem.at[0], recv_sem=hr_sem.at[owner],
            device_id={"head": other}, device_id_type=MESH,
        ).wait_recv()

    tile = 256
    tiles = (2 * inner + wide) // tile

    def multiply(at, start):
        k = pl.ds(pl.multiple_of(at * 2 * feat, 2 * feat), 2 * feat)

        @pl.loop(0, tiles)
        def _(n):
            cols = pl.ds(pl.multiple_of(n * tile, tile), tile)
            part = jnp.dot(tokbuf[at], w[k, cols], preferred_element_type=F32)
            if start:
                acc[:, cols] = part
            else:
                acc[:, cols] += part

        part = lax.dot_general(
            tokbuf[at, both, :], wdtp[:, k], (((1,), (1,)), ((), ())),
            preferred_element_type=F32,
        )
        if start:
            accdt[...] = part
        else:
            accdt[...] += part

    for one in loads:
        one.wait()
    arrive(mine.at[both, other_lanes], 0)
    halo_arrive(other)
    multiply(y, True)

    arrive(tokbuf.at[ym, first, lanes], 1)
    send(tokbuf.at[ym, first, lanes], tokbuf.at[ym, first, lanes], 5, to_up)
    arrive(tokbuf.at[yp, second, lanes], 3)
    send(tokbuf.at[yp, second, lanes], tokbuf.at[yp, second, lanes], 6, to_down)
    send(tokbuf.at[ym, first, lanes], tokbuf.at[ym, first, lanes], 7, to_other)
    send(tokbuf.at[yp, second, lanes], tokbuf.at[yp, second, lanes], 9, to_other)
    arrive(tokbuf.at[ym, second, lanes], 2)
    send(tokbuf.at[ym, second, lanes], tokbuf.at[ym, second, lanes], 8, to_other)
    arrive(tokbuf.at[yp, first, lanes], 4)
    send(tokbuf.at[yp, first, lanes], tokbuf.at[yp, first, lanes], 10, to_other)
    arrive(tokbuf.at[ym, first, other_lanes], 7)
    arrive(tokbuf.at[ym, second, other_lanes], 8)
    halo_arrive(ym * 2)
    halo_arrive(ym * 2 + 1)
    multiply(ym, False)
    arrive(tokbuf.at[yp, second, other_lanes], 9)
    arrive(tokbuf.at[yp, first, other_lanes], 10)
    halo_arrive(yp * 2)
    halo_arrive(yp * 2 + 1)
    multiply(yp, False)

    arrive(tokbuf.at[y2, first, lanes], 5)
    send(tokbuf.at[y2, first, lanes], tokbuf.at[y2, first, lanes], 11, to_other)
    arrive(tokbuf.at[y2, second, lanes], 6)
    send(tokbuf.at[y2, second, lanes], tokbuf.at[y2, second, lanes], 12, to_other)
    halo_arrive(y2 * 2)
    halo_arrive(y2 * 2 + 1)
    arrive(tokbuf.at[y2, first, other_lanes], 11)
    arrive(tokbuf.at[y2, second, other_lanes], 12)
    multiply(y2, False)

    u_out[:, pl.ds(0, inner)] = acc[:, pl.ds(0, inner)].astype(BF16)
    u_out[:, pl.ds(inner, wide)] = acc[:, pl.ds(2 * inner, wide)].astype(BF16)
    z_out[...] = acc[pl.ds(HALO, rows), pl.ds(inner, inner)].astype(BF16)
    dt_out[...] = accdt[...]
    for copy in sent + halo_sends:
        copy.wait_send()


def project(tokens, weight_x, weight_z, weight_bc, weight_dt, nseq, nhead, interpret=False):
    rows, feat = tokens.shape
    depth, inner = weight_x.shape
    wide = weight_bc.shape[1]
    total = 2 * inner + wide
    return pl.pallas_call(
        functools.partial(project_kernel, nseq, nhead),
        name="project",
        out_shape=(
            jax.ShapeDtypeStruct((rows + HALO, inner + wide), BF16),
            jax.ShapeDtypeStruct((rows, inner), BF16),
            jax.ShapeDtypeStruct((rows, 128), F32),
        ),
        in_specs=[hbm()] * 5,
        out_specs=(vmem(), vmem(), vmem()),
        scratch_shapes=[
            pltpu.VMEM((nhead // 2, rows + HALO, 2 * feat), BF16),
            pltpu.VMEM((depth, total), BF16),
            pltpu.VMEM((128, depth), BF16),
            pltpu.VMEM((rows + HALO, total), F32),
            pltpu.VMEM((rows, 128), F32),
            pltpu.SemaphoreType.DMA((5,)),
            pltpu.SemaphoreType.DMA((14,)),
            pltpu.SemaphoreType.DMA((14,)),
            pltpu.SemaphoreType.DMA((nhead,)),
            pltpu.SemaphoreType.DMA((nhead,)),
        ],
        compiler_params=pltpu.CompilerParams(
            collective_id=0, has_side_effects=True, vmem_limit_bytes=48 << 20
        ),
    )(tokens, weight_x, weight_z, weight_bc, weight_dt)


def read_prompts(len_ref, count):
    starts, ends = [], []
    at = jnp.int32(0)
    for r in range(count):
        starts.append(at)
        at = at + len_ref[r]
        ends.append(at - 1)
    return starts, ends


def ends_in_block(starts, ends, base, rows):
    count = len(starts)
    none = jnp.int32(-1)
    a_start, a_end = none, none
    b_start, b_end = none, none
    a_at = none
    for r in range(count - 1, -1, -1):
        here = (ends[r] >= base) & (ends[r] < base + rows)
        a_start = jnp.where(here, starts[r], a_start)
        a_end = jnp.where(here, ends[r], a_end)
        a_at = jnp.where(here, r, a_at)
    for r in range(count):
        here = (ends[r] >= base) & (ends[r] < base + rows) & (a_at != r)
        b_start = jnp.where(here, starts[r], b_start)
        b_end = jnp.where(here, ends[r], b_end)
    return a_start, a_end, b_start, b_end


def end_slots(starts, ends, rows):
    prompts = len(starts)
    slot, block = [], []
    for r in range(prompts):
        at = ends[r] // rows
        a = jnp.bool_(True) if r == 0 else (ends[r - 1] // rows) != at
        b = jnp.bool_(True) if r == prompts - 1 else (ends[r + 1] // rows) != at
        slot.append(jnp.where(a, 0, jnp.where(b, 1, 2)).astype(jnp.int32))
        block.append(at)
    return slot, block


def local_kernel(
    len_ref, page_ref, u, dt_raw, wconv_x, bconv_x, wconv_bc, bconv_bc, step_bias, decay_log,
    skip,
    s_out, d_out, ab_out, v_out, y_out, c_out, col_out, more_out,
    uf, xc, bcol, ccol, btr, scores, stage,
):
    rows = y_out.shape[0]
    inner = y_out.shape[1]
    state = c_out.shape[1]
    heads = step_bias.shape[0]
    lbs = inner // 128
    prompts = len_ref.shape[0]
    base = lax.axis_index("seq") * rows
    starts, ends = read_prompts(len_ref, prompts)

    def start_of(pos):
        found = jnp.zeros_like(pos)
        for r in range(prompts):
            found = jnp.where(starts[r] <= pos, starts[r], found)
        return found

    pos_col = base + lax.broadcasted_iota(jnp.int32, (rows, 1), 0)
    start_col = start_of(pos_col)
    stage[...] = jnp.broadcast_to((pos_col - start_col).astype(F32), stage.shape)
    width = u.shape[1]
    taps = wconv_x.shape[0]
    step = 32

    @pl.loop(0, rows // step)
    def _(t):
        r0 = pl.multiple_of(t * step, step)
        age = stage[pl.ds(r0, step), :]
        for j in range(width // 128):
            lanes = pl.ds(j * 128, 128)
            win = u[pl.ds(r0, step + HALO), lanes].astype(F32)
            uf[pl.ds(r0, step + HALO), lanes] = win
            if j < lbs:
                wl, wt, wb = lanes, wconv_x, bconv_x
            else:
                wl, wt, wb = pl.ds((j - lbs) * 128, 128), wconv_bc, bconv_bc
            total = jnp.broadcast_to(wb[:, wl], (step, 128))
            for k in range(taps):
                d = taps - 1 - k
                shifted = win if d == 0 else pltpu.roll(win, d, 0)
                term = shifted[HALO:, :] * wt[pl.ds(k, 1), wl]
                total = total + (term if d == 0 else jnp.where(age >= d, term, 0.0))
            out = jax.nn.silu(total)
            if j < lbs:
                xc[pl.ds(r0, step), lanes] = out.astype(BF16)
            elif j == lbs:
                bcol[pl.ds(r0, step), :] = out.astype(BF16).astype(F32)
            else:
                ccol[pl.ds(r0, step), :] = out.astype(BF16)

    c_out[...] = ccol[...]
    btr[...] = jnp.transpose(bcol[...]).astype(BF16)

    dtr = jnp.transpose(dt_raw[...])[0:heads, :]
    pre = dtr + step_bias[...]
    dt = jnp.maximum(pre, 0.0) + jnp.log1p(jnp.exp(-jnp.abs(pre)))
    cum = -dt * jnp.exp(decay_log[...])
    lane = lax.broadcasted_iota(jnp.int32, (heads, rows), 1)
    shift = 1
    while shift < rows:
        cum = cum + jnp.where(lane >= shift, pltpu.roll(cum, shift, 1), 0.0)
        shift *= 2
    pos = base + lane
    start_row = start_of(pos)
    a_start, a_end, b_start, b_end = ends_in_block(starts, ends, base, rows)
    more = jnp.int32(0)
    for kind in end_slots(starts, ends, rows)[0]:
        more = jnp.maximum(more, kind - 1)
    more_out[0] = more
    last_start = start_of(jnp.full((heads, rows), base + rows - 1, jnp.int32))

    def at_pos(where_pos):
        return jnp.sum(jnp.where(pos == where_pos, cum, 0.0), axis=1, keepdims=True)

    cum_last = at_pos(base + rows - 1)
    cum_a, cum_b = at_pos(a_end), at_pos(b_end)

    def weight_to(cum_end, keep):
        return jnp.where(keep, jnp.exp(jnp.minimum(cum_end - cum, 0.0)), 0.0) * dt

    w_end = weight_to(cum_last, pos >= last_start)
    w_a = weight_to(cum_a, (pos >= a_start) & (pos <= a_end))
    w_b = weight_to(cum_b, (pos >= b_start) & (pos <= b_end))
    inflow = jnp.where(start_row < base, jnp.exp(cum), 0.0)
    decay = jnp.where(last_start[:, 0:1] < base, jnp.exp(cum_last), 0.0)
    decay_a = jnp.where(
        (jnp.full((heads, 1), a_start) < base) & (jnp.full((heads, 1), a_end) >= 0),
        jnp.exp(cum_a), 0.0,
    )
    cum2 = cum * LOG2E
    packed = jnp.concatenate(
        [cum2, inflow, w_end, w_a, w_b]
        + [jnp.zeros((128 - 5 * heads, rows), F32)], axis=0,
    )
    cols = jnp.transpose(packed)
    col_out[...] = cols
    low = lax.broadcasted_iota(jnp.int32, (rows, 128), 1) < 64
    low_row = lax.broadcasted_iota(jnp.int32, (1, 128), 1) < 64

    for lb in range(lbs):
        h0, h1 = 2 * lb, 2 * lb + 1
        for k, value in enumerate((decay, decay_a)):
            d_out[lb, pl.ds(k, 1), :] = jnp.where(
                low_row,
                jnp.broadcast_to(value[h0 : h0 + 1, :], (1, 128)),
                jnp.broadcast_to(value[h1 : h1 + 1, :], (1, 128)),
            )

    per = s_out.shape[0] // lbs
    piece = state // per
    for lb in range(lbs):
        x_lb = xc[:, pl.ds(lb * 128, 128)].astype(F32)
        for kind in range(3):
            at = (2 + kind) * heads + 2 * lb
            scale = jnp.where(low, cols[:, at : at + 1], cols[:, at + 1 : at + 2])
            weighted = (x_lb * scale).astype(BF16)
            value = jnp.dot(btr[...], weighted, preferred_element_type=F32).astype(BF16)
            value = value.reshape(per, piece, 128)
            if kind == 0:
                s_out[pl.ds(lb * per, per)] = value
            else:
                ab_out[pl.ds(lb * per, per), kind - 1] = value

    tile = 128
    blocks = rows // tile
    for i in range(blocks):
        ri = pl.ds(i * tile, tile)
        reach = (i + 1) * tile
        sc = jnp.dot(ccol[ri, :], btr[:, 0:reach], preferred_element_type=F32)
        pi = base + i * tile + lax.broadcasted_iota(jnp.int32, (tile, reach), 0)
        pj = base + lax.broadcasted_iota(jnp.int32, (tile, reach), 1)
        si = start_col[i * tile : reach, :]
        sc = jnp.where((pj <= pi) & (pj >= si), sc, 0.0)
        scores[ri, 0:reach] = sc
    low_t = lax.broadcasted_iota(jnp.int32, (tile, 128), 1) < 64
    for lb in range(lbs):
        lanes = pl.ds(lb * 128, 128)
        for i in range(blocks):
            ri = pl.ds(i * tile, tile)
            reach = (i + 1) * tile
            parts = []
            for hh in range(2):
                h = 2 * lb + hh
                gap = jnp.minimum(
                    cols[i * tile : reach, h : h + 1] - cum2[h : h + 1, 0:reach], 0.0
                )
                wgt = (scores[ri, 0:reach] * jnp.exp2(gap) * dt[h : h + 1, 0:reach]).astype(BF16)
                parts.append(jnp.dot(wgt, xc[0:reach, lanes], preferred_element_type=F32))
            y_out[ri, lanes] = (
                jnp.where(low_t, parts[0], parts[1])
                + skip[:, lanes] * xc[ri, lanes].astype(F32)
            )

    v_out[...] = jnp.zeros(v_out.shape, BF16)
    zero_rows = jnp.zeros((32, 128), F32)
    for r in range(prompts):
        @pl.when((ends[r] >= base) & (ends[r] < base + rows))
        def _():
            stage[pl.ds(0, 32), :] = zero_rows
            local = ends[r] - base + HALO
            for k in range(taps - 1):
                back = taps - 2 - k
                line = uf[pl.ds(local - back, 1), :]
                keep = jnp.full((1, 128), ends[r] - back, jnp.int32) >= starts[r]
                for j in range(lbs):
                    stage[k * lbs + j : k * lbs + j + 1, :] = jnp.where(
                        keep, line[:, j * 128 : (j + 1) * 128], 0.0
                    )
                for j in range(2):
                    at = (taps - 1) * lbs + 2 * k + j
                    stage[at : at + 1, :] = jnp.where(
                        keep, line[:, (lbs + j) * 128 : (lbs + j + 1) * 128], 0.0
                    )
            v_out[page_ref[r]] = stage[pl.ds(0, 32), :].astype(BF16)


def local(u, dt_raw, wconv_x, bconv_x, wconv_bc, bconv_bc, step_bias, decay_log, skip,
          lengths, pages, nseq):
    rows = dt_raw.shape[0]
    inner = wconv_x.shape[1]
    state = wconv_bc.shape[1] // 2
    lbs = inner // 128
    piece = state * lbs // nseq
    return pl.pallas_call(
        local_kernel,
        name="local",
        out_shape=(
            jax.ShapeDtypeStruct((nseq, piece, 128), BF16),
            jax.ShapeDtypeStruct((lbs, 2, 128), F32),
            jax.ShapeDtypeStruct((nseq, 2, piece, 128), BF16),
            jax.ShapeDtypeStruct((nseq, 32, 128), BF16),
            jax.ShapeDtypeStruct((rows, inner), F32),
            jax.ShapeDtypeStruct((rows, state), BF16),
            jax.ShapeDtypeStruct((rows, 128), F32),
            jax.ShapeDtypeStruct((1,), jnp.int32),
        ),
        in_specs=[smem(), smem()] + [vmem()] * 9,
        out_specs=(vmem(),) * 7 + (smem(),),
        scratch_shapes=[
            pltpu.VMEM((rows + HALO, u.shape[1]), F32),
            pltpu.VMEM((rows, inner), BF16),
            pltpu.VMEM((rows, state), F32),
            pltpu.VMEM((rows, state), BF16),
            pltpu.VMEM((state, rows), BF16),
            pltpu.VMEM((rows, rows), F32),
            pltpu.VMEM((rows, 128), F32),
        ],
        compiler_params=pltpu.CompilerParams(vmem_limit_bytes=48 << 20),
    )(lengths, pages, u, dt_raw, wconv_x, bconv_x, wconv_bc, bconv_bc, step_bias, decay_log, skip)


def finish_kernel(
    nseq, nhead, heads,
    len_ref, page_ref, s_in, d_in, ab_in, v_in, y_in, c_in, col_in, z_in, gain,
    n_out, page_out, cx_out, cb_out,
    s_buf, d_buf, ab_buf, v_buf, h_all, h_send, h_buf, p_send, p_buf, q_send, q_buf, gated,
    send_sem, recv_sem, qs_sem, qr_sem,
):
    seq = lax.axis_index("seq")
    head = lax.axis_index("head")
    rows, inner = y_in.shape
    lbs = inner // 128
    per = nseq // lbs
    piece = s_in.shape[1]
    state = per * piece
    prompts = len_ref.shape[0]
    lb_me = seq // per

    barrier = pltpu.get_barrier_semaphore()

    @pl.loop(1, nseq)
    def _(d):
        pl.semaphore_signal(
            barrier, inc=1, device_id={"seq": (seq + d) % nseq}, device_id_type=MESH
        )

    for k in range(1, nhead):
        pl.semaphore_signal(
            barrier, inc=1, device_id={"head": (head + k) % nhead}, device_id_type=MESH
        )
    s_buf[seq] = s_in[seq]
    d_buf[seq] = d_in[lb_me]
    ab_buf[seq] = ab_in[seq]
    v_buf[seq] = v_in[seq]
    pl.semaphore_wait(barrier, nseq - 1 + nhead - 1)

    S, D, AB, V, H, PG = range(6)

    def copy(kind, src, dst, d, to):
        return pltpu.make_async_remote_copy(
            src_ref=src, dst_ref=dst, send_sem=send_sem.at[kind, d], recv_sem=recv_sem.at[kind, d],
            device_id={"seq": to}, device_id_type=MESH,
        )

    def out_copy(kind, d):
        to = (seq + d) % nseq
        if kind == S:
            return copy(S, s_in.at[to], s_buf.at[seq], d, to)
        if kind == D:
            return copy(D, d_in.at[to // per], d_buf.at[seq], d, to)
        if kind == AB:
            return copy(AB, ab_in.at[to], ab_buf.at[seq], d, to)
        if kind == V:
            return copy(V, v_in.at[to], v_buf.at[seq], d, to)
        if kind == H:
            return copy(H, h_send.at[to], h_buf.at[seq], d, to)
        return copy(PG, p_send.at[to], p_buf.at[seq], d, to)

    def in_copy(kind, d):
        frm = (seq + nseq - d) % nseq
        buf = (s_buf, d_buf, ab_buf, v_buf, h_buf, p_buf)[kind]
        return copy(kind, buf.at[frm], buf.at[frm], d, frm)

    def start_all(*kinds):
        @pl.loop(1, nseq)
        def _(d):
            for kind in kinds:
                out_copy(kind, d).start()

    def arrive_all(*kinds):
        @pl.loop(1, nseq)
        def _(d):
            for kind in kinds:
                in_copy(kind, d).wait_recv()

    start_all(S, D)
    start_all(AB)
    arrive_all(S, D)

    def advance(i, carried):
        h_all[i] = carried
        h_send[i] = carried.astype(BF16)
        return d_buf[i, 0:1, :] * carried + s_buf[i].astype(F32)

    lax.fori_loop(0, nseq, advance, jnp.zeros((piece, 128), F32))
    start_all(H)
    h_buf[seq] = h_send[seq]
    start_all(V)

    starts, ends = read_prompts(len_ref, prompts)
    slot, block = end_slots(starts, ends, rows)
    arrive_all(AB)

    @pl.loop(0, nseq)
    def _(q):
        kind = jnp.int32(2)
        at = jnp.int32(0)
        for r in range(prompts):
            hit = page_ref[r] == q
            kind = jnp.where(hit, slot[r], kind)
            at = jnp.where(hit, block[r], at)
        which = jnp.where(kind == 1, 1, 0)
        at = jnp.clip(at, 0, nseq - 1)
        value = ab_buf[at, which].astype(F32)
        first = value + d_buf[at, 1:2, :] * h_all[at]
        kinds = jnp.full((piece, 128), kind, jnp.int32)
        p_send[q] = jnp.where(kinds == 0, first, jnp.where(kinds == 1, value, 0.0)).astype(BF16)

    start_all(PG)
    p_buf[seq] = p_send[seq]

    arrive_all(H)
    tile = 64
    low = lax.broadcasted_iota(jnp.int32, (tile, 128), 1) < 64
    lanes128 = lax.broadcasted_iota(jnp.int32, (tile, 128), 1)
    subl = lax.broadcasted_iota(jnp.int32, (tile, 128), 0)
    per_row = 128 // tile

    for g in range(rows // 128):
        line = jnp.zeros((1, 128), F32)
        for s in range(per_row):
            r0 = g * 128 + s * tile
            ri = pl.ds(r0, tile)
            total = jnp.zeros((tile, 128), F32)
            for lb in range(lbs):
                lanes = pl.ds(lb * 128, 128)
                hmat = h_buf[pl.ds(lb * per, per)].reshape(state, 128)
                ac = jnp.dot(c_in[ri, :], hmat, preferred_element_type=F32)
                at = heads + 2 * lb
                scale = jnp.where(low, col_in[ri, at : at + 1], col_in[ri, at + 1 : at + 2])
                yv = (y_in[ri, lanes] + ac * scale).astype(BF16).astype(F32)
                zv = z_in[ri, lanes].astype(F32)
                gv = yv * jax.nn.silu(zv)
                gated[ri, lanes] = gv
                total = total + gv * gv
            col = jnp.sum(total, axis=1, keepdims=True)
            line = line + jnp.sum(
                jnp.where(lanes128 == subl + s * tile, col, 0.0), axis=0, keepdims=True
            )
        q_send[g : g + 1, :] = line

    q_copies = []
    for k in range(1, nhead):
        one = pltpu.make_async_remote_copy(
            src_ref=q_send, dst_ref=q_buf.at[head], send_sem=qs_sem.at[k], recv_sem=qr_sem.at[k],
            device_id={"head": (head + k) % nhead}, device_id_type=MESH,
        )
        one.start()
        q_copies.append(one)
    q_buf[head] = q_send[...]

    arrive_all(V)
    source = jnp.int32(0)
    found = jnp.int32(0)
    for r in range(prompts):
        hit = page_ref[r] == seq
        source = jnp.where(hit, block[r], source)
        found = jnp.where(hit, 1, found)
    source = jnp.clip(source, 0, nseq - 1)
    vv = jnp.where(
        jnp.full(v_buf.shape[1:], found, jnp.int32) == 1, v_buf[source].astype(F32), 0.0
    )
    kept = cx_out.shape[0]
    for k in range(kept):
        for j in range(lbs):
            cx_out[k : k + 1, j * 128 : (j + 1) * 128] = vv[k * lbs + j : k * lbs + j + 1, :]
        for j in range(2):
            at = kept * lbs + 2 * k + j
            cb_out[k : k + 1, j * 128 : (j + 1) * 128] = vv[at : at + 1, :]

    for k in range(1, nhead):
        frm = (head + nhead - k) % nhead
        pltpu.make_async_remote_copy(
            src_ref=q_send, dst_ref=q_buf.at[frm], send_sem=qs_sem.at[k], recv_sem=qr_sem.at[k],
            device_id={"head": frm}, device_id_type=MESH,
        ).wait_recv()
    squares = q_buf[0]
    for k in range(1, nhead):
        squares = squares + q_buf[k]
    scale_rows = lax.rsqrt(squares / (inner * nhead) + EPS)
    for g in range(rows // 128):
        for s in range(per_row):
            ri = pl.ds(g * 128 + s * tile, tile)
            diag = jnp.where(lanes128 == subl + s * tile, scale_rows[g : g + 1, :], 0.0)
            scale = jnp.sum(diag, axis=1, keepdims=True)
            n_out[ri, :] = (gated[ri, :] * scale * gain[...]).astype(BF16)

    arrive_all(PG)
    for lb in range(lbs):
        mat = p_buf[pl.ds(lb * per, per)].reshape(state, 128).astype(F32)
        page_out[pl.ds(lb * 128, 128), :] = jnp.transpose(mat)

    @pl.loop(1, nseq)
    def _(d):
        for kind in (S, D, AB, V, H, PG):
            out_copy(kind, d).wait_send()

    for one in q_copies:
        one.wait_send()


def finish(s, d, ab, v, y, c, col, z, gain, lengths, pages, heads, kept, nseq, nhead):
    rows, inner = y.shape
    state = c.shape[1]
    piece = s.shape[1]
    wide = 2 * state
    return pl.pallas_call(
        functools.partial(finish_kernel, nseq, nhead, heads),
        name="finish",
        out_shape=(
            jax.ShapeDtypeStruct((rows, inner), BF16),
            jax.ShapeDtypeStruct((inner, state), F32),
            jax.ShapeDtypeStruct((kept, inner), F32),
            jax.ShapeDtypeStruct((kept, wide), F32),
        ),
        in_specs=[smem(), smem()] + [vmem()] * 9,
        out_specs=(vmem(),) * 4,
        scratch_shapes=[
            pltpu.VMEM(s.shape, BF16),
            pltpu.VMEM((nseq, 2, 128), F32),
            pltpu.VMEM(ab.shape, BF16),
            pltpu.VMEM(v.shape, BF16),
            pltpu.VMEM((nseq, piece, 128), F32),
            pltpu.VMEM((nseq, piece, 128), BF16),
            pltpu.VMEM((nseq, piece, 128), BF16),
            pltpu.VMEM((nseq, piece, 128), BF16),
            pltpu.VMEM((nseq, piece, 128), BF16),
            pltpu.VMEM((rows // 128, 128), F32),
            pltpu.VMEM((nhead, rows // 128, 128), F32),
            pltpu.VMEM((rows, inner), F32),
            pltpu.SemaphoreType.DMA((6, nseq)),
            pltpu.SemaphoreType.DMA((6, nseq)),
            pltpu.SemaphoreType.DMA((nhead,)),
            pltpu.SemaphoreType.DMA((nhead,)),
        ],
        compiler_params=pltpu.CompilerParams(
            collective_id=1, has_side_effects=True, vmem_limit_bytes=48 << 20
        ),
    )(lengths, pages, s, d, ab, v, y, c, col, z, gain)


def crowded_pages(
    u, dt_raw, wconv_x, bconv_x, wconv_bc, bconv_bc, step_bias, decay_log, lengths, pages
):
    rows = dt_raw.shape[0]
    heads = step_bias.shape[0]
    inner = wconv_x.shape[1]
    state = wconv_bc.shape[1] // 2
    taps = wconv_x.shape[0]
    prompts = lengths.shape[0]
    nseq = lax.axis_size("seq")
    base = lax.axis_index("seq") * rows
    ends = jnp.cumsum(lengths) - 1
    starts = ends - lengths + 1
    pos = base + jnp.arange(rows, dtype=jnp.int32)
    age = pos - jnp.max(jnp.where(starts[None] <= pos[:, None], starts[None], 0), axis=1)
    weight = jnp.concatenate([wconv_x, wconv_bc], axis=1)[:, : inner + state]
    total = jnp.concatenate([bconv_x, bconv_bc])[None, : inner + state]
    for k in range(taps):
        d = taps - 1 - k
        term = u[HALO - d : HALO - d + rows, : inner + state].astype(F32) * weight[k][None]
        total = total + jnp.where((age >= d)[:, None], term, 0.0)
    conv = jax.nn.silu(total).astype(BF16)
    x, b = conv[:, :inner], conv[:, inner:]
    dt = jax.nn.softplus(dt_raw[:, :heads] + step_bias[None])
    cum = jnp.cumsum(-dt * jnp.exp(decay_log)[None], axis=0)
    block = ends // rows
    before = jnp.concatenate([jnp.full((1,), -1, block.dtype), block[:-1]])
    after = jnp.concatenate([block[1:], jnp.full((1,), -1, block.dtype)])
    mine = (before == block) & (after == block) & (block == lax.axis_index("seq"))
    at_end = cum[jnp.clip(ends - base, 0, rows - 1)]
    keep = mine[:, None] & (pos[None] >= starts[:, None]) & (pos[None] <= ends[:, None])
    scale = jnp.where(
        keep[:, :, None], jnp.exp(jnp.minimum(at_end[:, None] - cum[None], 0.0)) * dt[None], 0.0
    )
    x_heads = x.reshape(rows, heads, -1).astype(F32)
    weighted = (scale[:, :, :, None] * x_heads[None]).astype(BF16).reshape(prompts, rows, inner)
    finals = jnp.einsum("rjc,jn->rcn", weighted, b, preferred_element_type=F32)
    hits = (pages[None, :] == jnp.arange(nseq, dtype=jnp.int32)[:, None]).astype(BF16)
    pool = jnp.einsum("qr,rcn->qcn", hits, finals.astype(BF16), preferred_element_type=F32)
    moved = lax.all_to_all(pool.astype(BF16), "seq", 0, 0, tiled=True)
    return jnp.sum(moved.astype(F32), axis=0)


def body(
    tokens, weight_x, weight_z, weight_bc, weight_dt, conv_x_weight, conv_x_bias,
    conv_bc_weight, conv_bc_bias, step_bias, decay_log, skip_gain, norm_gain, lengths, page_table,
):
    nseq, nhead = lax.axis_size("seq"), lax.axis_size("head")
    heads = weight_dt.shape[0]
    inner = weight_x.shape[1]
    width = inner // heads
    kept = conv_x_weight.shape[0] - 1
    u, z, dt_raw = project(tokens, weight_x, weight_z, weight_bc, weight_dt, nseq, nhead)
    s, d, ab, v, y, c, col, more = local(
        u, dt_raw, conv_x_weight, conv_x_bias[None, :], conv_bc_weight, conv_bc_bias[None, :],
        step_bias[:, None], decay_log[:, None], jnp.repeat(skip_gain, width)[None, :],
        lengths, page_table, nseq,
    )
    normed, page, conv_x, conv_bc = finish(
        s, d, ab, v, y, c, col, z, norm_gain[None, :], lengths, page_table, heads, kept,
        nseq, nhead,
    )
    page = lax.cond(
        more[0] > 0,
        lambda page, *rest: page + crowded_pages(*rest),
        lambda page, *rest: page,
        page, u, dt_raw, conv_x_weight, conv_x_bias, conv_bc_weight, conv_bc_bias, step_bias,
        decay_log, lengths, page_table,
    )
    return (
        normed, page.reshape(1, heads, width, -1), conv_x[None], conv_bc[None],
    )


def solution(mesh):
    in_specs = (
        P("seq", "head"), P(None, "head"), P(None, "head"), P(), P("head", None),
        P(None, "head"), P("head"), P(), P(), P("head"), P("head"), P("head"), P("head"),
        P(), P(),
    )
    out_specs = (
        P("seq", "head"), P("seq", "head", None, None), P("seq", None, "head"),
        P("seq", None, None),
    )
    return jax.shard_map(body, mesh=mesh, in_specs=in_specs, out_specs=out_specs, check_vma=False)
```

```python
import functools

import jax
import jax.numpy as jnp
from jax import lax
from jax.experimental import pallas as pl
from jax.experimental.pallas import tpu as pltpu
from jax.sharding import PartitionSpec as P

MESH = pl.DeviceIdType.MESH
F32 = jnp.float32
BF16 = jnp.bfloat16
EPS = 1e-05
HALO = 16
PROJECT_VMEM = (60 << 20) + (1 << 19)
LOG2E = 1.4426950408889634


def vmem():
    return pl.BlockSpec(memory_space=pltpu.VMEM)


def hbm():
    return pl.BlockSpec(memory_space=pltpu.HBM)


def smem():
    return pl.BlockSpec(memory_space=pltpu.SMEM)


def project_kernel(
    nseq, nhead,
    tok, wx, wz, wbc, wdt,
    acc, accdt,
    tokbuf, w, wdtp,
    lsem, ssem, rsem, hs_sem, hr_sem,
):
    ny = nhead // 2
    seq = lax.axis_index("seq")
    head = lax.axis_index("head")
    y = head // 2
    core = head % 2
    rows, feat = tok.shape
    half = rows // 2
    inner = wx.shape[1]
    wide = wbc.shape[1]
    heads = wdt.shape[0]
    yp, ym = (y + 1) % ny, (y + ny - 1) % ny
    y2 = (y + 2) % ny
    up, down = yp * 2 + core, ym * 2 + core
    other = y * 2 + (1 - core)
    nxt, prv = (seq + 1) % nseq, (seq + nseq - 1) % nseq
    lanes = pl.ds(pl.multiple_of(core * feat, feat), feat)
    other_lanes = pl.ds(pl.multiple_of((1 - core) * feat, feat), feat)
    first, second = pl.ds(HALO, half), pl.ds(HALO + half, half)
    both = pl.ds(HALO, rows)
    edge = pl.ds(0, HALO)

    loads = [
        pltpu.make_async_copy(tok, tokbuf.at[y, both, lanes], lsem.at[0]),
        pltpu.make_async_copy(wx, w.at[:, pl.ds(0, inner)], lsem.at[1]),
        pltpu.make_async_copy(wbc, w.at[:, pl.ds(2 * inner, wide)], lsem.at[2]),
        pltpu.make_async_copy(wz, w.at[:, pl.ds(inner, inner)], lsem.at[3]),
        pltpu.make_async_copy(wdt, wdtp.at[pl.ds(0, heads)], lsem.at[4]),
    ]

    barrier = pltpu.get_barrier_semaphore()
    for k in range(1, nhead):
        pl.semaphore_signal(
            barrier, inc=1, device_id={"head": (head + k) % nhead}, device_id_type=MESH
        )
    pl.semaphore_signal(barrier, inc=1, device_id={"seq": nxt}, device_id_type=MESH)
    pl.semaphore_signal(barrier, inc=1, device_id={"seq": prv}, device_id_type=MESH)
    wdtp[pl.ds(heads, 128 - heads), :] = jnp.zeros((128 - heads, wdtp.shape[1]), BF16)
    for one in loads:
        one.start()
    pl.semaphore_wait(barrier, nhead + 1)

    sent = []

    def send(src, dst, number, to):
        copy = pltpu.make_async_remote_copy(
            src_ref=src, dst_ref=dst, send_sem=ssem.at[number], recv_sem=rsem.at[number],
            device_id=to, device_id_type=MESH,
        )
        copy.start()
        sent.append(copy)

    def arrive(region, number):
        pltpu.make_async_remote_copy(
            src_ref=region, dst_ref=region, send_sem=ssem.at[number], recv_sem=rsem.at[number],
            device_id={"head": other}, device_id_type=MESH,
        ).wait_recv()

    to_up, to_down, to_other = {"head": up}, {"head": down}, {"head": other}
    mine = tokbuf.at[y]
    send(tok.at[pl.ds(rows - HALO, HALO)], mine.at[edge, lanes], 13, {"seq": nxt})
    send(tok.at[pl.ds(0, half)], mine.at[first, lanes], 1, to_up)
    send(tok.at[pl.ds(half, half)], mine.at[second, lanes], 3, to_down)
    send(tok, mine.at[both, lanes], 0, to_other)
    send(tok.at[pl.ds(half, half)], mine.at[second, lanes], 2, to_up)
    send(tok.at[pl.ds(0, half)], mine.at[first, lanes], 4, to_down)

    def halo_piece(owner):
        return tokbuf.at[
            owner // 2, edge, pl.ds(pl.multiple_of((owner % 2) * feat, feat), feat)
        ]

    arrive(halo_piece(head), 13)
    halo_sends = []
    for k in range(1, nhead):
        copy = pltpu.make_async_remote_copy(
            src_ref=halo_piece(head), dst_ref=halo_piece(head),
            send_sem=hs_sem.at[k], recv_sem=hr_sem.at[head],
            device_id={"head": (head + k) % nhead}, device_id_type=MESH,
        )
        copy.start()
        halo_sends.append(copy)

    def halo_arrive(owner):
        pltpu.make_async_remote_copy(
            src_ref=halo_piece(owner), dst_ref=halo_piece(owner),
            send_sem=hs_sem.at[0], recv_sem=hr_sem.at[owner],
            device_id={"head": other}, device_id_type=MESH,
        ).wait_recv()

    tile = 256
    tiles = (2 * inner + wide) // tile

    def multiply(at, start):
        k = pl.ds(pl.multiple_of(at * 2 * feat, 2 * feat), 2 * feat)

        @pl.loop(0, tiles)
        def _(n):
            cols = pl.ds(pl.multiple_of(n * tile, tile), tile)
            part = jnp.dot(tokbuf[at], w[k, cols], preferred_element_type=F32)
            if start:
                acc[:, cols] = part
            else:
                acc[:, cols] += part

        part = lax.dot_general(
            tokbuf[at, both, :], wdtp[:, k], (((1,), (1,)), ((), ())),
            preferred_element_type=F32,
        )
        if start:
            accdt[...] = part
        else:
            accdt[...] += part

    for one in loads:
        one.wait()
    arrive(mine.at[both, other_lanes], 0)
    halo_arrive(other)
    multiply(y, True)

    arrive(tokbuf.at[ym, first, lanes], 1)
    send(tokbuf.at[ym, first, lanes], tokbuf.at[ym, first, lanes], 5, to_up)
    arrive(tokbuf.at[yp, second, lanes], 3)
    send(tokbuf.at[yp, second, lanes], tokbuf.at[yp, second, lanes], 6, to_down)
    send(tokbuf.at[ym, first, lanes], tokbuf.at[ym, first, lanes], 7, to_other)
    send(tokbuf.at[yp, second, lanes], tokbuf.at[yp, second, lanes], 9, to_other)
    arrive(tokbuf.at[ym, second, lanes], 2)
    send(tokbuf.at[ym, second, lanes], tokbuf.at[ym, second, lanes], 8, to_other)
    arrive(tokbuf.at[yp, first, lanes], 4)
    send(tokbuf.at[yp, first, lanes], tokbuf.at[yp, first, lanes], 10, to_other)
    arrive(tokbuf.at[ym, first, other_lanes], 7)
    arrive(tokbuf.at[ym, second, other_lanes], 8)
    halo_arrive(ym * 2)
    halo_arrive(ym * 2 + 1)
    multiply(ym, False)
    arrive(tokbuf.at[yp, second, other_lanes], 9)
    arrive(tokbuf.at[yp, first, other_lanes], 10)
    halo_arrive(yp * 2)
    halo_arrive(yp * 2 + 1)
    multiply(yp, False)

    arrive(tokbuf.at[y2, first, lanes], 5)
    send(tokbuf.at[y2, first, lanes], tokbuf.at[y2, first, lanes], 11, to_other)
    arrive(tokbuf.at[y2, second, lanes], 6)
    send(tokbuf.at[y2, second, lanes], tokbuf.at[y2, second, lanes], 12, to_other)
    halo_arrive(y2 * 2)
    halo_arrive(y2 * 2 + 1)
    arrive(tokbuf.at[y2, first, other_lanes], 11)
    arrive(tokbuf.at[y2, second, other_lanes], 12)
    multiply(y2, False)

    for copy in sent + halo_sends:
        copy.wait_send()


def project(tokens, weight_x, weight_z, weight_bc, weight_dt, nseq, nhead, interpret=False):
    rows, feat = tokens.shape
    depth, inner = weight_x.shape
    wide = weight_bc.shape[1]
    total = 2 * inner + wide
    return pl.pallas_call(
        functools.partial(project_kernel, nseq, nhead),
        name="project",
        out_shape=(
            jax.ShapeDtypeStruct((rows + HALO, total), F32),
            jax.ShapeDtypeStruct((rows, 128), F32),
        ),
        in_specs=[hbm()] * 5,
        out_specs=(vmem(), vmem()),
        scratch_shapes=[
            pltpu.VMEM((nhead // 2, rows + HALO, 2 * feat), BF16),
            pltpu.VMEM((depth, total), BF16),
            pltpu.VMEM((128, depth), BF16),
            pltpu.SemaphoreType.DMA((5,)),
            pltpu.SemaphoreType.DMA((14,)),
            pltpu.SemaphoreType.DMA((14,)),
            pltpu.SemaphoreType.DMA((nhead,)),
            pltpu.SemaphoreType.DMA((nhead,)),
        ],
        compiler_params=pltpu.CompilerParams(
            collective_id=0, has_side_effects=True, vmem_limit_bytes=PROJECT_VMEM
        ),
    )(tokens, weight_x, weight_z, weight_bc, weight_dt)


def silu(x):
    half = 0.5 * x
    return half + half * jnp.tanh(half)


def read_prompts(len_ref, count):
    starts, ends = [], []
    at = jnp.int32(0)
    for r in range(count):
        starts.append(at)
        at = at + len_ref[r]
        ends.append(at - 1)
    return starts, ends


def ends_in_block(starts, ends, base, rows):
    count = len(starts)
    none = jnp.int32(-1)
    a_start, a_end = none, none
    b_start, b_end = none, none
    a_at = none
    for r in range(count - 1, -1, -1):
        here = (ends[r] >= base) & (ends[r] < base + rows)
        a_start = jnp.where(here, starts[r], a_start)
        a_end = jnp.where(here, ends[r], a_end)
        a_at = jnp.where(here, r, a_at)
    for r in range(count):
        here = (ends[r] >= base) & (ends[r] < base + rows) & (a_at != r)
        b_start = jnp.where(here, starts[r], b_start)
        b_end = jnp.where(here, ends[r], b_end)
    return a_start, a_end, b_start, b_end


def end_slots(starts, ends, rows):
    prompts = len(starts)
    slot, block = [], []
    for r in range(prompts):
        at = ends[r] // rows
        a = jnp.bool_(True) if r == 0 else (ends[r - 1] // rows) != at
        b = jnp.bool_(True) if r == prompts - 1 else (ends[r + 1] // rows) != at
        slot.append(jnp.where(a, 0, jnp.where(b, 1, 2)).astype(jnp.int32))
        block.append(at)
    return slot, block


def by_head(values, shape):
    which = lax.broadcasted_iota(jnp.int32, shape, 0)
    out = jnp.zeros(shape, F32)
    for h in range(shape[0]):
        out = jnp.where(which == h, values[h], out)
    return out


def block_kernel(
    xs, zs, nhead,
    len_ref, page_ref, step_bias, decay_log, skip_gain,
    u, dt_raw, wconv_x, bconv_x, wconv_bc, bconv_bc,
    gated, scale_out, page_out, v_out, more_out,
    xc, bcol, ccol, btr, scores, cols, stage, y_loc,
    s_send, d_send, ab_send, v_all, v_send, s_buf, d_buf, ab_buf, v_buf,
    h_all, h_send, h_buf, p_send, q_send, q_buf, where_ref,
    send_sem, recv_sem, qs_sem, qr_sem,
):
    nseq = xs * zs
    seq = lax.axis_index("seq")
    head = lax.axis_index("head")
    my_x, my_z = seq // zs, seq % zs
    rows, inner = xc.shape
    state = ccol.shape[1]
    heads = step_bias.shape[0]
    lbs = inner // 128
    per = nseq // lbs
    piece = state // per
    prompts = len_ref.shape[0]
    taps = wconv_x.shape[0]
    lb_me = seq // per
    base = seq * rows

    barrier = pltpu.get_barrier_semaphore()

    @pl.loop(1, nseq)
    def _(d):
        pl.semaphore_signal(
            barrier, inc=1, device_id={"seq": (seq + d) % nseq}, device_id_type=MESH
        )

    for k in range(1, nhead):
        pl.semaphore_signal(
            barrier, inc=1, device_id={"head": (head + k) % nhead}, device_id_type=MESH
        )

    starts, ends = read_prompts(len_ref, prompts)
    slot, block = end_slots(starts, ends, rows)
    more = jnp.int32(0)
    for kind in slot:
        more = jnp.maximum(more, kind - 1)
    more_out[0] = more

    def start_of(pos):
        found = jnp.zeros_like(pos)
        for r in range(prompts):
            found = jnp.where(starts[r] <= pos, starts[r], found)
        return found

    dtr = jnp.transpose(dt_raw[...])[0:heads, :]
    pre = dtr + by_head(step_bias, (heads, rows))
    dt = jnp.maximum(pre, 0.0) + jnp.log1p(jnp.exp(-jnp.abs(pre)))
    cum = -dt * jnp.exp(by_head(decay_log, (heads, rows)))
    lane = lax.broadcasted_iota(jnp.int32, (heads, rows), 1)
    shift = 1
    while shift < rows:
        cum = cum + jnp.where(lane >= shift, pltpu.roll(cum, shift, 1), 0.0)
        shift *= 2
    pos = base + lane
    start_row = start_of(pos)
    a_start, a_end, b_start, b_end = ends_in_block(starts, ends, base, rows)
    last_start = start_of(jnp.full((heads, rows), base + rows - 1, jnp.int32))

    def at_pos(where_pos):
        return jnp.sum(jnp.where(pos == where_pos, cum, 0.0), axis=1, keepdims=True)

    cum_last = at_pos(base + rows - 1)
    cum_a, cum_b = at_pos(a_end), at_pos(b_end)

    def weight_to(cum_end, keep):
        return jnp.where(keep, jnp.exp(jnp.minimum(cum_end - cum, 0.0)), 0.0) * dt

    w_end = weight_to(cum_last, pos >= last_start)
    w_a = weight_to(cum_a, (pos >= a_start) & (pos <= a_end))
    w_b = weight_to(cum_b, (pos >= b_start) & (pos <= b_end))
    inflow = jnp.where(start_row < base, jnp.exp(cum), 0.0)
    decay = jnp.where(last_start[:, 0:1] < base, jnp.exp(cum_last), 0.0)
    decay_a = jnp.where(
        (jnp.full((heads, 1), a_start) < base) & (jnp.full((heads, 1), a_end) >= 0),
        jnp.exp(cum_a), 0.0,
    )
    cum2 = cum * LOG2E
    age_row = (pos - start_row).astype(F32)
    packed = jnp.concatenate(
        [cum2, inflow, w_end, w_a, w_b, age_row]
        + [jnp.zeros((128 - 6 * heads, rows), F32)], axis=0,
    )
    cols[...] = jnp.transpose(packed)
    low_row = lax.broadcasted_iota(jnp.int32, (1, 128), 1) < 64

    for lb in range(lbs):
        h0, h1 = 2 * lb, 2 * lb + 1
        for k, value in enumerate((decay, decay_a)):
            d_send[lb, pl.ds(k, 1), :] = jnp.where(
                low_row,
                jnp.broadcast_to(value[h0 : h0 + 1, :], (1, 128)),
                jnp.broadcast_to(value[h1 : h1 + 1, :], (1, 128)),
            )

    step = 64

    @pl.loop(0, rows // step)
    def _(t):
        r0 = pl.multiple_of(t * step, step)
        age = jnp.broadcast_to(cols[pl.ds(r0, step), 5 * heads : 5 * heads + 1], (step, 128))
        near = [age >= d for d in range(taps)]
        for j in range(lbs + 2):
            lanes = pl.ds(j * 128, 128)
            win = u[pl.ds(r0, step + HALO), pl.ds((j if j < lbs else j + lbs) * 128, 128)]
            if j < lbs:
                wl, wt, wb = lanes, wconv_x, bconv_x
            else:
                wl, wt, wb = pl.ds((j - lbs) * 128, 128), wconv_bc, bconv_bc
            total = jnp.broadcast_to(wb[:, wl], (step, 128))
            for k in range(taps):
                d = taps - 1 - k
                shifted = win if d == 0 else pltpu.roll(win, d, 0)
                term = shifted[HALO:, :] * wt[pl.ds(k, 1), wl]
                total = total + (term if d == 0 else jnp.where(near[d], term, 0.0))
            out = silu(total)
            if j < lbs:
                xc[pl.ds(r0, step), lanes] = out.astype(BF16)
            elif j == lbs:
                bcol[pl.ds(r0, step), :] = out.astype(BF16).astype(F32)
            else:
                ccol[pl.ds(r0, step), :] = out.astype(BF16)

    btr[...] = jnp.transpose(bcol[...]).astype(BF16)

    low = lax.broadcasted_iota(jnp.int32, (rows, 128), 1) < 64

    def state_of(kind, lb):
        at = (2 + kind) * heads + 2 * lb
        scale = jnp.where(low, cols[:, at : at + 1], cols[:, at + 1 : at + 2])
        weighted = (xc[:, pl.ds(lb * 128, 128)].astype(F32) * scale).astype(BF16)
        value = jnp.dot(btr[...], weighted, preferred_element_type=F32)
        return value.astype(BF16).reshape(per, piece, 128)

    for lb in range(lbs):
        s_send[pl.ds(lb * per, per)] = state_of(0, lb)
    pl.semaphore_wait(barrier, nseq - 1 + nhead - 1)

    S, D, AB, V, H, PG = range(6)

    def offset(n):
        t, s = n // xs, n % xs
        dz = (zs // 2 + (1 - 2 * (t % 2)) * ((t + 1) // 2)) % zs
        dx = (xs // 2 + (1 - 2 * (s % 2)) * ((s + 1) // 2)) % xs
        return dx, dz

    def copy(kind, src, dst, n, to):
        return pltpu.make_async_remote_copy(
            src_ref=src, dst_ref=dst, send_sem=send_sem.at[kind, n], recv_sem=recv_sem.at[kind, n],
            device_id={"seq": to}, device_id_type=MESH,
        )

    def out_copy(kind, n):
        dx, dz = offset(n)
        to = ((my_x + dx) % xs) * zs + (my_z + dz) % zs
        if kind == S:
            return copy(S, s_send.at[to], s_buf.at[seq], n, to)
        if kind == D:
            return copy(D, d_send.at[to // per], d_buf.at[seq], n, to)
        if kind == AB:
            return copy(AB, ab_send.at[to], ab_buf.at[seq], n, to)
        if kind == V:
            return copy(V, v_send.at[to], v_buf.at[seq], n, to)
        if kind == H:
            return copy(H, h_send.at[to], h_buf.at[seq], n, to)
        return copy(PG, p_send.at[to], page_out.at[seq], n, to)

    def in_copy(kind, n):
        dx, dz = offset(n)
        frm = ((my_x + xs - dx) % xs) * zs + (my_z + zs - dz) % zs
        buf = (s_buf, d_buf, ab_buf, v_buf, h_buf, page_out)[kind]
        return copy(kind, buf.at[frm], buf.at[frm], n, frm)

    def start_all(*kinds):
        @pl.loop(0, nseq - 1)
        def _(n):
            for kind in kinds:
                out_copy(kind, n).start()

    def arrive_all(*kinds):
        @pl.loop(0, nseq - 1)
        def _(n):
            for kind in kinds:
                in_copy(kind, n).wait_recv()

    start_all(S, D)
    for lb in range(lbs):
        for kind in range(2):
            ab_send[pl.ds(lb * per, per), kind] = state_of(1 + kind, lb)
    start_all(AB)
    s_buf[seq] = s_send[seq]
    d_buf[seq] = d_send[lb_me]
    ab_buf[seq] = ab_send[seq]

    tile = 128
    blocks = rows // tile
    for i in range(blocks):
        ri = pl.ds(i * tile, tile)
        reach = (i + 1) * tile
        sc = jnp.dot(ccol[ri, :], btr[:, 0:reach], preferred_element_type=F32)
        gap_i = i * tile + lax.broadcasted_iota(jnp.int32, (tile, reach), 0)
        gap_j = lax.broadcasted_iota(jnp.int32, (tile, reach), 1)
        back = (gap_i - gap_j).astype(F32)
        age = cols[ri, 5 * heads : 5 * heads + 1]
        scores[ri, 0:reach] = jnp.where((back >= 0.0) & (back <= age), sc, 0.0)
    low_t = lax.broadcasted_iota(jnp.int32, (tile, 128), 1) < 64
    for lb in range(lbs):
        lanes = pl.ds(lb * 128, 128)
        gain = jnp.where(low_row, skip_gain[2 * lb], skip_gain[2 * lb + 1])
        for i in range(blocks):
            ri = pl.ds(i * tile, tile)
            reach = (i + 1) * tile
            parts = []
            for hh in range(2):
                h = 2 * lb + hh
                gap = jnp.minimum(cols[ri, h : h + 1] - cum2[h : h + 1, 0:reach], 0.0)
                wgt = (scores[ri, 0:reach] * jnp.exp2(gap) * dt[h : h + 1, 0:reach]).astype(BF16)
                parts.append(jnp.dot(wgt, xc[0:reach, lanes], preferred_element_type=F32))
            y_loc[ri, lanes] = (
                jnp.where(low_t, parts[0], parts[1]) + gain * xc[ri, lanes].astype(F32)
            )

    arrive_all(S, D)

    def advance(i, carried):
        h_all[i] = carried
        h_send[i] = carried.astype(BF16)
        return d_buf[i, 0:1, :] * carried + s_buf[i].astype(F32)

    lax.fori_loop(0, nseq, advance, jnp.zeros((piece, 128), F32))
    start_all(H)
    h_buf[seq] = h_send[seq]

    @pl.loop(0, nseq)
    def _(q):
        kind = jnp.int32(2)
        at = jnp.int32(0)
        who = jnp.int32(prompts)
        for r in range(prompts):
            hit = page_ref[r] == q
            kind = jnp.where(hit, slot[r], kind)
            at = jnp.where(hit, block[r], at)
            who = jnp.where(hit & (block[r] == seq), r, who)
        where_ref[0, q] = kind
        where_ref[1, q] = jnp.clip(at, 0, nseq - 1)
        where_ref[2, q] = who

    v_rows = v_all.shape[1]
    v_all[prompts] = jnp.zeros((v_rows, 128), BF16)
    for r in range(prompts):
        local = jnp.clip(ends[r] - base, 0, rows - 1) + HALO
        for k in range(taps - 1):
            back = taps - 2 - k
            line = u[pl.ds(local - back, 1), :]
            keep = jnp.full((1, 128), ends[r] - back, jnp.int32) >= starts[r]
            for j in range(lbs):
                stage[k * lbs + j : k * lbs + j + 1, :] = jnp.where(
                    keep, line[:, j * 128 : (j + 1) * 128], 0.0
                )
            for j in range(2):
                at = (taps - 1) * lbs + 2 * k + j
                stage[at : at + 1, :] = jnp.where(
                    keep, line[:, (2 * lbs + j) * 128 : (2 * lbs + j + 1) * 128], 0.0
                )
        v_all[r] = stage[...].astype(BF16)

    @pl.loop(0, nseq)
    def _(q):
        v_send[q] = v_all[where_ref[2, q]]

    arrive_all(AB)

    @pl.loop(0, nseq)
    def _(q):
        kind = where_ref[0, q]
        at = where_ref[1, q]
        value = ab_buf[at, jnp.where(kind == 1, 1, 0)].astype(F32)
        first = value + d_buf[at, 1:2, :] * h_all[at]
        kinds = jnp.full((piece, 128), kind, jnp.int32)
        p_send[q] = jnp.where(kinds == 0, first, jnp.where(kinds == 1, value, 0.0)).astype(BF16)

    start_all(PG)
    start_all(V)
    page_out[seq] = p_send[seq]
    v_buf[seq] = v_send[seq]

    arrive_all(H)
    tile = 64
    low = lax.broadcasted_iota(jnp.int32, (tile, 128), 1) < 64
    lanes128 = lax.broadcasted_iota(jnp.int32, (tile, 128), 1)
    subl = lax.broadcasted_iota(jnp.int32, (tile, 128), 0)
    for g in range(rows // 128):
        line = jnp.zeros((1, 128), F32)
        for s in range(128 // tile):
            ri = pl.ds(g * 128 + s * tile, tile)
            total = jnp.zeros((tile, 128), F32)
            for lb in range(lbs):
                lanes = pl.ds(lb * 128, 128)
                hmat = h_buf[pl.ds(lb * per, per)].reshape(state, 128)
                ac = jnp.dot(ccol[ri, :], hmat, preferred_element_type=F32)
                at = heads + 2 * lb
                scale = jnp.where(low, cols[ri, at : at + 1], cols[ri, at + 1 : at + 2])
                yv = (y_loc[ri, lanes] + ac * scale).astype(BF16).astype(F32)
                zv = u[pl.ds(HALO + g * 128 + s * tile, tile), pl.ds(inner + lb * 128, 128)]
                gv = yv * silu(zv)
                gated[ri, lanes] = gv
                total = total + gv * gv
            col = jnp.sum(total, axis=1, keepdims=True)
            line = line + jnp.sum(
                jnp.where(lanes128 == subl + s * tile, col, 0.0), axis=0, keepdims=True
            )
        q_send[g : g + 1, :] = line

    q_copies = []
    for k in range(1, nhead):
        one = pltpu.make_async_remote_copy(
            src_ref=q_send, dst_ref=q_buf.at[head], send_sem=qs_sem.at[k], recv_sem=qr_sem.at[k],
            device_id={"head": (head + k) % nhead}, device_id_type=MESH,
        )
        one.start()
        q_copies.append(one)
    q_buf[head] = q_send[...]

    source = jnp.int32(0)
    found = jnp.int32(0)
    for r in range(prompts):
        hit = page_ref[r] == seq
        source = jnp.where(hit, block[r], source)
        found = jnp.where(hit, 1, found)
    source = jnp.clip(source, 0, nseq - 1)
    arrive_all(V)
    v_out[...] = jnp.where(
        jnp.full(v_out.shape, found, jnp.int32) == 1, v_buf[source].astype(F32), 0.0
    )

    for k in range(1, nhead):
        frm = (head + nhead - k) % nhead
        pltpu.make_async_remote_copy(
            src_ref=q_send, dst_ref=q_buf.at[frm], send_sem=qs_sem.at[k], recv_sem=qr_sem.at[k],
            device_id={"head": frm}, device_id_type=MESH,
        ).wait_recv()
    squares = q_buf[0]
    for k in range(1, nhead):
        squares = squares + q_buf[k]
    scale_out[...] = lax.rsqrt(squares / (inner * nhead) + EPS)
    arrive_all(PG)

    @pl.loop(0, nseq - 1)
    def _(n):
        for kind in (S, D, AB, V, H, PG):
            out_copy(kind, n).wait_send()

    for one in q_copies:
        one.wait_send()


def run_block(u, dt_raw, wconv_x, bconv_x, wconv_bc, bconv_bc, step_bias, decay_log, skip,
              lengths, pages, nseq, nhead):
    rows, inner = dt_raw.shape[0], wconv_x.shape[1]
    state = wconv_bc.shape[1] // 2
    lbs = inner // 128
    piece = state * lbs // nseq
    prompts = lengths.shape[0]
    xs = 4
    tiles = (nseq, piece, 128)
    v_rows = 24
    return pl.pallas_call(
        functools.partial(block_kernel, xs, nseq // xs, nhead),
        name="block",
        out_shape=(
            jax.ShapeDtypeStruct((rows, inner), F32),
            jax.ShapeDtypeStruct((rows // 128, 128), F32),
            jax.ShapeDtypeStruct(tiles, BF16),
            jax.ShapeDtypeStruct((v_rows, 128), F32),
            jax.ShapeDtypeStruct((1,), jnp.int32),
        ),
        in_specs=[smem()] * 5 + [vmem()] * 6,
        out_specs=(vmem(),) * 4 + (smem(),),
        scratch_shapes=[
            pltpu.VMEM((rows, inner), BF16),
            pltpu.VMEM((rows, state), F32),
            pltpu.VMEM((rows, state), BF16),
            pltpu.VMEM((state, rows), BF16),
            pltpu.VMEM((rows, rows), F32),
            pltpu.VMEM((rows, 128), F32),
            pltpu.VMEM((v_rows, 128), F32),
            pltpu.VMEM((rows, inner), F32),
            pltpu.VMEM(tiles, BF16),
            pltpu.VMEM((lbs, 2, 128), F32),
            pltpu.VMEM((nseq, 2, piece, 128), BF16),
            pltpu.VMEM((prompts + 1, v_rows, 128), BF16),
            pltpu.VMEM((nseq, v_rows, 128), BF16),
            pltpu.VMEM(tiles, BF16),
            pltpu.VMEM((nseq, 2, 128), F32),
            pltpu.VMEM((nseq, 2, piece, 128), BF16),
            pltpu.VMEM((nseq, v_rows, 128), BF16),
            pltpu.VMEM(tiles, F32),
            pltpu.VMEM(tiles, BF16),
            pltpu.VMEM(tiles, BF16),
            pltpu.VMEM(tiles, BF16),
            pltpu.VMEM((rows // 128, 128), F32),
            pltpu.VMEM((nhead, rows // 128, 128), F32),
            pltpu.SMEM((3, nseq), jnp.int32),
            pltpu.SemaphoreType.DMA((6, nseq)),
            pltpu.SemaphoreType.DMA((6, nseq)),
            pltpu.SemaphoreType.DMA((nhead,)),
            pltpu.SemaphoreType.DMA((nhead,)),
        ],
        compiler_params=pltpu.CompilerParams(
            collective_id=1, has_side_effects=True, vmem_limit_bytes=40 << 20
        ),
    )(lengths, pages, step_bias, decay_log, skip, u, dt_raw, wconv_x, bconv_x, wconv_bc,
      bconv_bc)


def write_kernel(gated, scale_rows, pages, v, gain, n_out, page_out, cx_out, cb_out):
    rows, inner = gated.shape
    lbs = inner // 128
    per = pages.shape[0] // lbs
    state = per * pages.shape[1]
    tile = 64
    lanes128 = lax.broadcasted_iota(jnp.int32, (tile, 128), 1)
    subl = lax.broadcasted_iota(jnp.int32, (tile, 128), 0)
    for g in range(rows // 128):
        for s in range(128 // tile):
            ri = pl.ds(g * 128 + s * tile, tile)
            diag = jnp.where(lanes128 == subl + s * tile, scale_rows[g : g + 1, :], 0.0)
            scale = jnp.sum(diag, axis=1, keepdims=True)
            n_out[ri, :] = (gated[ri, :] * scale * gain[...]).astype(BF16)
    for lb in range(lbs):
        mat = pages[pl.ds(lb * per, per)].reshape(state, 128).astype(F32)
        page_out[pl.ds(lb * 128, 128), :] = jnp.transpose(mat)
    kept = cx_out.shape[0]
    for k in range(kept):
        for j in range(lbs):
            cx_out[k, :, j * 128 : (j + 1) * 128] = v[k * lbs + j : k * lbs + j + 1, :]
        for j in range(2):
            at = kept * lbs + 2 * k + j
            cb_out[k, :, j * 128 : (j + 1) * 128] = v[at : at + 1, :]


def write(gated, scale_rows, pages, v, gain, state, kept):
    rows, inner = gated.shape
    return pl.pallas_call(
        write_kernel,
        name="write",
        out_shape=(
            jax.ShapeDtypeStruct((rows, inner), BF16),
            jax.ShapeDtypeStruct((inner, state), F32),
            jax.ShapeDtypeStruct((kept, 1, inner), F32),
            jax.ShapeDtypeStruct((kept, 1, 2 * state), F32),
        ),
        in_specs=[vmem()] * 5,
        out_specs=(vmem(),) * 4,
        compiler_params=pltpu.CompilerParams(vmem_limit_bytes=8 << 20),
    )(gated, scale_rows, pages, v, gain)


def crowded_pages(
    u, dt_raw, wconv_x, bconv_x, wconv_bc, bconv_bc, step_bias, decay_log, lengths, pages
):
    rows = dt_raw.shape[0]
    heads = step_bias.shape[0]
    inner = wconv_x.shape[1]
    state = wconv_bc.shape[1] // 2
    taps = wconv_x.shape[0]
    prompts = lengths.shape[0]
    nseq = lax.axis_size("seq")
    base = lax.axis_index("seq") * rows
    ends = jnp.cumsum(lengths) - 1
    starts = ends - lengths + 1
    pos = base + jnp.arange(rows, dtype=jnp.int32)
    age = pos - jnp.max(jnp.where(starts[None] <= pos[:, None], starts[None], 0), axis=1)
    weight = jnp.concatenate([wconv_x, wconv_bc], axis=1)[:, : inner + state]
    total = jnp.concatenate([bconv_x, bconv_bc])[None, : inner + state]
    joined = jnp.concatenate([u[:, :inner], u[:, 2 * inner : 2 * inner + state]], axis=1)
    for k in range(taps):
        d = taps - 1 - k
        term = joined[HALO - d : HALO - d + rows] * weight[k][None]
        total = total + jnp.where((age >= d)[:, None], term, 0.0)
    conv = jax.nn.silu(total).astype(BF16)
    x, b = conv[:, :inner], conv[:, inner:]
    dt = jax.nn.softplus(dt_raw[:, :heads] + step_bias[None])
    cum = jnp.cumsum(-dt * jnp.exp(decay_log)[None], axis=0)
    block = ends // rows
    before = jnp.concatenate([jnp.full((1,), -1, block.dtype), block[:-1]])
    after = jnp.concatenate([block[1:], jnp.full((1,), -1, block.dtype)])
    mine = (before == block) & (after == block) & (block == lax.axis_index("seq"))
    at_end = cum[jnp.clip(ends - base, 0, rows - 1)]
    keep = mine[:, None] & (pos[None] >= starts[:, None]) & (pos[None] <= ends[:, None])
    scale = jnp.where(
        keep[:, :, None], jnp.exp(jnp.minimum(at_end[:, None] - cum[None], 0.0)) * dt[None], 0.0
    )
    x_heads = x.reshape(rows, heads, -1).astype(F32)
    weighted = (scale[:, :, :, None] * x_heads[None]).astype(BF16).reshape(prompts, rows, inner)
    finals = jnp.einsum("rjc,jn->rcn", weighted, b, preferred_element_type=F32)
    hits = (pages[None, :] == jnp.arange(nseq, dtype=jnp.int32)[:, None]).astype(BF16)
    pool = jnp.einsum("qr,rcn->qcn", hits, finals.astype(BF16), preferred_element_type=F32)
    moved = lax.all_to_all(pool.astype(BF16), "seq", 0, 0, tiled=True)
    return jnp.sum(moved.astype(F32), axis=0)


def body(
    tokens, weight_x, weight_z, weight_bc, weight_dt, conv_x_weight, conv_x_bias,
    conv_bc_weight, conv_bc_bias, step_bias, decay_log, skip_gain, norm_gain, lengths, page_table,
):
    nseq, nhead = lax.axis_size("seq"), lax.axis_size("head")
    heads = weight_dt.shape[0]
    inner = weight_x.shape[1]
    width = inner // heads
    kept = conv_x_weight.shape[0] - 1
    u, dt_raw = project(tokens, weight_x, weight_z, weight_bc, weight_dt, nseq, nhead)
    gated, scale, pages, v, more = run_block(
        u, dt_raw, conv_x_weight, conv_x_bias[None, :], conv_bc_weight,
        conv_bc_bias[None, :], step_bias, decay_log, skip_gain, lengths, page_table, nseq, nhead,
    )
    normed, page, conv_x, conv_bc = write(
        gated, scale, pages, v, norm_gain[None, :], conv_bc_weight.shape[1] // 2, kept
    )
    page = lax.cond(
        more[0] > 0,
        lambda page, *rest: page + crowded_pages(*rest),
        lambda page, *rest: page,
        page, u, dt_raw, conv_x_weight, conv_x_bias, conv_bc_weight, conv_bc_bias, step_bias,
        decay_log, lengths, page_table,
    )
    return (
        normed, page.reshape(1, heads, width, -1), jnp.swapaxes(conv_x, 0, 1), jnp.swapaxes(conv_bc, 0, 1),
    )


def solution(mesh):
    in_specs = (
        P("seq", "head"), P(None, "head"), P(None, "head"), P(), P("head", None),
        P(None, "head"), P("head"), P(), P(), P("head"), P("head"), P("head"), P("head"),
        P(), P(),
    )
    out_specs = (
        P("seq", "head"), P("seq", "head", None, None), P("seq", None, "head"),
        P("seq", None, None),
    )
    return jax.shard_map(body, mesh=mesh, in_specs=in_specs, out_specs=out_specs, check_vma=False)
```

```python
import functools

import jax
import jax.numpy as jnp
from jax import lax
from jax.experimental import pallas as pl
from jax.experimental.pallas import tpu as pltpu
from jax.sharding import PartitionSpec as P

MESH = pl.DeviceIdType.MESH
F32 = jnp.float32
BF16 = jnp.bfloat16
EPS = 1e-05
HALO = 16
PROJECT_VMEM = (60 << 20) + (1 << 19)
LOG2E = 1.4426950408889634


def vmem():
    return pl.BlockSpec(memory_space=pltpu.VMEM)


def hbm():
    return pl.BlockSpec(memory_space=pltpu.HBM)


def smem():
    return pl.BlockSpec(memory_space=pltpu.SMEM)


def project_kernel(
    nseq, nhead,
    tok, wx, wz, wbc, wdt,
    acc, accdt,
    tokbuf, w, wdtp,
    lsem, ssem, rsem, hs_sem, hr_sem,
):
    ny = nhead // 2
    seq = lax.axis_index("seq")
    head = lax.axis_index("head")
    y = head // 2
    core = head % 2
    rows, feat = tok.shape
    half = rows // 2
    inner = wx.shape[1]
    wide = wbc.shape[1]
    heads = wdt.shape[0]
    yp, ym = (y + 1) % ny, (y + ny - 1) % ny
    y2 = (y + 2) % ny
    other = y * 2 + (1 - core)
    nxt, prv = (seq + 1) % nseq, (seq + nseq - 1) % nseq
    lanes = pl.ds(pl.multiple_of(core * feat, feat), feat)
    other_lanes = pl.ds(pl.multiple_of((1 - core) * feat, feat), feat)
    part = [pl.ds(HALO + q * half, half) for q in range(2)]
    from_tok = [pl.ds(q * half, half) for q in range(2)]
    both = pl.ds(HALO, rows)
    edge = pl.ds(0, HALO)

    loads = [
        pltpu.make_async_copy(tok, tokbuf.at[y, both, lanes], lsem.at[0]),
        pltpu.make_async_copy(wx, w.at[:, pl.ds(0, inner)], lsem.at[1]),
        pltpu.make_async_copy(wbc, w.at[:, pl.ds(2 * inner, wide)], lsem.at[2]),
        pltpu.make_async_copy(wz, w.at[:, pl.ds(inner, inner)], lsem.at[3]),
        pltpu.make_async_copy(wdt, wdtp.at[pl.ds(0, heads)], lsem.at[4]),
    ]

    barrier = pltpu.get_barrier_semaphore()
    for k in range(1, nhead):
        pl.semaphore_signal(
            barrier, inc=1, device_id={"head": (head + k) % nhead}, device_id_type=MESH
        )
    pl.semaphore_signal(barrier, inc=1, device_id={"seq": nxt}, device_id_type=MESH)
    pl.semaphore_signal(barrier, inc=1, device_id={"seq": prv}, device_id_type=MESH)
    wdtp[pl.ds(heads, 128 - heads), :] = jnp.zeros((128 - heads, wdtp.shape[1]), BF16)
    for one in loads:
        one.start()
    pl.semaphore_wait(barrier, nhead + 1)

    sent = []

    def send(src, dst, kind, q, to):
        copy = pltpu.make_async_remote_copy(
            src_ref=src, dst_ref=dst, send_sem=ssem.at[kind, q], recv_sem=rsem.at[kind, q],
            device_id=to, device_id_type=MESH,
        )
        copy.start()
        sent.append(copy)

    def arrive(region, kind, q):
        pltpu.make_async_remote_copy(
            src_ref=region, dst_ref=region, send_sem=ssem.at[kind, q], recv_sem=rsem.at[kind, q],
            device_id={"head": other}, device_id_type=MESH,
        ).wait_recv()

    UP, DOWN, TWO, FWD_M, FWD_P, FWD_2, OWN, EDGE = range(8)
    to_up, to_down = {"head": yp * 2 + core}, {"head": ym * 2 + core}
    to_other, to_two = {"head": other}, {"head": y2 * 2 + core}

    def piece(owner, q, core_lanes=lanes):
        return tokbuf.at[owner, part[q], core_lanes]

    mine = tokbuf.at[y]
    send(tok.at[pl.ds(rows - HALO, HALO)], mine.at[edge, lanes], EDGE, 0, {"seq": nxt})
    for q in range(2):
        send(tok.at[from_tok[q]], piece(y, q), UP, q, to_up)
        send(tok.at[from_tok[q]], piece(y, q), DOWN, q, to_down)
        if q == 0:
            send(tok, mine.at[both, lanes], OWN, 0, to_other)
    for q in range(2):
        send(tok.at[from_tok[q]], piece(y, q), TWO, q, to_two)

    def halo_piece(owner):
        return tokbuf.at[
            owner // 2, edge, pl.ds(pl.multiple_of((owner % 2) * feat, feat), feat)
        ]

    def halo_arrive(owner):
        pltpu.make_async_remote_copy(
            src_ref=halo_piece(owner), dst_ref=halo_piece(owner),
            send_sem=hs_sem.at[0], recv_sem=hr_sem.at[owner],
            device_id={"head": other}, device_id_type=MESH,
        ).wait_recv()

    tile = 256
    tiles = (2 * inner + wide) // tile

    def multiply(at, start, low, high):
        k = pl.ds(pl.multiple_of(at * 2 * feat, 2 * feat), 2 * feat)
        rs = pl.ds(low, high - low)

        @pl.loop(0, tiles)
        def _(n):
            cols = pl.ds(pl.multiple_of(n * tile, tile), tile)
            value = jnp.dot(tokbuf[at, rs, :], w[k, cols], preferred_element_type=F32)
            if start:
                acc[rs, cols] = value
            else:
                acc[rs, cols] += value

        value = lax.dot_general(
            tokbuf[at, rs, :], wdtp[:, k], (((1,), (1,)), ((), ())),
            preferred_element_type=F32,
        )
        if start:
            accdt[rs, :] = value
        else:
            accdt[rs, :] += value

    cut, full = HALO + half, HALO + rows

    def forward(owner, q, kind, onward):
        arrive(piece(owner, q), kind, q)
        send(piece(owner, q), piece(owner, q), onward, q, to_other)

    def halo_of(chip):
        halo_arrive(chip * 2)
        halo_arrive(chip * 2 + 1)

    for one in loads:
        one.wait()
    arrive(mine.at[both, other_lanes], OWN, 0)
    multiply(y, True, cut, full)
    arrive(halo_piece(head), EDGE, 0)
    halo_sends = []
    for k in range(1, nhead):
        copy = pltpu.make_async_remote_copy(
            src_ref=halo_piece(head), dst_ref=halo_piece(head),
            send_sem=hs_sem.at[k], recv_sem=hr_sem.at[head],
            device_id={"head": (head + k) % nhead}, device_id_type=MESH,
        )
        copy.start()
        halo_sends.append(copy)

    halo_arrive(other)
    multiply(y, True, 0, cut)
    forward(ym, 0, UP, FWD_M)
    forward(yp, 0, DOWN, FWD_P)
    arrive(piece(ym, 0, other_lanes), FWD_M, 0)
    halo_of(ym)
    multiply(ym, False, 0, cut)
    forward(ym, 1, UP, FWD_M)
    forward(yp, 1, DOWN, FWD_P)
    arrive(piece(yp, 0, other_lanes), FWD_P, 0)
    halo_of(yp)
    multiply(yp, False, 0, cut)
    arrive(piece(ym, 1, other_lanes), FWD_M, 1)
    multiply(ym, False, cut, full)
    forward(y2, 0, TWO, FWD_2)
    arrive(piece(yp, 1, other_lanes), FWD_P, 1)
    multiply(yp, False, cut, full)
    forward(y2, 1, TWO, FWD_2)
    arrive(piece(y2, 0, other_lanes), FWD_2, 0)
    halo_of(y2)
    multiply(y2, False, 0, cut)
    arrive(piece(y2, 1, other_lanes), FWD_2, 1)
    multiply(y2, False, cut, full)

    for copy in sent + halo_sends:
        copy.wait_send()


def project(tokens, weight_x, weight_z, weight_bc, weight_dt, nseq, nhead, interpret=False):
    rows, feat = tokens.shape
    depth, inner = weight_x.shape
    wide = weight_bc.shape[1]
    total = 2 * inner + wide
    return pl.pallas_call(
        functools.partial(project_kernel, nseq, nhead),
        name="project",
        out_shape=(
            jax.ShapeDtypeStruct((rows + HALO, total), F32),
            jax.ShapeDtypeStruct((rows + HALO, 128), F32),
        ),
        in_specs=[hbm()] * 5,
        out_specs=(vmem(), vmem()),
        scratch_shapes=[
            pltpu.VMEM((nhead // 2, rows + HALO, 2 * feat), BF16),
            pltpu.VMEM((depth, total), BF16),
            pltpu.VMEM((128, depth), BF16),
            pltpu.SemaphoreType.DMA((5,)),
            pltpu.SemaphoreType.DMA((8, 2)),
            pltpu.SemaphoreType.DMA((8, 2)),
            pltpu.SemaphoreType.DMA((nhead,)),
            pltpu.SemaphoreType.DMA((nhead,)),
        ],
        compiler_params=pltpu.CompilerParams(
            collective_id=0, has_side_effects=True, vmem_limit_bytes=PROJECT_VMEM
        ),
    )(tokens, weight_x, weight_z, weight_bc, weight_dt)


def silu(x):
    half = 0.5 * x
    return half + half * jnp.tanh(half)


def read_prompts(len_ref, count):
    starts, ends = [], []
    at = jnp.int32(0)
    for r in range(count):
        starts.append(at)
        at = at + len_ref[r]
        ends.append(at - 1)
    return starts, ends


def ends_in_block(starts, ends, base, rows):
    count = len(starts)
    none = jnp.int32(-1)
    a_start, a_end = none, none
    b_start, b_end = none, none
    a_at = none
    for r in range(count - 1, -1, -1):
        here = (ends[r] >= base) & (ends[r] < base + rows)
        a_start = jnp.where(here, starts[r], a_start)
        a_end = jnp.where(here, ends[r], a_end)
        a_at = jnp.where(here, r, a_at)
    for r in range(count):
        here = (ends[r] >= base) & (ends[r] < base + rows) & (a_at != r)
        b_start = jnp.where(here, starts[r], b_start)
        b_end = jnp.where(here, ends[r], b_end)
    return a_start, a_end, b_start, b_end


def end_slots(starts, ends, rows):
    prompts = len(starts)
    slot, block = [], []
    for r in range(prompts):
        at = ends[r] // rows
        a = jnp.bool_(True) if r == 0 else (ends[r - 1] // rows) != at
        b = jnp.bool_(True) if r == prompts - 1 else (ends[r + 1] // rows) != at
        slot.append(jnp.where(a, 0, jnp.where(b, 1, 2)).astype(jnp.int32))
        block.append(at)
    return slot, block


def by_head(values, shape):
    which = lax.broadcasted_iota(jnp.int32, shape, 0)
    out = jnp.zeros(shape, F32)
    for h in range(shape[0]):
        out = jnp.where(which == h, values[h], out)
    return out


def block_kernel(
    xs, zs, nhead,
    len_ref, page_ref, step_bias, decay_log, skip_gain,
    u, dt_raw, wconv_x, bconv_x, wconv_bc, bconv_bc,
    gated, scale_out, page_out, v_out, more_out,
    xc, bcol, btf, ccol, btr, scores, spread, cols, stage, y_loc,
    s_send, d_send, ab_send, v_all, v_send, s_buf, d_buf, ab_buf, v_buf,
    h_all, h_send, h_buf, p_send, q_send, q_buf, where_ref,
    send_sem, recv_sem, qs_sem, qr_sem,
):
    nseq = xs * zs
    seq = lax.axis_index("seq")
    head = lax.axis_index("head")
    my_x, my_z = seq // zs, seq % zs
    rows, inner = xc.shape
    state = ccol.shape[1]
    heads = step_bias.shape[0]
    lbs = inner // 128
    per = nseq // lbs
    piece = state // per
    prompts = len_ref.shape[0]
    taps = wconv_x.shape[0]
    lb_me = seq // per
    base = seq * rows

    barrier = pltpu.get_barrier_semaphore()

    @pl.loop(1, nseq)
    def _(d):
        pl.semaphore_signal(
            barrier, inc=1, device_id={"seq": (seq + d) % nseq}, device_id_type=MESH
        )

    for k in range(1, nhead):
        pl.semaphore_signal(
            barrier, inc=1, device_id={"head": (head + k) % nhead}, device_id_type=MESH
        )

    starts, ends = read_prompts(len_ref, prompts)
    slot, block = end_slots(starts, ends, rows)
    more = jnp.int32(0)
    for kind in slot:
        more = jnp.maximum(more, kind - 1)
    more_out[0] = more

    def start_of(pos):
        found = jnp.zeros_like(pos)
        for r in range(prompts):
            found = jnp.where(starts[r] <= pos, starts[r], found)
        return found

    dtr = jnp.transpose(dt_raw[pl.ds(HALO, rows), :])[0:heads, :]
    pre = dtr + by_head(step_bias, (heads, rows))
    dt = jnp.maximum(pre, 0.0) + jnp.log1p(jnp.exp(-jnp.abs(pre)))
    cum = -dt * jnp.exp(by_head(decay_log, (heads, rows)))
    lane = lax.broadcasted_iota(jnp.int32, (heads, rows), 1)
    shift = 1
    while shift < rows:
        cum = cum + jnp.where(lane >= shift, pltpu.roll(cum, shift, 1), 0.0)
        shift *= 2
    pos = base + lane
    start_row = start_of(pos)
    a_start, a_end, b_start, b_end = ends_in_block(starts, ends, base, rows)
    last_start = start_of(jnp.full((heads, rows), base + rows - 1, jnp.int32))

    def at_pos(where_pos):
        return jnp.sum(jnp.where(pos == where_pos, cum, 0.0), axis=1, keepdims=True)

    cum_last = at_pos(base + rows - 1)
    cum_a, cum_b = at_pos(a_end), at_pos(b_end)

    def weight_to(cum_end, keep):
        return jnp.where(keep, jnp.exp(jnp.minimum(cum_end - cum, 0.0)), 0.0) * dt

    w_end = weight_to(cum_last, pos >= last_start)
    w_a = weight_to(cum_a, (pos >= a_start) & (pos <= a_end))
    w_b = weight_to(cum_b, (pos >= b_start) & (pos <= b_end))
    inflow = jnp.where(start_row < base, jnp.exp(cum), 0.0)
    decay = jnp.where(last_start[:, 0:1] < base, jnp.exp(cum_last), 0.0)
    decay_a = jnp.where(
        (jnp.full((heads, 1), a_start) < base) & (jnp.full((heads, 1), a_end) >= 0),
        jnp.exp(cum_a), 0.0,
    )
    cum2 = cum * LOG2E
    age_row = (pos - start_row).astype(F32)
    packed = jnp.concatenate(
        [cum2, inflow, age_row] + [jnp.zeros((128 - 3 * heads, rows), F32)], axis=0,
    )
    cols[...] = jnp.transpose(packed)
    low_row = lax.broadcasted_iota(jnp.int32, (1, 128), 1) < 64

    for lb in range(lbs):
        h0, h1 = 2 * lb, 2 * lb + 1
        for k, value in enumerate((decay, decay_a)):
            d_send[lb, pl.ds(k, 1), :] = jnp.where(
                low_row,
                jnp.broadcast_to(value[h0 : h0 + 1, :], (1, 128)),
                jnp.broadcast_to(value[h1 : h1 + 1, :], (1, 128)),
            )

    step = 64

    @pl.loop(0, rows // step)
    def _(t):
        r0 = pl.multiple_of(t * step, step)
        age = jnp.broadcast_to(cols[pl.ds(r0, step), 2 * heads : 2 * heads + 1], (step, 128))
        near = [age >= d for d in range(taps)]
        for j in range(lbs + 2):
            lanes = pl.ds(j * 128, 128)
            win = u[pl.ds(r0, step + HALO), pl.ds((j if j < lbs else j + lbs) * 128, 128)]
            if j < lbs:
                wl, wt, wb = lanes, wconv_x, bconv_x
            else:
                wl, wt, wb = pl.ds((j - lbs) * 128, 128), wconv_bc, bconv_bc
            total = jnp.broadcast_to(wb[:, wl], (step, 128))
            for k in range(taps):
                d = taps - 1 - k
                shifted = win if d == 0 else pltpu.roll(win, d, 0)
                term = shifted[HALO:, :] * wt[pl.ds(k, 1), wl]
                total = total + (term if d == 0 else jnp.where(near[d], term, 0.0))
            out = silu(total)
            if j < lbs:
                xc[pl.ds(r0, step), lanes] = out.astype(BF16)
            elif j == lbs:
                bcol[pl.ds(r0, step), :] = out.astype(BF16).astype(F32)
            else:
                ccol[pl.ds(r0, step), :] = out.astype(BF16)

    btf[...] = jnp.transpose(bcol[...])
    btr[...] = btf[...].astype(BF16)

    low_state = lax.broadcasted_iota(jnp.int32, (state, 128), 1) < 64

    def state_of(weight, lb):
        pair = [
            (btf[...] * weight[2 * lb + k : 2 * lb + k + 1, :]).astype(BF16) for k in range(2)
        ]
        both = jnp.dot(
            jnp.concatenate(pair, axis=0), xc[:, pl.ds(lb * 128, 128)],
            preferred_element_type=F32,
        )
        value = jnp.where(low_state, both[0:state, :], both[state:, :])
        return value.astype(BF16).reshape(per, piece, 128)

    for lb in range(lbs):
        s_send[pl.ds(lb * per, per)] = state_of(w_end, lb)
    pl.semaphore_wait(barrier, nseq - 1 + nhead - 1)

    S, D, AB, V, H, PG = range(6)

    def offset(n):
        t, s = n // xs, n % xs
        dz = (zs // 2 + (1 - 2 * (t % 2)) * ((t + 1) // 2)) % zs
        dx = (xs // 2 + (1 - 2 * (s % 2)) * ((s + 1) // 2)) % xs
        return dx, dz

    def copy(kind, src, dst, n, to):
        return pltpu.make_async_remote_copy(
            src_ref=src, dst_ref=dst, send_sem=send_sem.at[kind, n], recv_sem=recv_sem.at[kind, n],
            device_id={"seq": to}, device_id_type=MESH,
        )

    x_order = [(xs // 2 + (1 - 2 * (k % 2)) * ((k + 1) // 2)) % xs for k in range(xs)]
    x_part = [lax.rem(my_x + dx, xs) * zs for dx in x_order]

    def out_copy(kind, n, to):
        if kind == S:
            return copy(S, s_send.at[to], s_buf.at[seq], n, to)
        if kind == D:
            return copy(D, d_send.at[to // per], d_buf.at[seq], n, to)
        if kind == AB:
            return copy(AB, ab_send.at[to], ab_buf.at[seq], n, to)
        if kind == V:
            return copy(V, v_send.at[to], v_buf.at[seq], n, to)
        if kind == H:
            return copy(H, h_send.at[to], h_buf.at[seq], n, to)
        return copy(PG, p_send.at[to], page_out.at[seq], n, to)

    def in_copy(kind, n):
        dx, dz = offset(n)
        frm = ((my_x + xs - dx) % xs) * zs + (my_z + zs - dz) % zs
        buf = (s_buf, d_buf, ab_buf, v_buf, h_buf, page_out)[kind]
        return copy(kind, buf.at[frm], buf.at[frm], n, frm)

    def start_all(*kinds):
        @pl.loop(0, zs - 1)
        def _(t):
            dz = zs // 2 + (1 - 2 * lax.rem(t, 2)) * ((t + 1) // 2)
            z_part = lax.rem(my_z + dz, zs)
            for k in range(xs):
                for kind in kinds:
                    out_copy(kind, t * xs + k, x_part[k] + z_part).start()

        for k in range(xs - 1):
            for kind in kinds:
                out_copy(kind, (zs - 1) * xs + k, x_part[k] + my_z).start()

    def arrive_all(*kinds):
        @pl.loop(0, nseq - 1)
        def _(n):
            for kind in kinds:
                in_copy(kind, n).wait_recv()

    start_all(S, D)
    for lb in range(lbs):
        for kind, weight in enumerate((w_a, w_b)):
            ab_send[pl.ds(lb * per, per), kind] = state_of(weight, lb)
    start_all(AB)
    s_buf[seq] = s_send[seq]
    d_buf[seq] = d_send[lb_me]
    ab_buf[seq] = ab_send[seq]

    tile = 128
    blocks = rows // tile
    for i in range(blocks):
        ri = pl.ds(i * tile, tile)
        reach = (i + 1) * tile
        sc = jnp.dot(ccol[ri, :], btr[:, 0:reach], preferred_element_type=F32)
        gap_i = i * tile + lax.broadcasted_iota(jnp.int32, (tile, reach), 0)
        gap_j = lax.broadcasted_iota(jnp.int32, (tile, reach), 1)
        back = (gap_i - gap_j).astype(F32)
        age = cols[ri, 2 * heads : 2 * heads + 1]
        scores[ri, 0:reach] = jnp.where((back >= 0.0) & (back <= age), sc, 0.0)
    low_t = lax.broadcasted_iota(jnp.int32, (tile, 128), 1) < 64
    for lb in range(lbs):
        lanes = pl.ds(lb * 128, 128)
        gain = jnp.where(low_row, skip_gain[2 * lb], skip_gain[2 * lb + 1])
        for i in range(blocks):
            ri = pl.ds(i * tile, tile)
            reach = (i + 1) * tile
            parts = []
            for hh in range(2):
                h = 2 * lb + hh
                gap = jnp.minimum(cols[ri, h : h + 1] - cum2[h : h + 1, 0:reach], 0.0)
                wgt = (scores[ri, 0:reach] * jnp.exp2(gap) * dt[h : h + 1, 0:reach]).astype(BF16)
                parts.append(jnp.dot(wgt, xc[0:reach, lanes], preferred_element_type=F32))
            y_loc[ri, lanes] = (
                jnp.where(low_t, parts[0], parts[1]) + gain * xc[ri, lanes].astype(F32)
            )

    @pl.loop(0, nseq)
    def _(q):
        kind = jnp.int32(2)
        at = jnp.int32(0)
        who = jnp.int32(prompts)
        for r in range(prompts):
            hit = page_ref[r] == q
            kind = jnp.where(hit, slot[r], kind)
            at = jnp.where(hit, block[r], at)
            who = jnp.where(hit & (block[r] == seq), r, who)
        where_ref[0, q] = kind
        where_ref[1, q] = jnp.clip(at, 0, nseq - 1)
        where_ref[2, q] = who

    v_rows = v_all.shape[1]
    v_all[prompts] = jnp.zeros((v_rows, 128), BF16)
    for r in range(prompts):
        local = jnp.clip(ends[r] - base, 0, rows - 1) + HALO
        for k in range(taps - 1):
            back = taps - 2 - k
            line = u[pl.ds(local - back, 1), :]
            keep = jnp.full((1, 128), ends[r] - back, jnp.int32) >= starts[r]
            for j in range(lbs):
                stage[k * lbs + j : k * lbs + j + 1, :] = jnp.where(
                    keep, line[:, j * 128 : (j + 1) * 128], 0.0
                )
            for j in range(2):
                at = (taps - 1) * lbs + 2 * k + j
                stage[at : at + 1, :] = jnp.where(
                    keep, line[:, (2 * lbs + j) * 128 : (2 * lbs + j + 1) * 128], 0.0
                )
        v_all[r] = stage[...].astype(BF16)

    @pl.loop(0, nseq)
    def _(q):
        v_send[q] = v_all[where_ref[2, q]]

    arrive_all(S, D)

    def advance(i, carried):
        h_all[i] = carried
        h_send[i] = carried.astype(BF16)
        return d_buf[i, 0:1, :] * carried + s_buf[i].astype(F32)

    lax.fori_loop(0, nseq, advance, jnp.zeros((piece, 128), F32))
    start_all(H)
    h_buf[seq] = h_send[seq]
    start_all(V)
    v_buf[seq] = v_send[seq]

    arrive_all(AB)

    @pl.loop(0, nseq)
    def _(q):
        kind = where_ref[0, q]
        at = where_ref[1, q]
        value = ab_buf[at, jnp.where(kind == 1, 1, 0)].astype(F32)
        first = value + d_buf[at, 1:2, :] * h_all[at]
        kinds = jnp.full((piece, 128), kind, jnp.int32)
        p_send[q] = jnp.where(kinds == 0, first, jnp.where(kinds == 1, value, 0.0)).astype(BF16)

    start_all(PG)
    page_out[seq] = p_send[seq]

    tile = 64
    low = lax.broadcasted_iota(jnp.int32, (tile, 128), 1) < 64
    lanes128 = lax.broadcasted_iota(jnp.int32, (tile, 128), 1)
    subl = lax.broadcasted_iota(jnp.int32, (tile, 128), 0)
    for g in range(rows // tile):
        ri = pl.ds(g * tile, tile)
        for lb in range(lbs):
            lanes = pl.ds(lb * 128, 128)
            at = heads + 2 * lb
            scores[ri, lanes] = silu(u[pl.ds(HALO + g * tile, tile), pl.ds(inner + lb * 128, 128)])
            spread[ri, lanes] = jnp.where(low, cols[ri, at : at + 1], cols[ri, at + 1 : at + 2])

    arrive_all(H)
    for g in range(rows // 128):
        line = jnp.zeros((1, 128), F32)
        for s in range(128 // tile):
            ri = pl.ds(g * 128 + s * tile, tile)
            total = jnp.zeros((tile, 128), F32)
            for lb in range(lbs):
                lanes = pl.ds(lb * 128, 128)
                hmat = h_buf[pl.ds(lb * per, per)].reshape(state, 128)
                ac = jnp.dot(ccol[ri, :], hmat, preferred_element_type=F32)
                yv = (y_loc[ri, lanes] + ac * spread[ri, lanes]).astype(BF16).astype(F32)
                gv = yv * scores[ri, lanes]
                gated[ri, lanes] = gv
                total = total + gv * gv
            col = jnp.sum(total, axis=1, keepdims=True)
            line = line + jnp.sum(
                jnp.where(lanes128 == subl + s * tile, col, 0.0), axis=0, keepdims=True
            )
        q_send[g : g + 1, :] = line

    q_copies = []
    for k in range(1, nhead):
        one = pltpu.make_async_remote_copy(
            src_ref=q_send, dst_ref=q_buf.at[head], send_sem=qs_sem.at[k], recv_sem=qr_sem.at[k],
            device_id={"head": (head + k) % nhead}, device_id_type=MESH,
        )
        one.start()
        q_copies.append(one)
    q_buf[head] = q_send[...]

    source = jnp.int32(0)
    found = jnp.int32(0)
    for r in range(prompts):
        hit = page_ref[r] == seq
        source = jnp.where(hit, block[r], source)
        found = jnp.where(hit, 1, found)
    source = jnp.clip(source, 0, nseq - 1)
    arrive_all(V)
    v_out[...] = jnp.where(
        jnp.full(v_out.shape, found, jnp.int32) == 1, v_buf[source].astype(F32), 0.0
    )

    for k in range(1, nhead):
        frm = (head + nhead - k) % nhead
        pltpu.make_async_remote_copy(
            src_ref=q_send, dst_ref=q_buf.at[frm], send_sem=qs_sem.at[k], recv_sem=qr_sem.at[k],
            device_id={"head": frm}, device_id_type=MESH,
        ).wait_recv()
    squares = q_buf[0]
    for k in range(1, nhead):
        squares = squares + q_buf[k]
    scale_out[...] = lax.rsqrt(squares / (inner * nhead) + EPS)
    arrive_all(PG)

    @pl.loop(0, nseq - 1)
    def _(n):
        for kind in (S, D, AB, V, H, PG):
            in_copy(kind, n).wait_send()

    for one in q_copies:
        one.wait_send()


def run_block(u, dt_raw, wconv_x, bconv_x, wconv_bc, bconv_bc, step_bias, decay_log, skip,
              lengths, pages, nseq, nhead):
    rows, inner = dt_raw.shape[0] - HALO, wconv_x.shape[1]
    state = wconv_bc.shape[1] // 2
    lbs = inner // 128
    piece = state * lbs // nseq
    prompts = lengths.shape[0]
    xs = 4
    tiles = (nseq, piece, 128)
    v_rows = 24
    return pl.pallas_call(
        functools.partial(block_kernel, xs, nseq // xs, nhead),
        name="block",
        out_shape=(
            jax.ShapeDtypeStruct((rows, inner), F32),
            jax.ShapeDtypeStruct((rows // 128, 128), F32),
            jax.ShapeDtypeStruct(tiles, BF16),
            jax.ShapeDtypeStruct((v_rows, 128), F32),
            jax.ShapeDtypeStruct((1,), jnp.int32),
        ),
        in_specs=[smem()] * 5 + [vmem()] * 6,
        out_specs=(vmem(),) * 4 + (smem(),),
        scratch_shapes=[
            pltpu.VMEM((rows, inner), BF16),
            pltpu.VMEM((rows, state), F32),
            pltpu.VMEM((state, rows), F32),
            pltpu.VMEM((rows, state), BF16),
            pltpu.VMEM((state, rows), BF16),
            pltpu.VMEM((rows, max(rows, inner)), F32),
            pltpu.VMEM((rows, inner), F32),
            pltpu.VMEM((rows, 128), F32),
            pltpu.VMEM((v_rows, 128), F32),
            pltpu.VMEM((rows, inner), F32),
            pltpu.VMEM(tiles, BF16),
            pltpu.VMEM((lbs, 2, 128), F32),
            pltpu.VMEM((nseq, 2, piece, 128), BF16),
            pltpu.VMEM((prompts + 1, v_rows, 128), BF16),
            pltpu.VMEM((nseq, v_rows, 128), BF16),
            pltpu.VMEM(tiles, BF16),
            pltpu.VMEM((nseq, 2, 128), F32),
            pltpu.VMEM((nseq, 2, piece, 128), BF16),
            pltpu.VMEM((nseq, v_rows, 128), BF16),
            pltpu.VMEM(tiles, F32),
            pltpu.VMEM(tiles, BF16),
            pltpu.VMEM(tiles, BF16),
            pltpu.VMEM(tiles, BF16),
            pltpu.VMEM((rows // 128, 128), F32),
            pltpu.VMEM((nhead, rows // 128, 128), F32),
            pltpu.SMEM((3, nseq), jnp.int32),
            pltpu.SemaphoreType.DMA((6, nseq)),
            pltpu.SemaphoreType.DMA((6, nseq)),
            pltpu.SemaphoreType.DMA((nhead,)),
            pltpu.SemaphoreType.DMA((nhead,)),
        ],
        compiler_params=pltpu.CompilerParams(
            collective_id=1, has_side_effects=True, vmem_limit_bytes=40 << 20
        ),
    )(lengths, pages, step_bias, decay_log, skip, u, dt_raw, wconv_x, bconv_x, wconv_bc,
      bconv_bc)


def write_kernel(gated, scale_rows, pages, v, gain, n_out, page_out, cx_out, cb_out):
    rows, inner = gated.shape
    lbs = inner // 128
    per = pages.shape[0] // lbs
    state = per * pages.shape[1]
    tile = 64
    lanes128 = lax.broadcasted_iota(jnp.int32, (tile, 128), 1)
    subl = lax.broadcasted_iota(jnp.int32, (tile, 128), 0)
    for g in range(rows // 128):
        for s in range(128 // tile):
            ri = pl.ds(g * 128 + s * tile, tile)
            diag = jnp.where(lanes128 == subl + s * tile, scale_rows[g : g + 1, :], 0.0)
            scale = jnp.sum(diag, axis=1, keepdims=True)
            n_out[ri, :] = (gated[ri, :] * scale * gain[...]).astype(BF16)
    for lb in range(lbs):
        mat = pages[pl.ds(lb * per, per)].reshape(state, 128).astype(F32)
        page_out[pl.ds(lb * 128, 128), :] = jnp.transpose(mat)
    kept = cx_out.shape[0]
    for k in range(kept):
        for j in range(lbs):
            cx_out[k, :, j * 128 : (j + 1) * 128] = v[k * lbs + j : k * lbs + j + 1, :]
        for j in range(2):
            at = kept * lbs + 2 * k + j
            cb_out[k, :, j * 128 : (j + 1) * 128] = v[at : at + 1, :]


def write(gated, scale_rows, pages, v, gain, state, kept):
    rows, inner = gated.shape
    return pl.pallas_call(
        write_kernel,
        name="write",
        out_shape=(
            jax.ShapeDtypeStruct((rows, inner), BF16),
            jax.ShapeDtypeStruct((inner, state), F32),
            jax.ShapeDtypeStruct((kept, 1, inner), F32),
            jax.ShapeDtypeStruct((kept, 1, 2 * state), F32),
        ),
        in_specs=[vmem()] * 5,
        out_specs=(vmem(),) * 4,
        compiler_params=pltpu.CompilerParams(vmem_limit_bytes=8 << 20),
    )(gated, scale_rows, pages, v, gain)


def crowded_pages(
    u, dt_raw, wconv_x, bconv_x, wconv_bc, bconv_bc, step_bias, decay_log, lengths, pages
):
    rows = dt_raw.shape[0] - HALO
    heads = step_bias.shape[0]
    inner = wconv_x.shape[1]
    state = wconv_bc.shape[1] // 2
    taps = wconv_x.shape[0]
    prompts = lengths.shape[0]
    nseq = lax.axis_size("seq")
    base = lax.axis_index("seq") * rows
    ends = jnp.cumsum(lengths) - 1
    starts = ends - lengths + 1
    pos = base + jnp.arange(rows, dtype=jnp.int32)
    age = pos - jnp.max(jnp.where(starts[None] <= pos[:, None], starts[None], 0), axis=1)
    weight = jnp.concatenate([wconv_x, wconv_bc], axis=1)[:, : inner + state]
    total = jnp.concatenate([bconv_x, bconv_bc])[None, : inner + state]
    joined = jnp.concatenate([u[:, :inner], u[:, 2 * inner : 2 * inner + state]], axis=1)
    for k in range(taps):
        d = taps - 1 - k
        term = joined[HALO - d : HALO - d + rows] * weight[k][None]
        total = total + jnp.where((age >= d)[:, None], term, 0.0)
    conv = jax.nn.silu(total).astype(BF16)
    x, b = conv[:, :inner], conv[:, inner:]
    dt = jax.nn.softplus(dt_raw[HALO:, :heads] + step_bias[None])
    cum = jnp.cumsum(-dt * jnp.exp(decay_log)[None], axis=0)
    block = ends // rows
    before = jnp.concatenate([jnp.full((1,), -1, block.dtype), block[:-1]])
    after = jnp.concatenate([block[1:], jnp.full((1,), -1, block.dtype)])
    mine = (before == block) & (after == block) & (block == lax.axis_index("seq"))
    at_end = cum[jnp.clip(ends - base, 0, rows - 1)]
    keep = mine[:, None] & (pos[None] >= starts[:, None]) & (pos[None] <= ends[:, None])
    scale = jnp.where(
        keep[:, :, None], jnp.exp(jnp.minimum(at_end[:, None] - cum[None], 0.0)) * dt[None], 0.0
    )
    x_heads = x.reshape(rows, heads, -1).astype(F32)
    weighted = (scale[:, :, :, None] * x_heads[None]).astype(BF16).reshape(prompts, rows, inner)
    finals = jnp.einsum("rjc,jn->rcn", weighted, b, preferred_element_type=F32)
    hits = (pages[None, :] == jnp.arange(nseq, dtype=jnp.int32)[:, None]).astype(BF16)
    pool = jnp.einsum("qr,rcn->qcn", hits, finals.astype(BF16), preferred_element_type=F32)
    moved = lax.all_to_all(pool.astype(BF16), "seq", 0, 0, tiled=True)
    return jnp.sum(moved.astype(F32), axis=0)


def body(
    tokens, weight_x, weight_z, weight_bc, weight_dt, conv_x_weight, conv_x_bias,
    conv_bc_weight, conv_bc_bias, step_bias, decay_log, skip_gain, norm_gain, lengths, page_table,
):
    nseq, nhead = lax.axis_size("seq"), lax.axis_size("head")
    heads = weight_dt.shape[0]
    inner = weight_x.shape[1]
    width = inner // heads
    kept = conv_x_weight.shape[0] - 1
    u, dt_raw = project(tokens, weight_x, weight_z, weight_bc, weight_dt, nseq, nhead)
    gated, scale, pages, v, more = run_block(
        u, dt_raw, conv_x_weight, conv_x_bias[None, :], conv_bc_weight,
        conv_bc_bias[None, :], step_bias, decay_log, skip_gain, lengths, page_table, nseq, nhead,
    )
    normed, page, conv_x, conv_bc = write(
        gated, scale, pages, v, norm_gain[None, :], conv_bc_weight.shape[1] // 2, kept
    )
    page = lax.cond(
        more[0] > 0,
        lambda page, *rest: page + crowded_pages(*rest),
        lambda page, *rest: page,
        page, u, dt_raw, conv_x_weight, conv_x_bias, conv_bc_weight, conv_bc_bias, step_bias,
        decay_log, lengths, page_table,
    )
    return (
        normed, page.reshape(1, heads, width, -1), jnp.swapaxes(conv_x, 0, 1), jnp.swapaxes(conv_bc, 0, 1),
    )


def solution(mesh):
    in_specs = (
        P("seq", "head"), P(None, "head"), P(None, "head"), P(), P("head", None),
        P(None, "head"), P("head"), P(), P(), P("head"), P("head"), P("head"), P("head"),
        P(), P(),
    )
    out_specs = (
        P("seq", "head"), P("seq", "head", None, None), P("seq", None, "head"),
        P("seq", None, None),
    )
    return jax.shard_map(body, mesh=mesh, in_specs=in_specs, out_specs=out_specs, check_vma=False)
```

```python
import functools

import jax
import jax.numpy as jnp
from jax import lax
from jax.experimental import pallas as pl
from jax.experimental.pallas import tpu as pltpu
from jax.sharding import PartitionSpec as P

MESH = pl.DeviceIdType.MESH
F32 = jnp.float32
BF16 = jnp.bfloat16
EPS = 1e-05
HALO = 16
PROJECT_VMEM = (60 << 20) + (1 << 19)
LOG2E = 1.4426950408889634


def vmem():
    return pl.BlockSpec(memory_space=pltpu.VMEM)


def hbm():
    return pl.BlockSpec(memory_space=pltpu.HBM)


def smem():
    return pl.BlockSpec(memory_space=pltpu.SMEM)


def project_kernel(
    nseq, nhead,
    tok, wx, wz, wbc, wdt,
    acc, accdt,
    tokbuf, w, wdtp,
    lsem, ssem, rsem, hs_sem, hr_sem,
):
    ny = nhead // 2
    seq = lax.axis_index("seq")
    head = lax.axis_index("head")
    y = head // 2
    core = head % 2
    rows, feat = tok.shape
    half = rows // 2
    inner = wx.shape[1]
    wide = wbc.shape[1]
    heads = wdt.shape[0]
    yp, ym = (y + 1) % ny, (y + ny - 1) % ny
    y2 = (y + 2) % ny
    other = y * 2 + (1 - core)
    nxt, prv = (seq + 1) % nseq, (seq + nseq - 1) % nseq
    lanes = pl.ds(pl.multiple_of(core * feat, feat), feat)
    other_lanes = pl.ds(pl.multiple_of((1 - core) * feat, feat), feat)
    part = [pl.ds(HALO + q * half, half) for q in range(2)]
    from_tok = [pl.ds(q * half, half) for q in range(2)]
    both = pl.ds(HALO, rows)
    edge = pl.ds(0, HALO)

    loads = [
        pltpu.make_async_copy(tok, tokbuf.at[y, both, lanes], lsem.at[0]),
        pltpu.make_async_copy(wx, w.at[:, pl.ds(0, inner)], lsem.at[1]),
        pltpu.make_async_copy(wbc, w.at[:, pl.ds(2 * inner, wide)], lsem.at[2]),
        pltpu.make_async_copy(wz, w.at[:, pl.ds(inner, inner)], lsem.at[3]),
        pltpu.make_async_copy(wdt, wdtp.at[pl.ds(0, heads)], lsem.at[4]),
    ]

    barrier = pltpu.get_barrier_semaphore()
    for k in range(1, nhead):
        pl.semaphore_signal(
            barrier, inc=1, device_id={"head": (head + k) % nhead}, device_id_type=MESH
        )
    pl.semaphore_signal(barrier, inc=1, device_id={"seq": nxt}, device_id_type=MESH)
    pl.semaphore_signal(barrier, inc=1, device_id={"seq": prv}, device_id_type=MESH)
    wdtp[pl.ds(heads, 128 - heads), :] = jnp.zeros((128 - heads, wdtp.shape[1]), BF16)
    for one in loads:
        one.start()
    pl.semaphore_wait(barrier, nhead + 1)

    sent = []

    def send(src, dst, kind, q, to):
        copy = pltpu.make_async_remote_copy(
            src_ref=src, dst_ref=dst, send_sem=ssem.at[kind, q], recv_sem=rsem.at[kind, q],
            device_id=to, device_id_type=MESH,
        )
        copy.start()
        sent.append(copy)

    def arrive(region, kind, q):
        pltpu.make_async_remote_copy(
            src_ref=region, dst_ref=region, send_sem=ssem.at[kind, q], recv_sem=rsem.at[kind, q],
            device_id={"head": other}, device_id_type=MESH,
        ).wait_recv()

    UP, DOWN, RELAY, FWD_M, FWD_P, FWD_2, OWN, EDGE = range(8)
    to_up, to_down = {"head": yp * 2 + core}, {"head": ym * 2 + core}
    to_other = {"head": other}

    def piece(owner, q, core_lanes=lanes):
        return tokbuf.at[owner, part[q], core_lanes]

    mine = tokbuf.at[y]
    send(tok.at[pl.ds(rows - HALO, HALO)], mine.at[edge, lanes], EDGE, 0, {"seq": nxt})
    for q in range(2):
        send(tok.at[from_tok[q]], piece(y, q), UP, q, to_up)
        send(tok.at[from_tok[1 - q]], piece(y, 1 - q), DOWN, 1 - q, to_down)
        if q == 0:
            send(tok, mine.at[both, lanes], OWN, 0, to_other)
    def halo_piece(owner):
        return tokbuf.at[
            owner // 2, edge, pl.ds(pl.multiple_of((owner % 2) * feat, feat), feat)
        ]

    def halo_arrive(owner):
        pltpu.make_async_remote_copy(
            src_ref=halo_piece(owner), dst_ref=halo_piece(owner),
            send_sem=hs_sem.at[0], recv_sem=hr_sem.at[owner],
            device_id={"head": other}, device_id_type=MESH,
        ).wait_recv()

    tile = 256
    tiles = (2 * inner + wide) // tile

    def multiply(at, start, low, high):
        k = pl.ds(pl.multiple_of(at * 2 * feat, 2 * feat), 2 * feat)
        rs = pl.ds(low, high - low)

        @pl.loop(0, tiles)
        def _(n):
            cols = pl.ds(pl.multiple_of(n * tile, tile), tile)
            value = jnp.dot(tokbuf[at, rs, :], w[k, cols], preferred_element_type=F32)
            if start:
                acc[rs, cols] = value
            else:
                acc[rs, cols] += value

        value = lax.dot_general(
            tokbuf[at, rs, :], wdtp[:, k], (((1,), (1,)), ((), ())),
            preferred_element_type=F32,
        )
        if start:
            accdt[rs, :] = value
        else:
            accdt[rs, :] += value

    cut, full = HALO + half, HALO + rows

    def forward(owner, q, kind, onward):
        arrive(piece(owner, q), kind, q)
        send(piece(owner, q), piece(owner, q), onward, q, to_other)

    def halo_of(chip):
        halo_arrive(chip * 2)
        halo_arrive(chip * 2 + 1)

    for one in loads:
        one.wait()
    arrive(mine.at[both, other_lanes], OWN, 0)
    multiply(y, True, cut, full)
    arrive(halo_piece(head), EDGE, 0)
    halo_sends = []
    for k in range(1, nhead):
        copy = pltpu.make_async_remote_copy(
            src_ref=halo_piece(head), dst_ref=halo_piece(head),
            send_sem=hs_sem.at[k], recv_sem=hr_sem.at[head],
            device_id={"head": (head + k) % nhead}, device_id_type=MESH,
        )
        copy.start()
        halo_sends.append(copy)

    arrive(piece(ym, 0), UP, 0)
    send(piece(ym, 0), piece(ym, 0), RELAY, 0, to_up)
    send(piece(ym, 0), piece(ym, 0), FWD_M, 0, to_other)
    arrive(piece(yp, 1), DOWN, 1)
    send(piece(yp, 1), piece(yp, 1), RELAY, 1, to_down)
    send(piece(yp, 1), piece(yp, 1), FWD_P, 1, to_other)
    halo_arrive(other)
    multiply(y, True, 0, cut)
    arrive(piece(ym, 0, other_lanes), FWD_M, 0)
    halo_of(ym)
    multiply(ym, False, 0, cut)
    forward(ym, 1, UP, FWD_M)
    forward(yp, 0, DOWN, FWD_P)
    arrive(piece(yp, 1, other_lanes), FWD_P, 1)
    multiply(yp, False, cut, full)
    arrive(piece(ym, 1, other_lanes), FWD_M, 1)
    multiply(ym, False, cut, full)
    forward(y2, 0, RELAY, FWD_2)
    forward(y2, 1, RELAY, FWD_2)
    arrive(piece(yp, 0, other_lanes), FWD_P, 0)
    halo_of(yp)
    multiply(yp, False, 0, cut)
    arrive(piece(y2, 0, other_lanes), FWD_2, 0)
    halo_of(y2)
    multiply(y2, False, 0, cut)
    arrive(piece(y2, 1, other_lanes), FWD_2, 1)
    multiply(y2, False, cut, full)

    for copy in sent + halo_sends:
        copy.wait_send()


def project(tokens, weight_x, weight_z, weight_bc, weight_dt, nseq, nhead, interpret=False):
    rows, feat = tokens.shape
    depth, inner = weight_x.shape
    wide = weight_bc.shape[1]
    total = 2 * inner + wide
    return pl.pallas_call(
        functools.partial(project_kernel, nseq, nhead),
        name="project",
        out_shape=(
            jax.ShapeDtypeStruct((rows + HALO, total), F32),
            jax.ShapeDtypeStruct((rows + HALO, 128), F32),
        ),
        in_specs=[hbm()] * 5,
        out_specs=(vmem(), vmem()),
        scratch_shapes=[
            pltpu.VMEM((nhead // 2, rows + HALO, 2 * feat), BF16),
            pltpu.VMEM((depth, total), BF16),
            pltpu.VMEM((128, depth), BF16),
            pltpu.SemaphoreType.DMA((5,)),
            pltpu.SemaphoreType.DMA((8, 2)),
            pltpu.SemaphoreType.DMA((8, 2)),
            pltpu.SemaphoreType.DMA((nhead,)),
            pltpu.SemaphoreType.DMA((nhead,)),
        ],
        compiler_params=pltpu.CompilerParams(
            collective_id=0, has_side_effects=True, vmem_limit_bytes=PROJECT_VMEM
        ),
    )(tokens, weight_x, weight_z, weight_bc, weight_dt)


def silu(x):
    half = 0.5 * x
    return half + half * jnp.tanh(half)


def read_prompts(len_ref, count):
    starts, ends = [], []
    at = jnp.int32(0)
    for r in range(count):
        starts.append(at)
        at = at + len_ref[r]
        ends.append(at - 1)
    return starts, ends


def ends_in_block(starts, ends, base, rows):
    count = len(starts)
    none = jnp.int32(-1)
    a_start, a_end = none, none
    b_start, b_end = none, none
    a_at = none
    for r in range(count - 1, -1, -1):
        here = (ends[r] >= base) & (ends[r] < base + rows)
        a_start = jnp.where(here, starts[r], a_start)
        a_end = jnp.where(here, ends[r], a_end)
        a_at = jnp.where(here, r, a_at)
    for r in range(count):
        here = (ends[r] >= base) & (ends[r] < base + rows) & (a_at != r)
        b_start = jnp.where(here, starts[r], b_start)
        b_end = jnp.where(here, ends[r], b_end)
    return a_start, a_end, b_start, b_end


def end_slots(starts, ends, rows):
    prompts = len(starts)
    slot, block = [], []
    for r in range(prompts):
        at = ends[r] // rows
        a = jnp.bool_(True) if r == 0 else (ends[r - 1] // rows) != at
        b = jnp.bool_(True) if r == prompts - 1 else (ends[r + 1] // rows) != at
        slot.append(jnp.where(a, 0, jnp.where(b, 1, 2)).astype(jnp.int32))
        block.append(at)
    return slot, block


def by_head(values, shape):
    which = lax.broadcasted_iota(jnp.int32, shape, 0)
    out = jnp.zeros(shape, F32)
    for h in range(shape[0]):
        out = jnp.where(which == h, values[h], out)
    return out


def block_kernel(
    xs, zs, nhead,
    len_ref, page_ref, step_bias, decay_log, skip_gain,
    u, dt_raw, wconv_x, bconv_x, wconv_bc, bconv_bc,
    gated, scale_out, page_out, v_out, more_out,
    xc, bcol, btf, ccol, btr, scores, spread, cols, stage, y_loc,
    s_send, d_send, ab_send, v_all, v_send, s_buf, d_buf, ab_buf, v_buf,
    h_all, h_send, h_buf, p_send, q_send, q_buf, where_ref,
    send_sem, recv_sem, qs_sem, qr_sem,
):
    nseq = xs * zs
    seq = lax.axis_index("seq")
    head = lax.axis_index("head")
    my_x, my_z = seq // zs, seq % zs
    rows, inner = xc.shape
    state = ccol.shape[1]
    heads = step_bias.shape[0]
    lbs = inner // 128
    per = nseq // lbs
    piece = state // per
    prompts = len_ref.shape[0]
    taps = wconv_x.shape[0]
    lb_me = seq // per
    base = seq * rows

    barrier = pltpu.get_barrier_semaphore()

    @pl.loop(1, nseq)
    def _(d):
        pl.semaphore_signal(
            barrier, inc=1, device_id={"seq": (seq + d) % nseq}, device_id_type=MESH
        )

    for k in range(1, nhead):
        pl.semaphore_signal(
            barrier, inc=1, device_id={"head": (head + k) % nhead}, device_id_type=MESH
        )

    starts, ends = read_prompts(len_ref, prompts)
    slot, block = end_slots(starts, ends, rows)
    more = jnp.int32(0)
    for kind in slot:
        more = jnp.maximum(more, kind - 1)
    more_out[0] = more

    def start_of(pos):
        found = jnp.zeros_like(pos)
        for r in range(prompts):
            found = jnp.where(starts[r] <= pos, starts[r], found)
        return found

    dtr = jnp.transpose(dt_raw[pl.ds(HALO, rows), :])[0:heads, :]
    pre = dtr + by_head(step_bias, (heads, rows))
    dt = jnp.maximum(pre, 0.0) + jnp.log1p(jnp.exp(-jnp.abs(pre)))
    cum = -dt * jnp.exp(by_head(decay_log, (heads, rows)))
    lane = lax.broadcasted_iota(jnp.int32, (heads, rows), 1)
    shift = 1
    while shift < rows:
        cum = cum + jnp.where(lane >= shift, pltpu.roll(cum, shift, 1), 0.0)
        shift *= 2
    pos = base + lane
    start_row = start_of(pos)
    a_start, a_end, b_start, b_end = ends_in_block(starts, ends, base, rows)
    last_start = start_of(jnp.full((heads, rows), base + rows - 1, jnp.int32))

    def at_pos(where_pos):
        return jnp.sum(jnp.where(pos == where_pos, cum, 0.0), axis=1, keepdims=True)

    cum_last = at_pos(base + rows - 1)
    cum_a, cum_b = at_pos(a_end), at_pos(b_end)

    def weight_to(cum_end, keep):
        return jnp.where(keep, jnp.exp(jnp.minimum(cum_end - cum, 0.0)), 0.0) * dt

    w_end = weight_to(cum_last, pos >= last_start)
    w_a = weight_to(cum_a, (pos >= a_start) & (pos <= a_end))
    w_b = weight_to(cum_b, (pos >= b_start) & (pos <= b_end))
    inflow = jnp.where(start_row < base, jnp.exp(cum), 0.0)
    decay = jnp.where(last_start[:, 0:1] < base, jnp.exp(cum_last), 0.0)
    decay_a = jnp.where(
        (jnp.full((heads, 1), a_start) < base) & (jnp.full((heads, 1), a_end) >= 0),
        jnp.exp(cum_a), 0.0,
    )
    cum2 = cum * LOG2E
    age_row = (pos - start_row).astype(F32)
    packed = jnp.concatenate(
        [cum2, inflow, age_row] + [jnp.zeros((128 - 3 * heads, rows), F32)], axis=0,
    )
    cols[...] = jnp.transpose(packed)
    low_row = lax.broadcasted_iota(jnp.int32, (1, 128), 1) < 64

    for lb in range(lbs):
        h0, h1 = 2 * lb, 2 * lb + 1
        for k, value in enumerate((decay, decay_a)):
            d_send[lb, pl.ds(k, 1), :] = jnp.where(
                low_row,
                jnp.broadcast_to(value[h0 : h0 + 1, :], (1, 128)),
                jnp.broadcast_to(value[h1 : h1 + 1, :], (1, 128)),
            )

    step = 64

    @pl.loop(0, rows // step)
    def _(t):
        r0 = pl.multiple_of(t * step, step)
        age = jnp.broadcast_to(cols[pl.ds(r0, step), 2 * heads : 2 * heads + 1], (step, 128))
        near = [age >= d for d in range(taps)]
        for j in range(lbs + 2):
            lanes = pl.ds(j * 128, 128)
            win = u[pl.ds(r0, step + HALO), pl.ds((j if j < lbs else j + lbs) * 128, 128)]
            if j < lbs:
                wl, wt, wb = lanes, wconv_x, bconv_x
            else:
                wl, wt, wb = pl.ds((j - lbs) * 128, 128), wconv_bc, bconv_bc
            total = jnp.broadcast_to(wb[:, wl], (step, 128))
            for k in range(taps):
                d = taps - 1 - k
                shifted = win if d == 0 else pltpu.roll(win, d, 0)
                term = shifted[HALO:, :] * wt[pl.ds(k, 1), wl]
                total = total + (term if d == 0 else jnp.where(near[d], term, 0.0))
            out = silu(total)
            if j < lbs:
                xc[pl.ds(r0, step), lanes] = out.astype(BF16)
            elif j == lbs:
                bcol[pl.ds(r0, step), :] = out.astype(BF16).astype(F32)
            else:
                ccol[pl.ds(r0, step), :] = out.astype(BF16)

    btf[...] = jnp.transpose(bcol[...])
    btr[...] = btf[...].astype(BF16)

    low_state = lax.broadcasted_iota(jnp.int32, (state, 128), 1) < 64

    def state_of(weight, lb):
        pair = [
            (btf[...] * weight[2 * lb + k : 2 * lb + k + 1, :]).astype(BF16) for k in range(2)
        ]
        both = jnp.dot(
            jnp.concatenate(pair, axis=0), xc[:, pl.ds(lb * 128, 128)],
            preferred_element_type=F32,
        )
        value = jnp.where(low_state, both[0:state, :], both[state:, :])
        return value.astype(BF16).reshape(per, piece, 128)

    for lb in range(lbs):
        s_send[pl.ds(lb * per, per)] = state_of(w_end, lb)
    pl.semaphore_wait(barrier, nseq - 1 + nhead - 1)

    S, D, AB, V, H, PG = range(6)

    def offset(n):
        t, s = n // xs, n % xs
        dz = (zs // 2 + (1 - 2 * (t % 2)) * ((t + 1) // 2)) % zs
        dx = (xs // 2 + (1 - 2 * (s % 2)) * ((s + 1) // 2)) % xs
        return dx, dz

    def copy(kind, src, dst, n, to):
        return pltpu.make_async_remote_copy(
            src_ref=src, dst_ref=dst, send_sem=send_sem.at[kind, n], recv_sem=recv_sem.at[kind, n],
            device_id={"seq": to}, device_id_type=MESH,
        )

    x_order = [(xs // 2 + (1 - 2 * (k % 2)) * ((k + 1) // 2)) % xs for k in range(xs)]
    x_part = [lax.rem(my_x + dx, xs) * zs for dx in x_order]

    def out_copy(kind, n, to):
        if kind == S:
            return copy(S, s_send.at[to], s_buf.at[seq], n, to)
        if kind == D:
            return copy(D, d_send.at[to // per], d_buf.at[seq], n, to)
        if kind == AB:
            return copy(AB, ab_send.at[to], ab_buf.at[seq], n, to)
        if kind == V:
            return copy(V, v_send.at[to], v_buf.at[seq], n, to)
        if kind == H:
            return copy(H, h_send.at[to], h_buf.at[seq], n, to)
        return copy(PG, p_send.at[to], page_out.at[seq], n, to)

    def in_copy(kind, n):
        dx, dz = offset(n)
        frm = ((my_x + xs - dx) % xs) * zs + (my_z + zs - dz) % zs
        buf = (s_buf, d_buf, ab_buf, v_buf, h_buf, page_out)[kind]
        return copy(kind, buf.at[frm], buf.at[frm], n, frm)

    def start_all(*kinds):
        @pl.loop(0, zs - 1)
        def _(t):
            dz = zs // 2 + (1 - 2 * lax.rem(t, 2)) * ((t + 1) // 2)
            z_part = lax.rem(my_z + dz, zs)
            for k in range(xs):
                for kind in kinds:
                    out_copy(kind, t * xs + k, x_part[k] + z_part).start()

        for k in range(xs - 1):
            for kind in kinds:
                out_copy(kind, (zs - 1) * xs + k, x_part[k] + my_z).start()

    def arrive_all(*kinds):
        @pl.loop(0, nseq - 1)
        def _(n):
            for kind in kinds:
                in_copy(kind, n).wait_recv()

    start_all(S, D)
    for lb in range(lbs):
        for kind, weight in enumerate((w_a, w_b)):
            ab_send[pl.ds(lb * per, per), kind] = state_of(weight, lb)
    start_all(AB)
    s_buf[seq] = s_send[seq]
    d_buf[seq] = d_send[lb_me]
    ab_buf[seq] = ab_send[seq]

    tile = 128
    blocks = rows // tile
    for i in range(blocks):
        ri = pl.ds(i * tile, tile)
        reach = (i + 1) * tile
        sc = jnp.dot(ccol[ri, :], btr[:, 0:reach], preferred_element_type=F32)
        gap_i = i * tile + lax.broadcasted_iota(jnp.int32, (tile, reach), 0)
        gap_j = lax.broadcasted_iota(jnp.int32, (tile, reach), 1)
        back = (gap_i - gap_j).astype(F32)
        age = cols[ri, 2 * heads : 2 * heads + 1]
        scores[ri, 0:reach] = jnp.where((back >= 0.0) & (back <= age), sc, 0.0)
    low_t = lax.broadcasted_iota(jnp.int32, (tile, 128), 1) < 64
    for lb in range(lbs):
        lanes = pl.ds(lb * 128, 128)
        gain = jnp.where(low_row, skip_gain[2 * lb], skip_gain[2 * lb + 1])
        for i in range(blocks):
            ri = pl.ds(i * tile, tile)
            reach = (i + 1) * tile
            parts = []
            for hh in range(2):
                h = 2 * lb + hh
                gap = jnp.minimum(cols[ri, h : h + 1] - cum2[h : h + 1, 0:reach], 0.0)
                wgt = (scores[ri, 0:reach] * jnp.exp2(gap) * dt[h : h + 1, 0:reach]).astype(BF16)
                parts.append(jnp.dot(wgt, xc[0:reach, lanes], preferred_element_type=F32))
            y_loc[ri, lanes] = (
                jnp.where(low_t, parts[0], parts[1]) + gain * xc[ri, lanes].astype(F32)
            )

    @pl.loop(0, nseq)
    def _(q):
        kind = jnp.int32(2)
        at = jnp.int32(0)
        who = jnp.int32(prompts)
        for r in range(prompts):
            hit = page_ref[r] == q
            kind = jnp.where(hit, slot[r], kind)
            at = jnp.where(hit, block[r], at)
            who = jnp.where(hit & (block[r] == seq), r, who)
        where_ref[0, q] = kind
        where_ref[1, q] = jnp.clip(at, 0, nseq - 1)
        where_ref[2, q] = who

    v_rows = v_all.shape[1]
    v_all[prompts] = jnp.zeros((v_rows, 128), BF16)
    for r in range(prompts):
        local = jnp.clip(ends[r] - base, 0, rows - 1) + HALO
        for k in range(taps - 1):
            back = taps - 2 - k
            line = u[pl.ds(local - back, 1), :]
            keep = jnp.full((1, 128), ends[r] - back, jnp.int32) >= starts[r]
            for j in range(lbs):
                stage[k * lbs + j : k * lbs + j + 1, :] = jnp.where(
                    keep, line[:, j * 128 : (j + 1) * 128], 0.0
                )
            for j in range(2):
                at = (taps - 1) * lbs + 2 * k + j
                stage[at : at + 1, :] = jnp.where(
                    keep, line[:, (2 * lbs + j) * 128 : (2 * lbs + j + 1) * 128], 0.0
                )
        v_all[r] = stage[...].astype(BF16)

    @pl.loop(0, nseq)
    def _(q):
        v_send[q] = v_all[where_ref[2, q]]

    arrive_all(S, D)

    def advance(i, carried):
        h_all[i] = carried
        h_send[i] = carried.astype(BF16)
        return d_buf[i, 0:1, :] * carried + s_buf[i].astype(F32)

    lax.fori_loop(0, nseq, advance, jnp.zeros((piece, 128), F32))
    start_all(H)
    h_buf[seq] = h_send[seq]
    start_all(V)
    v_buf[seq] = v_send[seq]

    arrive_all(AB)

    @pl.loop(0, nseq)
    def _(q):
        kind = where_ref[0, q]
        at = where_ref[1, q]
        value = ab_buf[at, jnp.where(kind == 1, 1, 0)].astype(F32)
        first = value + d_buf[at, 1:2, :] * h_all[at]
        kinds = jnp.full((piece, 128), kind, jnp.int32)
        p_send[q] = jnp.where(kinds == 0, first, jnp.where(kinds == 1, value, 0.0)).astype(BF16)

    start_all(PG)
    page_out[seq] = p_send[seq]

    tile = 64
    low = lax.broadcasted_iota(jnp.int32, (tile, 128), 1) < 64
    lanes128 = lax.broadcasted_iota(jnp.int32, (tile, 128), 1)
    subl = lax.broadcasted_iota(jnp.int32, (tile, 128), 0)
    for g in range(rows // tile):
        ri = pl.ds(g * tile, tile)
        for lb in range(lbs):
            lanes = pl.ds(lb * 128, 128)
            at = heads + 2 * lb
            scores[ri, lanes] = silu(u[pl.ds(HALO + g * tile, tile), pl.ds(inner + lb * 128, 128)])
            spread[ri, lanes] = jnp.where(low, cols[ri, at : at + 1], cols[ri, at + 1 : at + 2])

    arrive_all(H)
    for g in range(rows // 128):
        line = jnp.zeros((1, 128), F32)
        for s in range(128 // tile):
            ri = pl.ds(g * 128 + s * tile, tile)
            total = jnp.zeros((tile, 128), F32)
            for lb in range(lbs):
                lanes = pl.ds(lb * 128, 128)
                hmat = h_buf[pl.ds(lb * per, per)].reshape(state, 128)
                ac = jnp.dot(ccol[ri, :], hmat, preferred_element_type=F32)
                yv = (y_loc[ri, lanes] + ac * spread[ri, lanes]).astype(BF16).astype(F32)
                gv = yv * scores[ri, lanes]
                gated[ri, lanes] = gv
                total = total + gv * gv
            col = jnp.sum(total, axis=1, keepdims=True)
            line = line + jnp.sum(
                jnp.where(lanes128 == subl + s * tile, col, 0.0), axis=0, keepdims=True
            )
        q_send[g : g + 1, :] = line

    q_copies = []
    for k in range(1, nhead):
        one = pltpu.make_async_remote_copy(
            src_ref=q_send, dst_ref=q_buf.at[head], send_sem=qs_sem.at[k], recv_sem=qr_sem.at[k],
            device_id={"head": (head + k) % nhead}, device_id_type=MESH,
        )
        one.start()
        q_copies.append(one)
    q_buf[head] = q_send[...]

    source = jnp.int32(0)
    found = jnp.int32(0)
    for r in range(prompts):
        hit = page_ref[r] == seq
        source = jnp.where(hit, block[r], source)
        found = jnp.where(hit, 1, found)
    source = jnp.clip(source, 0, nseq - 1)
    arrive_all(V)
    v_out[...] = jnp.where(
        jnp.full(v_out.shape, found, jnp.int32) == 1, v_buf[source].astype(F32), 0.0
    )

    arrive_all(PG)

    @pl.loop(0, nseq - 1)
    def _(n):
        for kind in (S, D, AB, V, H, PG):
            in_copy(kind, n).wait_send()

    for k in range(1, nhead):
        frm = (head + nhead - k) % nhead
        pltpu.make_async_remote_copy(
            src_ref=q_send, dst_ref=q_buf.at[frm], send_sem=qs_sem.at[k], recv_sem=qr_sem.at[k],
            device_id={"head": frm}, device_id_type=MESH,
        ).wait_recv()
    squares = q_buf[0]
    for k in range(1, nhead):
        squares = squares + q_buf[k]
    scale_out[...] = lax.rsqrt(squares / (inner * nhead) + EPS)

    for one in q_copies:
        one.wait_send()


def run_block(u, dt_raw, wconv_x, bconv_x, wconv_bc, bconv_bc, step_bias, decay_log, skip,
              lengths, pages, nseq, nhead):
    rows, inner = dt_raw.shape[0] - HALO, wconv_x.shape[1]
    state = wconv_bc.shape[1] // 2
    lbs = inner // 128
    piece = state * lbs // nseq
    prompts = lengths.shape[0]
    xs = 4
    tiles = (nseq, piece, 128)
    v_rows = 24
    return pl.pallas_call(
        functools.partial(block_kernel, xs, nseq // xs, nhead),
        name="block",
        out_shape=(
            jax.ShapeDtypeStruct((rows, inner), F32),
            jax.ShapeDtypeStruct((rows // 128, 128), F32),
            jax.ShapeDtypeStruct(tiles, BF16),
            jax.ShapeDtypeStruct((v_rows, 128), F32),
            jax.ShapeDtypeStruct((1,), jnp.int32),
        ),
        in_specs=[smem()] * 5 + [vmem()] * 6,
        out_specs=(vmem(),) * 4 + (smem(),),
        scratch_shapes=[
            pltpu.VMEM((rows, inner), BF16),
            pltpu.VMEM((rows, state), F32),
            pltpu.VMEM((state, rows), F32),
            pltpu.VMEM((rows, state), BF16),
            pltpu.VMEM((state, rows), BF16),
            pltpu.VMEM((rows, max(rows, inner)), F32),
            pltpu.VMEM((rows, inner), F32),
            pltpu.VMEM((rows, 128), F32),
            pltpu.VMEM((v_rows, 128), F32),
            pltpu.VMEM((rows, inner), F32),
            pltpu.VMEM(tiles, BF16),
            pltpu.VMEM((lbs, 2, 128), F32),
            pltpu.VMEM((nseq, 2, piece, 128), BF16),
            pltpu.VMEM((prompts + 1, v_rows, 128), BF16),
            pltpu.VMEM((nseq, v_rows, 128), BF16),
            pltpu.VMEM(tiles, BF16),
            pltpu.VMEM((nseq, 2, 128), F32),
            pltpu.VMEM((nseq, 2, piece, 128), BF16),
            pltpu.VMEM((nseq, v_rows, 128), BF16),
            pltpu.VMEM(tiles, F32),
            pltpu.VMEM(tiles, BF16),
            pltpu.VMEM(tiles, BF16),
            pltpu.VMEM(tiles, BF16),
            pltpu.VMEM((rows // 128, 128), F32),
            pltpu.VMEM((nhead, rows // 128, 128), F32),
            pltpu.SMEM((3, nseq), jnp.int32),
            pltpu.SemaphoreType.DMA((6, nseq)),
            pltpu.SemaphoreType.DMA((6, nseq)),
            pltpu.SemaphoreType.DMA((nhead,)),
            pltpu.SemaphoreType.DMA((nhead,)),
        ],
        compiler_params=pltpu.CompilerParams(
            collective_id=1, has_side_effects=True, vmem_limit_bytes=40 << 20
        ),
    )(lengths, pages, step_bias, decay_log, skip, u, dt_raw, wconv_x, bconv_x, wconv_bc,
      bconv_bc)


def write_kernel(gated, scale_rows, pages, v, gain, n_out, page_out, cx_out, cb_out):
    rows, inner = gated.shape
    lbs = inner // 128
    per = pages.shape[0] // lbs
    state = per * pages.shape[1]
    tile = 64
    lanes128 = lax.broadcasted_iota(jnp.int32, (tile, 128), 1)
    subl = lax.broadcasted_iota(jnp.int32, (tile, 128), 0)
    for g in range(rows // 128):
        for s in range(128 // tile):
            ri = pl.ds(g * 128 + s * tile, tile)
            diag = jnp.where(lanes128 == subl + s * tile, scale_rows[g : g + 1, :], 0.0)
            scale = jnp.sum(diag, axis=1, keepdims=True)
            n_out[ri, :] = (gated[ri, :] * scale * gain[...]).astype(BF16)
    for lb in range(lbs):
        mat = pages[pl.ds(lb * per, per)].reshape(state, 128).astype(F32)
        page_out[pl.ds(lb * 128, 128), :] = jnp.transpose(mat)
    kept = cx_out.shape[0]
    for k in range(kept):
        for j in range(lbs):
            cx_out[k, :, j * 128 : (j + 1) * 128] = v[k * lbs + j : k * lbs + j + 1, :]
        for j in range(2):
            at = kept * lbs + 2 * k + j
            cb_out[k, :, j * 128 : (j + 1) * 128] = v[at : at + 1, :]


def write(gated, scale_rows, pages, v, gain, state, kept):
    rows, inner = gated.shape
    return pl.pallas_call(
        write_kernel,
        name="write",
        out_shape=(
            jax.ShapeDtypeStruct((rows, inner), BF16),
            jax.ShapeDtypeStruct((inner, state), F32),
            jax.ShapeDtypeStruct((kept, 1, inner), F32),
            jax.ShapeDtypeStruct((kept, 1, 2 * state), F32),
        ),
        in_specs=[vmem()] * 5,
        out_specs=(vmem(),) * 4,
        compiler_params=pltpu.CompilerParams(vmem_limit_bytes=8 << 20),
    )(gated, scale_rows, pages, v, gain)


def crowded_pages(
    u, dt_raw, wconv_x, bconv_x, wconv_bc, bconv_bc, step_bias, decay_log, lengths, pages
):
    rows = dt_raw.shape[0] - HALO
    heads = step_bias.shape[0]
    inner = wconv_x.shape[1]
    state = wconv_bc.shape[1] // 2
    taps = wconv_x.shape[0]
    prompts = lengths.shape[0]
    nseq = lax.axis_size("seq")
    base = lax.axis_index("seq") * rows
    ends = jnp.cumsum(lengths) - 1
    starts = ends - lengths + 1
    pos = base + jnp.arange(rows, dtype=jnp.int32)
    age = pos - jnp.max(jnp.where(starts[None] <= pos[:, None], starts[None], 0), axis=1)
    weight = jnp.concatenate([wconv_x, wconv_bc], axis=1)[:, : inner + state]
    total = jnp.concatenate([bconv_x, bconv_bc])[None, : inner + state]
    joined = jnp.concatenate([u[:, :inner], u[:, 2 * inner : 2 * inner + state]], axis=1)
    for k in range(taps):
        d = taps - 1 - k
        term = joined[HALO - d : HALO - d + rows] * weight[k][None]
        total = total + jnp.where((age >= d)[:, None], term, 0.0)
    conv = jax.nn.silu(total).astype(BF16)
    x, b = conv[:, :inner], conv[:, inner:]
    dt = jax.nn.softplus(dt_raw[HALO:, :heads] + step_bias[None])
    cum = jnp.cumsum(-dt * jnp.exp(decay_log)[None], axis=0)
    block = ends // rows
    before = jnp.concatenate([jnp.full((1,), -1, block.dtype), block[:-1]])
    after = jnp.concatenate([block[1:], jnp.full((1,), -1, block.dtype)])
    mine = (before == block) & (after == block) & (block == lax.axis_index("seq"))
    at_end = cum[jnp.clip(ends - base, 0, rows - 1)]
    keep = mine[:, None] & (pos[None] >= starts[:, None]) & (pos[None] <= ends[:, None])
    scale = jnp.where(
        keep[:, :, None], jnp.exp(jnp.minimum(at_end[:, None] - cum[None], 0.0)) * dt[None], 0.0
    )
    x_heads = x.reshape(rows, heads, -1).astype(F32)
    weighted = (scale[:, :, :, None] * x_heads[None]).astype(BF16).reshape(prompts, rows, inner)
    finals = jnp.einsum("rjc,jn->rcn", weighted, b, preferred_element_type=F32)
    hits = (pages[None, :] == jnp.arange(nseq, dtype=jnp.int32)[:, None]).astype(BF16)
    pool = jnp.einsum("qr,rcn->qcn", hits, finals.astype(BF16), preferred_element_type=F32)
    moved = lax.all_to_all(pool.astype(BF16), "seq", 0, 0, tiled=True)
    return jnp.sum(moved.astype(F32), axis=0)


def body(
    tokens, weight_x, weight_z, weight_bc, weight_dt, conv_x_weight, conv_x_bias,
    conv_bc_weight, conv_bc_bias, step_bias, decay_log, skip_gain, norm_gain, lengths, page_table,
):
    nseq, nhead = lax.axis_size("seq"), lax.axis_size("head")
    heads = weight_dt.shape[0]
    inner = weight_x.shape[1]
    width = inner // heads
    kept = conv_x_weight.shape[0] - 1
    u, dt_raw = project(tokens, weight_x, weight_z, weight_bc, weight_dt, nseq, nhead)
    gated, scale, pages, v, more = run_block(
        u, dt_raw, conv_x_weight, conv_x_bias[None, :], conv_bc_weight,
        conv_bc_bias[None, :], step_bias, decay_log, skip_gain, lengths, page_table, nseq, nhead,
    )
    normed, page, conv_x, conv_bc = write(
        gated, scale, pages, v, norm_gain[None, :], conv_bc_weight.shape[1] // 2, kept
    )
    page = lax.cond(
        more[0] > 0,
        lambda page, *rest: page + crowded_pages(*rest),
        lambda page, *rest: page,
        page, u, dt_raw, conv_x_weight, conv_x_bias, conv_bc_weight, conv_bc_bias, step_bias,
        decay_log, lengths, page_table,
    )
    return (
        normed, page.reshape(1, heads, width, -1), jnp.swapaxes(conv_x, 0, 1), jnp.swapaxes(conv_bc, 0, 1),
    )


def solution(mesh):
    in_specs = (
        P("seq", "head"), P(None, "head"), P(None, "head"), P(), P("head", None),
        P(None, "head"), P("head"), P(), P(), P("head"), P("head"), P("head"), P("head"),
        P(), P(),
    )
    out_specs = (
        P("seq", "head"), P("seq", "head", None, None), P("seq", None, "head"),
        P("seq", None, None),
    )
    return jax.shard_map(body, mesh=mesh, in_specs=in_specs, out_specs=out_specs, check_vma=False)
```

```python
import functools

import jax
import jax.numpy as jnp
from jax import lax
from jax.experimental import pallas as pl
from jax.experimental.pallas import tpu as pltpu
from jax.sharding import PartitionSpec as P

MESH = pl.DeviceIdType.MESH
F32 = jnp.float32
BF16 = jnp.bfloat16
EPS = 1e-05
HALO = 16
PROJECT_VMEM = (60 << 20) + (1 << 19)
LOG2E = 1.4426950408889634


def vmem():
    return pl.BlockSpec(memory_space=pltpu.VMEM)


def hbm():
    return pl.BlockSpec(memory_space=pltpu.HBM)


def smem():
    return pl.BlockSpec(memory_space=pltpu.SMEM)


def project_kernel(
    nseq, nhead,
    tok, wx, wz, wbc, wdt,
    acc, accdt,
    tokbuf, w, wdtp,
    lsem, ssem, rsem, hs_sem, hr_sem,
):
    ny = nhead // 2
    seq = lax.axis_index("seq")
    head = lax.axis_index("head")
    y = head // 2
    core = head % 2
    rows, feat = tok.shape
    half = rows // 2
    inner = wx.shape[1]
    wide = wbc.shape[1]
    heads = wdt.shape[0]
    yp, ym = (y + 1) % ny, (y + ny - 1) % ny
    y2 = (y + 2) % ny
    up, down = yp * 2 + core, ym * 2 + core
    other = y * 2 + (1 - core)
    nxt, prv = (seq + 1) % nseq, (seq + nseq - 1) % nseq
    lanes = pl.ds(pl.multiple_of(core * feat, feat), feat)
    other_lanes = pl.ds(pl.multiple_of((1 - core) * feat, feat), feat)
    first, second = pl.ds(HALO, half), pl.ds(HALO + half, half)
    both = pl.ds(HALO, rows)
    edge = pl.ds(0, HALO)

    loads = [
        pltpu.make_async_copy(tok, tokbuf.at[y, both, lanes], lsem.at[0]),
        pltpu.make_async_copy(wx, w.at[:, pl.ds(0, inner)], lsem.at[1]),
        pltpu.make_async_copy(wbc, w.at[:, pl.ds(2 * inner, wide)], lsem.at[2]),
        pltpu.make_async_copy(wz, w.at[:, pl.ds(inner, inner)], lsem.at[3]),
        pltpu.make_async_copy(wdt, wdtp.at[pl.ds(0, heads)], lsem.at[4]),
    ]

    barrier = pltpu.get_barrier_semaphore()
    for k in range(1, nhead):
        pl.semaphore_signal(
            barrier, inc=1, device_id={"head": (head + k) % nhead}, device_id_type=MESH
        )
    pl.semaphore_signal(barrier, inc=1, device_id={"seq": nxt}, device_id_type=MESH)
    pl.semaphore_signal(barrier, inc=1, device_id={"seq": prv}, device_id_type=MESH)
    wdtp[pl.ds(heads, 128 - heads), :] = jnp.zeros((128 - heads, wdtp.shape[1]), BF16)
    for one in loads:
        one.start()
    pl.semaphore_wait(barrier, nhead + 1)

    sent = []

    def send(src, dst, number, to):
        copy = pltpu.make_async_remote_copy(
            src_ref=src, dst_ref=dst, send_sem=ssem.at[number], recv_sem=rsem.at[number],
            device_id=to, device_id_type=MESH,
        )
        copy.start()
        sent.append(copy)

    def arrive(region, number):
        pltpu.make_async_remote_copy(
            src_ref=region, dst_ref=region, send_sem=ssem.at[number], recv_sem=rsem.at[number],
            device_id={"head": other}, device_id_type=MESH,
        ).wait_recv()

    to_up, to_down, to_other = {"head": up}, {"head": down}, {"head": other}
    mine = tokbuf.at[y]
    send(tok.at[pl.ds(rows - HALO, HALO)], mine.at[edge, lanes], 13, {"seq": nxt})
    send(tok.at[pl.ds(0, half)], mine.at[first, lanes], 1, to_up)
    send(tok.at[pl.ds(half, half)], mine.at[second, lanes], 3, to_down)
    send(tok, mine.at[both, lanes], 0, to_other)
    send(tok.at[pl.ds(half, half)], mine.at[second, lanes], 2, to_up)
    send(tok.at[pl.ds(0, half)], mine.at[first, lanes], 4, to_down)

    def halo_piece(owner):
        return tokbuf.at[
            owner // 2, edge, pl.ds(pl.multiple_of((owner % 2) * feat, feat), feat)
        ]

    arrive(halo_piece(head), 13)
    halo_sends = []
    for k in range(1, nhead):
        copy = pltpu.make_async_remote_copy(
            src_ref=halo_piece(head), dst_ref=halo_piece(head),
            send_sem=hs_sem.at[k], recv_sem=hr_sem.at[head],
            device_id={"head": (head + k) % nhead}, device_id_type=MESH,
        )
        copy.start()
        halo_sends.append(copy)

    def halo_arrive(owner):
        pltpu.make_async_remote_copy(
            src_ref=halo_piece(owner), dst_ref=halo_piece(owner),
            send_sem=hs_sem.at[0], recv_sem=hr_sem.at[owner],
            device_id={"head": other}, device_id_type=MESH,
        ).wait_recv()

    tile = 256
    tiles = (2 * inner + wide) // tile

    def multiply(at, start):
        k = pl.ds(pl.multiple_of(at * 2 * feat, 2 * feat), 2 * feat)

        @pl.loop(0, tiles)
        def _(n):
            cols = pl.ds(pl.multiple_of(n * tile, tile), tile)
            part = jnp.dot(tokbuf[at], w[k, cols], preferred_element_type=F32)
            if start:
                acc[:, cols] = part
            else:
                acc[:, cols] += part

        part = lax.dot_general(
            tokbuf[at, both, :], wdtp[:, k], (((1,), (1,)), ((), ())),
            preferred_element_type=F32,
        )
        if start:
            accdt[...] = part
        else:
            accdt[...] += part

    for one in loads:
        one.wait()
    arrive(mine.at[both, other_lanes], 0)
    halo_arrive(other)
    multiply(y, True)

    arrive(tokbuf.at[ym, first, lanes], 1)
    send(tokbuf.at[ym, first, lanes], tokbuf.at[ym, first, lanes], 5, to_up)
    arrive(tokbuf.at[yp, second, lanes], 3)
    send(tokbuf.at[yp, second, lanes], tokbuf.at[yp, second, lanes], 6, to_down)
    send(tokbuf.at[ym, first, lanes], tokbuf.at[ym, first, lanes], 7, to_other)
    send(tokbuf.at[yp, second, lanes], tokbuf.at[yp, second, lanes], 9, to_other)
    arrive(tokbuf.at[ym, second, lanes], 2)
    send(tokbuf.at[ym, second, lanes], tokbuf.at[ym, second, lanes], 8, to_other)
    arrive(tokbuf.at[yp, first, lanes], 4)
    send(tokbuf.at[yp, first, lanes], tokbuf.at[yp, first, lanes], 10, to_other)
    arrive(tokbuf.at[ym, first, other_lanes], 7)
    arrive(tokbuf.at[ym, second, other_lanes], 8)
    halo_arrive(ym * 2)
    halo_arrive(ym * 2 + 1)
    multiply(ym, False)
    arrive(tokbuf.at[yp, second, other_lanes], 9)
    arrive(tokbuf.at[yp, first, other_lanes], 10)
    halo_arrive(yp * 2)
    halo_arrive(yp * 2 + 1)
    multiply(yp, False)

    arrive(tokbuf.at[y2, first, lanes], 5)
    send(tokbuf.at[y2, first, lanes], tokbuf.at[y2, first, lanes], 11, to_other)
    arrive(tokbuf.at[y2, second, lanes], 6)
    send(tokbuf.at[y2, second, lanes], tokbuf.at[y2, second, lanes], 12, to_other)
    halo_arrive(y2 * 2)
    halo_arrive(y2 * 2 + 1)
    arrive(tokbuf.at[y2, first, other_lanes], 11)
    arrive(tokbuf.at[y2, second, other_lanes], 12)
    multiply(y2, False)

    for copy in sent + halo_sends:
        copy.wait_send()


def project(tokens, weight_x, weight_z, weight_bc, weight_dt, nseq, nhead, interpret=False):
    rows, feat = tokens.shape
    depth, inner = weight_x.shape
    wide = weight_bc.shape[1]
    total = 2 * inner + wide
    return pl.pallas_call(
        functools.partial(project_kernel, nseq, nhead),
        name="project",
        out_shape=(
            jax.ShapeDtypeStruct((rows + HALO, total), F32),
            jax.ShapeDtypeStruct((rows, 128), F32),
        ),
        in_specs=[hbm()] * 5,
        out_specs=(vmem(), vmem()),
        scratch_shapes=[
            pltpu.VMEM((nhead // 2, rows + HALO, 2 * feat), BF16),
            pltpu.VMEM((depth, total), BF16),
            pltpu.VMEM((128, depth), BF16),
            pltpu.SemaphoreType.DMA((5,)),
            pltpu.SemaphoreType.DMA((14,)),
            pltpu.SemaphoreType.DMA((14,)),
            pltpu.SemaphoreType.DMA((nhead,)),
            pltpu.SemaphoreType.DMA((nhead,)),
        ],
        compiler_params=pltpu.CompilerParams(
            collective_id=0, has_side_effects=True, vmem_limit_bytes=PROJECT_VMEM
        ),
    )(tokens, weight_x, weight_z, weight_bc, weight_dt)


def silu(x):
    half = 0.5 * x
    return half + half * jnp.tanh(half)


def read_prompts(len_ref, count):
    starts, ends = [], []
    at = jnp.int32(0)
    for r in range(count):
        starts.append(at)
        at = at + len_ref[r]
        ends.append(at - 1)
    return starts, ends


def ends_in_block(starts, ends, base, rows):
    count = len(starts)
    none = jnp.int32(-1)
    a_start, a_end = none, none
    b_start, b_end = none, none
    a_at = none
    for r in range(count - 1, -1, -1):
        here = (ends[r] >= base) & (ends[r] < base + rows)
        a_start = jnp.where(here, starts[r], a_start)
        a_end = jnp.where(here, ends[r], a_end)
        a_at = jnp.where(here, r, a_at)
    for r in range(count):
        here = (ends[r] >= base) & (ends[r] < base + rows) & (a_at != r)
        b_start = jnp.where(here, starts[r], b_start)
        b_end = jnp.where(here, ends[r], b_end)
    return a_start, a_end, b_start, b_end


def end_slots(starts, ends, rows):
    prompts = len(starts)
    slot, block = [], []
    for r in range(prompts):
        at = ends[r] // rows
        a = jnp.bool_(True) if r == 0 else (ends[r - 1] // rows) != at
        b = jnp.bool_(True) if r == prompts - 1 else (ends[r + 1] // rows) != at
        slot.append(jnp.where(a, 0, jnp.where(b, 1, 2)).astype(jnp.int32))
        block.append(at)
    return slot, block


def by_head(values, shape):
    which = lax.broadcasted_iota(jnp.int32, shape, 0)
    out = jnp.zeros(shape, F32)
    for h in range(shape[0]):
        out = jnp.where(which == h, values[h], out)
    return out


def block_kernel(
    xs, zs, nhead,
    len_ref, page_ref, step_bias, decay_log, skip_gain,
    u, dt_raw, wconv_x, bconv_x, wconv_bc, bconv_bc,
    gated, scale_out, page_out, v_out, more_out,
    xc, bcol, btf, ccol, btr, scores, spread, cols, stage, y_loc,
    s_send, d_send, ab_send, v_all, v_send, s_buf, d_buf, ab_buf, v_buf,
    h_all, h_send, h_buf, p_send, q_send, q_buf, where_ref,
    send_sem, recv_sem, qs_sem, qr_sem,
):
    nseq = xs * zs
    seq = lax.axis_index("seq")
    head = lax.axis_index("head")
    my_x, my_z = seq // zs, seq % zs
    rows, inner = xc.shape
    state = ccol.shape[1]
    heads = step_bias.shape[0]
    lbs = inner // 128
    per = nseq // lbs
    piece = state // per
    prompts = len_ref.shape[0]
    taps = wconv_x.shape[0]
    lb_me = seq // per
    base = seq * rows

    barrier = pltpu.get_barrier_semaphore()

    @pl.loop(1, nseq)
    def _(d):
        pl.semaphore_signal(
            barrier, inc=1, device_id={"seq": (seq + d) % nseq}, device_id_type=MESH
        )

    for k in range(1, nhead):
        pl.semaphore_signal(
            barrier, inc=1, device_id={"head": (head + k) % nhead}, device_id_type=MESH
        )

    starts, ends = read_prompts(len_ref, prompts)
    slot, block = end_slots(starts, ends, rows)
    more = jnp.int32(0)
    for kind in slot:
        more = jnp.maximum(more, kind - 1)
    more_out[0] = more

    def start_of(pos):
        found = jnp.zeros_like(pos)
        for r in range(prompts):
            found = jnp.where(starts[r] <= pos, starts[r], found)
        return found

    dtr = jnp.transpose(dt_raw[...])[0:heads, :]
    pre = dtr + by_head(step_bias, (heads, rows))
    dt = jnp.maximum(pre, 0.0) + jnp.log1p(jnp.exp(-jnp.abs(pre)))
    cum = -dt * jnp.exp(by_head(decay_log, (heads, rows)))
    lane = lax.broadcasted_iota(jnp.int32, (heads, rows), 1)
    shift = 1
    while shift < rows:
        cum = cum + jnp.where(lane >= shift, pltpu.roll(cum, shift, 1), 0.0)
        shift *= 2
    pos = base + lane
    start_row = start_of(pos)
    a_start, a_end, b_start, b_end = ends_in_block(starts, ends, base, rows)
    last_start = start_of(jnp.full((heads, rows), base + rows - 1, jnp.int32))

    def at_pos(where_pos):
        return jnp.sum(jnp.where(pos == where_pos, cum, 0.0), axis=1, keepdims=True)

    cum_last = at_pos(base + rows - 1)
    cum_a, cum_b = at_pos(a_end), at_pos(b_end)

    def weight_to(cum_end, keep):
        return jnp.where(keep, jnp.exp(jnp.minimum(cum_end - cum, 0.0)), 0.0) * dt

    w_end = weight_to(cum_last, pos >= last_start)
    w_a = weight_to(cum_a, (pos >= a_start) & (pos <= a_end))
    w_b = weight_to(cum_b, (pos >= b_start) & (pos <= b_end))
    inflow = jnp.where(start_row < base, jnp.exp(cum), 0.0)
    decay = jnp.where(last_start[:, 0:1] < base, jnp.exp(cum_last), 0.0)
    decay_a = jnp.where(
        (jnp.full((heads, 1), a_start) < base) & (jnp.full((heads, 1), a_end) >= 0),
        jnp.exp(cum_a), 0.0,
    )
    cum2 = cum * LOG2E
    age_row = (pos - start_row).astype(F32)
    packed = jnp.concatenate(
        [cum2, inflow, age_row] + [jnp.zeros((128 - 3 * heads, rows), F32)], axis=0,
    )
    cols[...] = jnp.transpose(packed)
    low_row = lax.broadcasted_iota(jnp.int32, (1, 128), 1) < 64

    for lb in range(lbs):
        h0, h1 = 2 * lb, 2 * lb + 1
        for k, value in enumerate((decay, decay_a)):
            d_send[lb, pl.ds(k, 1), :] = jnp.where(
                low_row,
                jnp.broadcast_to(value[h0 : h0 + 1, :], (1, 128)),
                jnp.broadcast_to(value[h1 : h1 + 1, :], (1, 128)),
            )

    step = 64

    @pl.loop(0, rows // step)
    def _(t):
        r0 = pl.multiple_of(t * step, step)
        age = jnp.broadcast_to(cols[pl.ds(r0, step), 2 * heads : 2 * heads + 1], (step, 128))
        near = [age >= d for d in range(taps)]
        for j in range(lbs + 2):
            lanes = pl.ds(j * 128, 128)
            win = u[pl.ds(r0, step + HALO), pl.ds((j if j < lbs else j + lbs) * 128, 128)]
            if j < lbs:
                wl, wt, wb = lanes, wconv_x, bconv_x
            else:
                wl, wt, wb = pl.ds((j - lbs) * 128, 128), wconv_bc, bconv_bc
            total = jnp.broadcast_to(wb[:, wl], (step, 128))
            for k in range(taps):
                d = taps - 1 - k
                shifted = win if d == 0 else pltpu.roll(win, d, 0)
                term = shifted[HALO:, :] * wt[pl.ds(k, 1), wl]
                total = total + (term if d == 0 else jnp.where(near[d], term, 0.0))
            out = silu(total)
            if j < lbs:
                xc[pl.ds(r0, step), lanes] = out.astype(BF16)
            elif j == lbs:
                bcol[pl.ds(r0, step), :] = out.astype(BF16).astype(F32)
            else:
                ccol[pl.ds(r0, step), :] = out.astype(BF16)

    btf[...] = jnp.transpose(bcol[...])
    btr[...] = btf[...].astype(BF16)

    low_state = lax.broadcasted_iota(jnp.int32, (state, 128), 1) < 64

    def state_of(weight, lb):
        pair = [
            (btf[...] * weight[2 * lb + k : 2 * lb + k + 1, :]).astype(BF16) for k in range(2)
        ]
        both = jnp.dot(
            jnp.concatenate(pair, axis=0), xc[:, pl.ds(lb * 128, 128)],
            preferred_element_type=F32,
        )
        value = jnp.where(low_state, both[0:state, :], both[state:, :])
        return value.astype(BF16).reshape(per, piece, 128)

    for lb in range(lbs):
        s_send[pl.ds(lb * per, per)] = state_of(w_end, lb)
    pl.semaphore_wait(barrier, nseq - 1 + nhead - 1)

    S, D, AB, V, H, PG = range(6)

    def offset(n):
        t, s = n // xs, n % xs
        dz = (zs // 2 + (1 - 2 * (t % 2)) * ((t + 1) // 2)) % zs
        dx = (xs // 2 + (1 - 2 * (s % 2)) * ((s + 1) // 2)) % xs
        return dx, dz

    def copy(kind, src, dst, n, to):
        return pltpu.make_async_remote_copy(
            src_ref=src, dst_ref=dst, send_sem=send_sem.at[kind, n], recv_sem=recv_sem.at[kind, n],
            device_id={"seq": to}, device_id_type=MESH,
        )

    x_order = [(xs // 2 + (1 - 2 * (k % 2)) * ((k + 1) // 2)) % xs for k in range(xs)]
    x_part = [lax.rem(my_x + dx, xs) * zs for dx in x_order]

    def out_copy(kind, n, to):
        if kind == S:
            return copy(S, s_send.at[to], s_buf.at[seq], n, to)
        if kind == D:
            return copy(D, d_send.at[to // per], d_buf.at[seq], n, to)
        if kind == AB:
            return copy(AB, ab_send.at[to], ab_buf.at[seq], n, to)
        if kind == V:
            return copy(V, v_send.at[to], v_buf.at[seq], n, to)
        if kind == H:
            return copy(H, h_send.at[to], h_buf.at[seq], n, to)
        return copy(PG, p_send.at[to], page_out.at[seq], n, to)

    def in_copy(kind, n):
        dx, dz = offset(n)
        frm = ((my_x + xs - dx) % xs) * zs + (my_z + zs - dz) % zs
        buf = (s_buf, d_buf, ab_buf, v_buf, h_buf, page_out)[kind]
        return copy(kind, buf.at[frm], buf.at[frm], n, frm)

    def start_all(*kinds):
        @pl.loop(0, zs - 1)
        def _(t):
            dz = zs // 2 + (1 - 2 * lax.rem(t, 2)) * ((t + 1) // 2)
            z_part = lax.rem(my_z + dz, zs)
            for k in range(xs):
                for kind in kinds:
                    out_copy(kind, t * xs + k, x_part[k] + z_part).start()

        for k in range(xs - 1):
            for kind in kinds:
                out_copy(kind, (zs - 1) * xs + k, x_part[k] + my_z).start()

    def arrive_all(*kinds):
        @pl.loop(0, nseq - 1)
        def _(n):
            for kind in kinds:
                in_copy(kind, n).wait_recv()

    start_all(S, D)
    for lb in range(lbs):
        for kind, weight in enumerate((w_a, w_b)):
            ab_send[pl.ds(lb * per, per), kind] = state_of(weight, lb)
    start_all(AB)
    s_buf[seq] = s_send[seq]
    d_buf[seq] = d_send[lb_me]
    ab_buf[seq] = ab_send[seq]

    tile = 128
    blocks = rows // tile
    for i in range(blocks):
        ri = pl.ds(i * tile, tile)
        reach = (i + 1) * tile
        sc = jnp.dot(ccol[ri, :], btr[:, 0:reach], preferred_element_type=F32)
        gap_i = i * tile + lax.broadcasted_iota(jnp.int32, (tile, reach), 0)
        gap_j = lax.broadcasted_iota(jnp.int32, (tile, reach), 1)
        back = (gap_i - gap_j).astype(F32)
        age = cols[ri, 2 * heads : 2 * heads + 1]
        scores[ri, 0:reach] = jnp.where((back >= 0.0) & (back <= age), sc, 0.0)
    low_t = lax.broadcasted_iota(jnp.int32, (tile, 128), 1) < 64
    for lb in range(lbs):
        lanes = pl.ds(lb * 128, 128)
        gain = jnp.where(low_row, skip_gain[2 * lb], skip_gain[2 * lb + 1])
        for i in range(blocks):
            ri = pl.ds(i * tile, tile)
            reach = (i + 1) * tile
            parts = []
            for hh in range(2):
                h = 2 * lb + hh
                gap = jnp.minimum(cols[ri, h : h + 1] - cum2[h : h + 1, 0:reach], 0.0)
                wgt = (scores[ri, 0:reach] * jnp.exp2(gap) * dt[h : h + 1, 0:reach]).astype(BF16)
                parts.append(jnp.dot(wgt, xc[0:reach, lanes], preferred_element_type=F32))
            y_loc[ri, lanes] = (
                jnp.where(low_t, parts[0], parts[1]) + gain * xc[ri, lanes].astype(F32)
            )

    @pl.loop(0, nseq)
    def _(q):
        kind = jnp.int32(2)
        at = jnp.int32(0)
        who = jnp.int32(prompts)
        for r in range(prompts):
            hit = page_ref[r] == q
            kind = jnp.where(hit, slot[r], kind)
            at = jnp.where(hit, block[r], at)
            who = jnp.where(hit & (block[r] == seq), r, who)
        where_ref[0, q] = kind
        where_ref[1, q] = jnp.clip(at, 0, nseq - 1)
        where_ref[2, q] = who

    v_rows = v_all.shape[1]
    v_all[prompts] = jnp.zeros((v_rows, 128), BF16)
    for r in range(prompts):
        local = jnp.clip(ends[r] - base, 0, rows - 1) + HALO
        for k in range(taps - 1):
            back = taps - 2 - k
            line = u[pl.ds(local - back, 1), :]
            keep = jnp.full((1, 128), ends[r] - back, jnp.int32) >= starts[r]
            for j in range(lbs):
                stage[k * lbs + j : k * lbs + j + 1, :] = jnp.where(
                    keep, line[:, j * 128 : (j + 1) * 128], 0.0
                )
            for j in range(2):
                at = (taps - 1) * lbs + 2 * k + j
                stage[at : at + 1, :] = jnp.where(
                    keep, line[:, (2 * lbs + j) * 128 : (2 * lbs + j + 1) * 128], 0.0
                )
        v_all[r] = stage[...].astype(BF16)

    @pl.loop(0, nseq)
    def _(q):
        v_send[q] = v_all[where_ref[2, q]]

    arrive_all(S, D)

    def advance(i, carried):
        h_all[i] = carried
        h_send[i] = carried.astype(BF16)
        return d_buf[i, 0:1, :] * carried + s_buf[i].astype(F32)

    lax.fori_loop(0, nseq, advance, jnp.zeros((piece, 128), F32))
    start_all(H)
    h_buf[seq] = h_send[seq]
    start_all(V)
    v_buf[seq] = v_send[seq]

    arrive_all(AB)

    @pl.loop(0, nseq)
    def _(q):
        kind = where_ref[0, q]
        at = where_ref[1, q]
        value = ab_buf[at, jnp.where(kind == 1, 1, 0)].astype(F32)
        first = value + d_buf[at, 1:2, :] * h_all[at]
        kinds = jnp.full((piece, 128), kind, jnp.int32)
        p_send[q] = jnp.where(kinds == 0, first, jnp.where(kinds == 1, value, 0.0)).astype(BF16)

    start_all(PG)
    page_out[seq] = p_send[seq]

    tile = 64
    low = lax.broadcasted_iota(jnp.int32, (tile, 128), 1) < 64
    lanes128 = lax.broadcasted_iota(jnp.int32, (tile, 128), 1)
    subl = lax.broadcasted_iota(jnp.int32, (tile, 128), 0)
    for g in range(rows // tile):
        ri = pl.ds(g * tile, tile)
        for lb in range(lbs):
            lanes = pl.ds(lb * 128, 128)
            at = heads + 2 * lb
            scores[ri, lanes] = silu(u[pl.ds(HALO + g * tile, tile), pl.ds(inner + lb * 128, 128)])
            spread[ri, lanes] = jnp.where(low, cols[ri, at : at + 1], cols[ri, at + 1 : at + 2])

    arrive_all(H)
    for g in range(rows // 128):
        line = jnp.zeros((1, 128), F32)
        for s in range(128 // tile):
            ri = pl.ds(g * 128 + s * tile, tile)
            total = jnp.zeros((tile, 128), F32)
            for lb in range(lbs):
                lanes = pl.ds(lb * 128, 128)
                hmat = h_buf[pl.ds(lb * per, per)].reshape(state, 128)
                ac = jnp.dot(ccol[ri, :], hmat, preferred_element_type=F32)
                yv = (y_loc[ri, lanes] + ac * spread[ri, lanes]).astype(BF16).astype(F32)
                gv = yv * scores[ri, lanes]
                gated[ri, lanes] = gv
                total = total + gv * gv
            col = jnp.sum(total, axis=1, keepdims=True)
            line = line + jnp.sum(
                jnp.where(lanes128 == subl + s * tile, col, 0.0), axis=0, keepdims=True
            )
        q_send[g : g + 1, :] = line

    q_copies = []
    for k in range(1, nhead):
        one = pltpu.make_async_remote_copy(
            src_ref=q_send, dst_ref=q_buf.at[head], send_sem=qs_sem.at[k], recv_sem=qr_sem.at[k],
            device_id={"head": (head + k) % nhead}, device_id_type=MESH,
        )
        one.start()
        q_copies.append(one)
    q_buf[head] = q_send[...]

    source = jnp.int32(0)
    found = jnp.int32(0)
    for r in range(prompts):
        hit = page_ref[r] == seq
        source = jnp.where(hit, block[r], source)
        found = jnp.where(hit, 1, found)
    source = jnp.clip(source, 0, nseq - 1)
    arrive_all(V)
    v_out[...] = jnp.where(
        jnp.full(v_out.shape, found, jnp.int32) == 1, v_buf[source].astype(F32), 0.0
    )

    arrive_all(PG)

    @pl.loop(0, nseq - 1)
    def _(n):
        for kind in (S, D, AB, V, H, PG):
            in_copy(kind, n).wait_send()

    for k in range(1, nhead):
        frm = (head + nhead - k) % nhead
        pltpu.make_async_remote_copy(
            src_ref=q_send, dst_ref=q_buf.at[frm], send_sem=qs_sem.at[k], recv_sem=qr_sem.at[k],
            device_id={"head": frm}, device_id_type=MESH,
        ).wait_recv()
    squares = q_buf[0]
    for k in range(1, nhead):
        squares = squares + q_buf[k]
    scale_out[...] = lax.rsqrt(squares / (inner * nhead) + EPS)

    for one in q_copies:
        one.wait_send()


def run_block(u, dt_raw, wconv_x, bconv_x, wconv_bc, bconv_bc, step_bias, decay_log, skip,
              lengths, pages, nseq, nhead):
    rows, inner = dt_raw.shape[0], wconv_x.shape[1]
    state = wconv_bc.shape[1] // 2
    lbs = inner // 128
    piece = state * lbs // nseq
    prompts = lengths.shape[0]
    xs = 4
    tiles = (nseq, piece, 128)
    v_rows = 24
    return pl.pallas_call(
        functools.partial(block_kernel, xs, nseq // xs, nhead),
        name="block",
        out_shape=(
            jax.ShapeDtypeStruct((rows, inner), F32),
            jax.ShapeDtypeStruct((rows // 128, 128), F32),
            jax.ShapeDtypeStruct(tiles, BF16),
            jax.ShapeDtypeStruct((v_rows, 128), F32),
            jax.ShapeDtypeStruct((1,), jnp.int32),
        ),
        in_specs=[smem()] * 5 + [vmem()] * 6,
        out_specs=(vmem(),) * 4 + (smem(),),
        scratch_shapes=[
            pltpu.VMEM((rows, inner), BF16),
            pltpu.VMEM((rows, state), F32),
            pltpu.VMEM((state, rows), F32),
            pltpu.VMEM((rows, state), BF16),
            pltpu.VMEM((state, rows), BF16),
            pltpu.VMEM((rows, max(rows, inner)), F32),
            pltpu.VMEM((rows, inner), F32),
            pltpu.VMEM((rows, 128), F32),
            pltpu.VMEM((v_rows, 128), F32),
            pltpu.VMEM((rows, inner), F32),
            pltpu.VMEM(tiles, BF16),
            pltpu.VMEM((lbs, 2, 128), F32),
            pltpu.VMEM((nseq, 2, piece, 128), BF16),
            pltpu.VMEM((prompts + 1, v_rows, 128), BF16),
            pltpu.VMEM((nseq, v_rows, 128), BF16),
            pltpu.VMEM(tiles, BF16),
            pltpu.VMEM((nseq, 2, 128), F32),
            pltpu.VMEM((nseq, 2, piece, 128), BF16),
            pltpu.VMEM((nseq, v_rows, 128), BF16),
            pltpu.VMEM(tiles, F32),
            pltpu.VMEM(tiles, BF16),
            pltpu.VMEM(tiles, BF16),
            pltpu.VMEM(tiles, BF16),
            pltpu.VMEM((rows // 128, 128), F32),
            pltpu.VMEM((nhead, rows // 128, 128), F32),
            pltpu.SMEM((3, nseq), jnp.int32),
            pltpu.SemaphoreType.DMA((6, nseq)),
            pltpu.SemaphoreType.DMA((6, nseq)),
            pltpu.SemaphoreType.DMA((nhead,)),
            pltpu.SemaphoreType.DMA((nhead,)),
        ],
        compiler_params=pltpu.CompilerParams(
            collective_id=1, has_side_effects=True, vmem_limit_bytes=40 << 20
        ),
    )(lengths, pages, step_bias, decay_log, skip, u, dt_raw, wconv_x, bconv_x, wconv_bc,
      bconv_bc)


def write_kernel(gated, scale_rows, pages, v, gain, n_out, page_out, cx_out, cb_out):
    rows, inner = gated.shape
    lbs = inner // 128
    per = pages.shape[0] // lbs
    state = per * pages.shape[1]
    tile = 64
    lanes128 = lax.broadcasted_iota(jnp.int32, (tile, 128), 1)
    subl = lax.broadcasted_iota(jnp.int32, (tile, 128), 0)
    for g in range(rows // 128):
        for s in range(128 // tile):
            ri = pl.ds(g * 128 + s * tile, tile)
            diag = jnp.where(lanes128 == subl + s * tile, scale_rows[g : g + 1, :], 0.0)
            scale = jnp.sum(diag, axis=1, keepdims=True)
            n_out[ri, :] = (gated[ri, :] * scale * gain[...]).astype(BF16)
    for lb in range(lbs):
        mat = pages[pl.ds(lb * per, per)].reshape(state, 128).astype(F32)
        page_out[pl.ds(lb * 128, 128), :] = jnp.transpose(mat)
    kept = cx_out.shape[0]
    for k in range(kept):
        for j in range(lbs):
            cx_out[k, :, j * 128 : (j + 1) * 128] = v[k * lbs + j : k * lbs + j + 1, :]
        for j in range(2):
            at = kept * lbs + 2 * k + j
            cb_out[k, :, j * 128 : (j + 1) * 128] = v[at : at + 1, :]


def write(gated, scale_rows, pages, v, gain, state, kept):
    rows, inner = gated.shape
    return pl.pallas_call(
        write_kernel,
        name="write",
        out_shape=(
            jax.ShapeDtypeStruct((rows, inner), BF16),
            jax.ShapeDtypeStruct((inner, state), F32),
            jax.ShapeDtypeStruct((kept, 1, inner), F32),
            jax.ShapeDtypeStruct((kept, 1, 2 * state), F32),
        ),
        in_specs=[vmem()] * 5,
        out_specs=(vmem(),) * 4,
        compiler_params=pltpu.CompilerParams(vmem_limit_bytes=8 << 20),
    )(gated, scale_rows, pages, v, gain)


def crowded_pages(
    u, dt_raw, wconv_x, bconv_x, wconv_bc, bconv_bc, step_bias, decay_log, lengths, pages
):
    rows = dt_raw.shape[0]
    heads = step_bias.shape[0]
    inner = wconv_x.shape[1]
    state = wconv_bc.shape[1] // 2
    taps = wconv_x.shape[0]
    prompts = lengths.shape[0]
    nseq = lax.axis_size("seq")
    base = lax.axis_index("seq") * rows
    ends = jnp.cumsum(lengths) - 1
    starts = ends - lengths + 1
    pos = base + jnp.arange(rows, dtype=jnp.int32)
    age = pos - jnp.max(jnp.where(starts[None] <= pos[:, None], starts[None], 0), axis=1)
    weight = jnp.concatenate([wconv_x, wconv_bc], axis=1)[:, : inner + state]
    total = jnp.concatenate([bconv_x, bconv_bc])[None, : inner + state]
    joined = jnp.concatenate([u[:, :inner], u[:, 2 * inner : 2 * inner + state]], axis=1)
    for k in range(taps):
        d = taps - 1 - k
        term = joined[HALO - d : HALO - d + rows] * weight[k][None]
        total = total + jnp.where((age >= d)[:, None], term, 0.0)
    conv = jax.nn.silu(total).astype(BF16)
    x, b = conv[:, :inner], conv[:, inner:]
    dt = jax.nn.softplus(dt_raw[:, :heads] + step_bias[None])
    cum = jnp.cumsum(-dt * jnp.exp(decay_log)[None], axis=0)
    block = ends // rows
    before = jnp.concatenate([jnp.full((1,), -1, block.dtype), block[:-1]])
    after = jnp.concatenate([block[1:], jnp.full((1,), -1, block.dtype)])
    mine = (before == block) & (after == block) & (block == lax.axis_index("seq"))
    at_end = cum[jnp.clip(ends - base, 0, rows - 1)]
    keep = mine[:, None] & (pos[None] >= starts[:, None]) & (pos[None] <= ends[:, None])
    scale = jnp.where(
        keep[:, :, None], jnp.exp(jnp.minimum(at_end[:, None] - cum[None], 0.0)) * dt[None], 0.0
    )
    x_heads = x.reshape(rows, heads, -1).astype(F32)
    weighted = (scale[:, :, :, None] * x_heads[None]).astype(BF16).reshape(prompts, rows, inner)
    finals = jnp.einsum("rjc,jn->rcn", weighted, b, preferred_element_type=F32)
    hits = (pages[None, :] == jnp.arange(nseq, dtype=jnp.int32)[:, None]).astype(BF16)
    pool = jnp.einsum("qr,rcn->qcn", hits, finals.astype(BF16), preferred_element_type=F32)
    moved = lax.all_to_all(pool.astype(BF16), "seq", 0, 0, tiled=True)
    return jnp.sum(moved.astype(F32), axis=0)


def body(
    tokens, weight_x, weight_z, weight_bc, weight_dt, conv_x_weight, conv_x_bias,
    conv_bc_weight, conv_bc_bias, step_bias, decay_log, skip_gain, norm_gain, lengths, page_table,
):
    nseq, nhead = lax.axis_size("seq"), lax.axis_size("head")
    heads = weight_dt.shape[0]
    inner = weight_x.shape[1]
    width = inner // heads
    kept = conv_x_weight.shape[0] - 1
    u, dt_raw = project(tokens, weight_x, weight_z, weight_bc, weight_dt, nseq, nhead)
    gated, scale, pages, v, more = run_block(
        u, dt_raw, conv_x_weight, conv_x_bias[None, :], conv_bc_weight,
        conv_bc_bias[None, :], step_bias, decay_log, skip_gain, lengths, page_table, nseq, nhead,
    )
    normed, page, conv_x, conv_bc = write(
        gated, scale, pages, v, norm_gain[None, :], conv_bc_weight.shape[1] // 2, kept
    )
    page = lax.cond(
        more[0] > 0,
        lambda page, *rest: page + crowded_pages(*rest),
        lambda page, *rest: page,
        page, u, dt_raw, conv_x_weight, conv_x_bias, conv_bc_weight, conv_bc_bias, step_bias,
        decay_log, lengths, page_table,
    )
    return (
        normed, page.reshape(1, heads, width, -1), jnp.swapaxes(conv_x, 0, 1), jnp.swapaxes(conv_bc, 0, 1),
    )


def solution(mesh):
    in_specs = (
        P("seq", "head"), P(None, "head"), P(None, "head"), P(), P("head", None),
        P(None, "head"), P("head"), P(), P(), P("head"), P("head"), P("head"), P("head"),
        P(), P(),
    )
    out_specs = (
        P("seq", "head"), P("seq", "head", None, None), P("seq", None, "head"),
        P("seq", None, None),
    )
    return jax.shard_map(body, mesh=mesh, in_specs=in_specs, out_specs=out_specs, check_vma=False)
```

```python
import functools

import jax
import jax.numpy as jnp
from jax import lax
from jax.experimental import pallas as pl
from jax.experimental.pallas import tpu as pltpu
from jax.sharding import PartitionSpec as P

MESH = pl.DeviceIdType.MESH
F32 = jnp.float32
BF16 = jnp.bfloat16
EPS = 1e-05
HALO = 16
PROJECT_VMEM = (60 << 20) + (1 << 19)
LOG2E = 1.4426950408889634


def vmem():
    return pl.BlockSpec(memory_space=pltpu.VMEM)


def hbm():
    return pl.BlockSpec(memory_space=pltpu.HBM)


def smem():
    return pl.BlockSpec(memory_space=pltpu.SMEM)


def project_kernel(
    nseq, nhead,
    tok, wx, wz, wbc, wdt,
    acc, accdt,
    tokbuf, w, wdtp,
    lsem, ssem, rsem, hs_sem, hr_sem,
):
    ny = nhead // 2
    seq = lax.axis_index("seq")
    head = lax.axis_index("head")
    y = head // 2
    core = head % 2
    rows, feat = tok.shape
    half = rows // 2
    inner = wx.shape[1]
    wide = wbc.shape[1]
    heads = wdt.shape[0]
    yp, ym = (y + 1) % ny, (y + ny - 1) % ny
    y2 = (y + 2) % ny
    up, down = yp * 2 + core, ym * 2 + core
    other = y * 2 + (1 - core)
    nxt, prv = (seq + 1) % nseq, (seq + nseq - 1) % nseq
    lanes = pl.ds(pl.multiple_of(core * feat, feat), feat)
    other_lanes = pl.ds(pl.multiple_of((1 - core) * feat, feat), feat)
    first, second = pl.ds(HALO, half), pl.ds(HALO + half, half)
    both = pl.ds(HALO, rows)
    edge = pl.ds(0, HALO)

    loads = [
        pltpu.make_async_copy(tok, tokbuf.at[y, both, lanes], lsem.at[0]),
        pltpu.make_async_copy(wx, w.at[:, pl.ds(0, inner)], lsem.at[1]),
        pltpu.make_async_copy(wbc, w.at[:, pl.ds(2 * inner, wide)], lsem.at[2]),
        pltpu.make_async_copy(wz, w.at[:, pl.ds(inner, inner)], lsem.at[3]),
        pltpu.make_async_copy(wdt, wdtp.at[pl.ds(0, heads)], lsem.at[4]),
    ]

    barrier = pltpu.get_barrier_semaphore()
    for k in range(1, nhead):
        pl.semaphore_signal(
            barrier, inc=1, device_id={"head": (head + k) % nhead}, device_id_type=MESH
        )
    pl.semaphore_signal(barrier, inc=1, device_id={"seq": nxt}, device_id_type=MESH)
    pl.semaphore_signal(barrier, inc=1, device_id={"seq": prv}, device_id_type=MESH)
    wdtp[pl.ds(heads, 128 - heads), :] = jnp.zeros((128 - heads, wdtp.shape[1]), BF16)
    for one in loads:
        one.start()
    pl.semaphore_wait(barrier, nhead + 1)

    sent = []

    def send(src, dst, number, to):
        copy = pltpu.make_async_remote_copy(
            src_ref=src, dst_ref=dst, send_sem=ssem.at[number], recv_sem=rsem.at[number],
            device_id=to, device_id_type=MESH,
        )
        copy.start()
        sent.append(copy)

    def arrive(region, number):
        pltpu.make_async_remote_copy(
            src_ref=region, dst_ref=region, send_sem=ssem.at[number], recv_sem=rsem.at[number],
            device_id={"head": other}, device_id_type=MESH,
        ).wait_recv()

    to_up, to_down, to_other = {"head": up}, {"head": down}, {"head": other}
    mine = tokbuf.at[y]
    send(tok.at[pl.ds(rows - HALO, HALO)], mine.at[edge, lanes], 13, {"seq": nxt})
    send(tok.at[pl.ds(0, half)], mine.at[first, lanes], 1, to_up)
    send(tok.at[pl.ds(half, half)], mine.at[second, lanes], 3, to_down)
    send(tok, mine.at[both, lanes], 0, to_other)
    send(tok.at[pl.ds(half, half)], mine.at[second, lanes], 2, to_up)
    send(tok.at[pl.ds(0, half)], mine.at[first, lanes], 4, to_down)

    def halo_piece(owner):
        return tokbuf.at[
            owner // 2, edge, pl.ds(pl.multiple_of((owner % 2) * feat, feat), feat)
        ]

    arrive(halo_piece(head), 13)
    halo_sends = []
    for k in range(1, nhead):
        copy = pltpu.make_async_remote_copy(
            src_ref=halo_piece(head), dst_ref=halo_piece(head),
            send_sem=hs_sem.at[k], recv_sem=hr_sem.at[head],
            device_id={"head": (head + k) % nhead}, device_id_type=MESH,
        )
        copy.start()
        halo_sends.append(copy)

    def halo_arrive(owner):
        pltpu.make_async_remote_copy(
            src_ref=halo_piece(owner), dst_ref=halo_piece(owner),
            send_sem=hs_sem.at[0], recv_sem=hr_sem.at[owner],
            device_id={"head": other}, device_id_type=MESH,
        ).wait_recv()

    tile = 256
    tiles = (2 * inner + wide) // tile

    def multiply(at, start):
        k = pl.ds(pl.multiple_of(at * 2 * feat, 2 * feat), 2 * feat)

        @pl.loop(0, tiles)
        def _(n):
            cols = pl.ds(pl.multiple_of(n * tile, tile), tile)
            part = jnp.dot(tokbuf[at], w[k, cols], preferred_element_type=F32)
            if start:
                acc[:, cols] = part
            else:
                acc[:, cols] += part

        part = lax.dot_general(
            tokbuf[at, both, :], wdtp[:, k], (((1,), (1,)), ((), ())),
            preferred_element_type=F32,
        )
        if start:
            accdt[...] = part
        else:
            accdt[...] += part

    for one in loads:
        one.wait()
    arrive(mine.at[both, other_lanes], 0)
    halo_arrive(other)
    arrive(tokbuf.at[ym, first, lanes], 1)
    send(tokbuf.at[ym, first, lanes], tokbuf.at[ym, first, lanes], 5, to_up)
    arrive(tokbuf.at[yp, second, lanes], 3)
    send(tokbuf.at[yp, second, lanes], tokbuf.at[yp, second, lanes], 6, to_down)
    multiply(y, True)

    send(tokbuf.at[ym, first, lanes], tokbuf.at[ym, first, lanes], 7, to_other)
    send(tokbuf.at[yp, second, lanes], tokbuf.at[yp, second, lanes], 9, to_other)
    arrive(tokbuf.at[ym, second, lanes], 2)
    send(tokbuf.at[ym, second, lanes], tokbuf.at[ym, second, lanes], 8, to_other)
    arrive(tokbuf.at[yp, first, lanes], 4)
    send(tokbuf.at[yp, first, lanes], tokbuf.at[yp, first, lanes], 10, to_other)
    arrive(tokbuf.at[ym, first, other_lanes], 7)
    arrive(tokbuf.at[ym, second, other_lanes], 8)
    halo_arrive(ym * 2)
    halo_arrive(ym * 2 + 1)
    multiply(ym, False)
    arrive(tokbuf.at[yp, second, other_lanes], 9)
    arrive(tokbuf.at[yp, first, other_lanes], 10)
    halo_arrive(yp * 2)
    halo_arrive(yp * 2 + 1)
    multiply(yp, False)

    arrive(tokbuf.at[y2, first, lanes], 5)
    send(tokbuf.at[y2, first, lanes], tokbuf.at[y2, first, lanes], 11, to_other)
    arrive(tokbuf.at[y2, second, lanes], 6)
    send(tokbuf.at[y2, second, lanes], tokbuf.at[y2, second, lanes], 12, to_other)
    halo_arrive(y2 * 2)
    halo_arrive(y2 * 2 + 1)
    arrive(tokbuf.at[y2, first, other_lanes], 11)
    arrive(tokbuf.at[y2, second, other_lanes], 12)
    multiply(y2, False)

    for copy in sent + halo_sends:
        copy.wait_send()


def project(tokens, weight_x, weight_z, weight_bc, weight_dt, nseq, nhead, interpret=False):
    rows, feat = tokens.shape
    depth, inner = weight_x.shape
    wide = weight_bc.shape[1]
    total = 2 * inner + wide
    return pl.pallas_call(
        functools.partial(project_kernel, nseq, nhead),
        name="project",
        out_shape=(
            jax.ShapeDtypeStruct((rows + HALO, total), F32),
            jax.ShapeDtypeStruct((rows, 128), F32),
        ),
        in_specs=[hbm()] * 5,
        out_specs=(vmem(), vmem()),
        scratch_shapes=[
            pltpu.VMEM((nhead // 2, rows + HALO, 2 * feat), BF16),
            pltpu.VMEM((depth, total), BF16),
            pltpu.VMEM((128, depth), BF16),
            pltpu.SemaphoreType.DMA((5,)),
            pltpu.SemaphoreType.DMA((14,)),
            pltpu.SemaphoreType.DMA((14,)),
            pltpu.SemaphoreType.DMA((nhead,)),
            pltpu.SemaphoreType.DMA((nhead,)),
        ],
        compiler_params=pltpu.CompilerParams(
            collective_id=0, has_side_effects=True, vmem_limit_bytes=PROJECT_VMEM
        ),
    )(tokens, weight_x, weight_z, weight_bc, weight_dt)


def silu(x):
    half = 0.5 * x
    return half + half * jnp.tanh(half)


def read_prompts(len_ref, count):
    starts, ends = [], []
    at = jnp.int32(0)
    for r in range(count):
        starts.append(at)
        at = at + len_ref[r]
        ends.append(at - 1)
    return starts, ends


def ends_in_block(starts, ends, base, rows):
    count = len(starts)
    none = jnp.int32(-1)
    a_start, a_end = none, none
    b_start, b_end = none, none
    a_at = none
    for r in range(count - 1, -1, -1):
        here = (ends[r] >= base) & (ends[r] < base + rows)
        a_start = jnp.where(here, starts[r], a_start)
        a_end = jnp.where(here, ends[r], a_end)
        a_at = jnp.where(here, r, a_at)
    for r in range(count):
        here = (ends[r] >= base) & (ends[r] < base + rows) & (a_at != r)
        b_start = jnp.where(here, starts[r], b_start)
        b_end = jnp.where(here, ends[r], b_end)
    return a_start, a_end, b_start, b_end


def end_slots(starts, ends, rows):
    prompts = len(starts)
    slot, block = [], []
    for r in range(prompts):
        at = ends[r] // rows
        a = jnp.bool_(True) if r == 0 else (ends[r - 1] // rows) != at
        b = jnp.bool_(True) if r == prompts - 1 else (ends[r + 1] // rows) != at
        slot.append(jnp.where(a, 0, jnp.where(b, 1, 2)).astype(jnp.int32))
        block.append(at)
    return slot, block


def by_head(values, shape):
    which = lax.broadcasted_iota(jnp.int32, shape, 0)
    out = jnp.zeros(shape, F32)
    for h in range(shape[0]):
        out = jnp.where(which == h, values[h], out)
    return out


def block_kernel(
    xs, zs, nhead,
    len_ref, page_ref, step_bias, decay_log, skip_gain,
    u, dt_raw, wconv_x, bconv_x, wconv_bc, bconv_bc,
    gated, scale_out, page_out, v_out, more_out,
    xc, bcol, btf, ccol, btr, scores, spread, cols, stage, y_loc,
    s_send, d_send, ab_send, v_all, v_send, s_buf, d_buf, ab_buf, v_buf,
    h_all, h_send, h_buf, p_send, q_send, q_buf, where_ref,
    send_sem, recv_sem, qs_sem, qr_sem,
):
    nseq = xs * zs
    seq = lax.axis_index("seq")
    head = lax.axis_index("head")
    my_x, my_z = seq // zs, seq % zs
    rows, inner = xc.shape
    state = ccol.shape[1]
    heads = step_bias.shape[0]
    lbs = inner // 128
    per = nseq // lbs
    piece = state // per
    prompts = len_ref.shape[0]
    taps = wconv_x.shape[0]
    lb_me = seq // per
    base = seq * rows

    barrier = pltpu.get_barrier_semaphore()

    @pl.loop(1, nseq)
    def _(d):
        pl.semaphore_signal(
            barrier, inc=1, device_id={"seq": (seq + d) % nseq}, device_id_type=MESH
        )

    for k in range(1, nhead):
        pl.semaphore_signal(
            barrier, inc=1, device_id={"head": (head + k) % nhead}, device_id_type=MESH
        )

    starts, ends = read_prompts(len_ref, prompts)
    slot, block = end_slots(starts, ends, rows)
    more = jnp.int32(0)
    for kind in slot:
        more = jnp.maximum(more, kind - 1)
    more_out[0] = more

    def start_of(pos):
        found = jnp.zeros_like(pos)
        for r in range(prompts):
            found = jnp.where(starts[r] <= pos, starts[r], found)
        return found

    dtr = jnp.transpose(dt_raw[...])[0:heads, :]
    pre = dtr + by_head(step_bias, (heads, rows))
    dt = jnp.maximum(pre, 0.0) + jnp.log1p(jnp.exp(-jnp.abs(pre)))
    cum = -dt * jnp.exp(by_head(decay_log, (heads, rows)))
    lane = lax.broadcasted_iota(jnp.int32, (heads, rows), 1)
    shift = 1
    while shift < rows:
        cum = cum + jnp.where(lane >= shift, pltpu.roll(cum, shift, 1), 0.0)
        shift *= 2
    pos = base + lane
    start_row = start_of(pos)
    a_start, a_end, b_start, b_end = ends_in_block(starts, ends, base, rows)
    last_start = start_of(jnp.full((heads, rows), base + rows - 1, jnp.int32))

    def at_pos(where_pos):
        return jnp.sum(jnp.where(pos == where_pos, cum, 0.0), axis=1, keepdims=True)

    cum_last = at_pos(base + rows - 1)
    cum_a, cum_b = at_pos(a_end), at_pos(b_end)

    def weight_to(cum_end, keep):
        return jnp.where(keep, jnp.exp(jnp.minimum(cum_end - cum, 0.0)), 0.0) * dt

    w_end = weight_to(cum_last, pos >= last_start)
    w_a = weight_to(cum_a, (pos >= a_start) & (pos <= a_end))
    w_b = weight_to(cum_b, (pos >= b_start) & (pos <= b_end))
    inflow = jnp.where(start_row < base, jnp.exp(cum), 0.0)
    decay = jnp.where(last_start[:, 0:1] < base, jnp.exp(cum_last), 0.0)
    decay_a = jnp.where(
        (jnp.full((heads, 1), a_start) < base) & (jnp.full((heads, 1), a_end) >= 0),
        jnp.exp(cum_a), 0.0,
    )
    cum2 = cum * LOG2E
    age_row = (pos - start_row).astype(F32)
    packed = jnp.concatenate(
        [cum2, inflow, age_row] + [jnp.zeros((128 - 3 * heads, rows), F32)], axis=0,
    )
    cols[...] = jnp.transpose(packed)
    low_row = lax.broadcasted_iota(jnp.int32, (1, 128), 1) < 64

    for lb in range(lbs):
        h0, h1 = 2 * lb, 2 * lb + 1
        for k, value in enumerate((decay, decay_a)):
            d_send[lb, pl.ds(k, 1), :] = jnp.where(
                low_row,
                jnp.broadcast_to(value[h0 : h0 + 1, :], (1, 128)),
                jnp.broadcast_to(value[h1 : h1 + 1, :], (1, 128)),
            )

    step = 64

    @pl.loop(0, rows // step)
    def _(t):
        r0 = pl.multiple_of(t * step, step)
        age = jnp.broadcast_to(cols[pl.ds(r0, step), 2 * heads : 2 * heads + 1], (step, 128))
        near = [age >= d for d in range(taps)]
        for j in range(lbs + 2):
            lanes = pl.ds(j * 128, 128)
            win = u[pl.ds(r0, step + HALO), pl.ds((j if j < lbs else j + lbs) * 128, 128)]
            if j < lbs:
                wl, wt, wb = lanes, wconv_x, bconv_x
            else:
                wl, wt, wb = pl.ds((j - lbs) * 128, 128), wconv_bc, bconv_bc
            total = jnp.broadcast_to(wb[:, wl], (step, 128))
            for k in range(taps):
                d = taps - 1 - k
                shifted = win if d == 0 else pltpu.roll(win, d, 0)
                term = shifted[HALO:, :] * wt[pl.ds(k, 1), wl]
                total = total + (term if d == 0 else jnp.where(near[d], term, 0.0))
            out = silu(total)
            if j < lbs:
                xc[pl.ds(r0, step), lanes] = out.astype(BF16)
            elif j == lbs:
                bcol[pl.ds(r0, step), :] = out.astype(BF16).astype(F32)
            else:
                ccol[pl.ds(r0, step), :] = out.astype(BF16)

    btf[...] = jnp.transpose(bcol[...])
    btr[...] = btf[...].astype(BF16)

    low_state = lax.broadcasted_iota(jnp.int32, (state, 128), 1) < 64

    def state_of(weight, lb):
        pair = [
            (btf[...] * weight[2 * lb + k : 2 * lb + k + 1, :]).astype(BF16) for k in range(2)
        ]
        both = jnp.dot(
            jnp.concatenate(pair, axis=0), xc[:, pl.ds(lb * 128, 128)],
            preferred_element_type=F32,
        )
        value = jnp.where(low_state, both[0:state, :], both[state:, :])
        return value.astype(BF16).reshape(per, piece, 128)

    for lb in range(lbs):
        s_send[pl.ds(lb * per, per)] = state_of(w_end, lb)
    pl.semaphore_wait(barrier, nseq - 1 + nhead - 1)

    S, D, AB, V, H, PG = range(6)

    def offset(n):
        t, s = n // xs, n % xs
        dz = (zs // 2 + (1 - 2 * (t % 2)) * ((t + 1) // 2)) % zs
        dx = (xs // 2 + (1 - 2 * (s % 2)) * ((s + 1) // 2)) % xs
        return dx, dz

    def copy(kind, src, dst, n, to):
        return pltpu.make_async_remote_copy(
            src_ref=src, dst_ref=dst, send_sem=send_sem.at[kind, n], recv_sem=recv_sem.at[kind, n],
            device_id={"seq": to}, device_id_type=MESH,
        )

    x_order = [(xs // 2 + (1 - 2 * (k % 2)) * ((k + 1) // 2)) % xs for k in range(xs)]
    x_part = [lax.rem(my_x + dx, xs) * zs for dx in x_order]

    def out_copy(kind, n, to):
        if kind == S:
            return copy(S, s_send.at[to], s_buf.at[seq], n, to)
        if kind == D:
            return copy(D, d_send.at[to // per], d_buf.at[seq], n, to)
        if kind == AB:
            return copy(AB, ab_send.at[to], ab_buf.at[seq], n, to)
        if kind == V:
            return copy(V, v_send.at[to], v_buf.at[seq], n, to)
        if kind == H:
            return copy(H, h_send.at[to], h_buf.at[seq], n, to)
        return copy(PG, p_send.at[to], page_out.at[seq], n, to)

    def in_copy(kind, n):
        dx, dz = offset(n)
        frm = ((my_x + xs - dx) % xs) * zs + (my_z + zs - dz) % zs
        buf = (s_buf, d_buf, ab_buf, v_buf, h_buf, page_out)[kind]
        return copy(kind, buf.at[frm], buf.at[frm], n, frm)

    def start_all(*kinds):
        @pl.loop(0, zs - 1)
        def _(t):
            dz = zs // 2 + (1 - 2 * lax.rem(t, 2)) * ((t + 1) // 2)
            z_part = lax.rem(my_z + dz, zs)
            for k in range(xs):
                for kind in kinds:
                    out_copy(kind, t * xs + k, x_part[k] + z_part).start()

        for k in range(xs - 1):
            for kind in kinds:
                out_copy(kind, (zs - 1) * xs + k, x_part[k] + my_z).start()

    def arrive_all(*kinds):
        @pl.loop(0, nseq - 1)
        def _(n):
            for kind in kinds:
                in_copy(kind, n).wait_recv()

    start_all(S, D)
    for lb in range(lbs):
        for kind, weight in enumerate((w_a, w_b)):
            ab_send[pl.ds(lb * per, per), kind] = state_of(weight, lb)
    start_all(AB)
    s_buf[seq] = s_send[seq]
    d_buf[seq] = d_send[lb_me]
    ab_buf[seq] = ab_send[seq]

    tile = 128
    blocks = rows // tile
    for i in range(blocks):
        ri = pl.ds(i * tile, tile)
        reach = (i + 1) * tile
        sc = jnp.dot(ccol[ri, :], btr[:, 0:reach], preferred_element_type=F32)
        gap_i = i * tile + lax.broadcasted_iota(jnp.int32, (tile, reach), 0)
        gap_j = lax.broadcasted_iota(jnp.int32, (tile, reach), 1)
        back = (gap_i - gap_j).astype(F32)
        age = cols[ri, 2 * heads : 2 * heads + 1]
        scores[ri, 0:reach] = jnp.where((back >= 0.0) & (back <= age), sc, 0.0)
    low_t = lax.broadcasted_iota(jnp.int32, (tile, 128), 1) < 64
    for lb in range(lbs):
        lanes = pl.ds(lb * 128, 128)
        gain = jnp.where(low_row, skip_gain[2 * lb], skip_gain[2 * lb + 1])
        for i in range(blocks):
            ri = pl.ds(i * tile, tile)
            reach = (i + 1) * tile
            parts = []
            for hh in range(2):
                h = 2 * lb + hh
                gap = jnp.minimum(cols[ri, h : h + 1] - cum2[h : h + 1, 0:reach], 0.0)
                wgt = (scores[ri, 0:reach] * jnp.exp2(gap) * dt[h : h + 1, 0:reach]).astype(BF16)
                parts.append(jnp.dot(wgt, xc[0:reach, lanes], preferred_element_type=F32))
            y_loc[ri, lanes] = (
                jnp.where(low_t, parts[0], parts[1]) + gain * xc[ri, lanes].astype(F32)
            )

    @pl.loop(0, nseq)
    def _(q):
        kind = jnp.int32(2)
        at = jnp.int32(0)
        who = jnp.int32(prompts)
        for r in range(prompts):
            hit = page_ref[r] == q
            kind = jnp.where(hit, slot[r], kind)
            at = jnp.where(hit, block[r], at)
            who = jnp.where(hit & (block[r] == seq), r, who)
        where_ref[0, q] = kind
        where_ref[1, q] = jnp.clip(at, 0, nseq - 1)
        where_ref[2, q] = who

    v_rows = v_all.shape[1]
    v_all[prompts] = jnp.zeros((v_rows, 128), BF16)
    for r in range(prompts):
        local = jnp.clip(ends[r] - base, 0, rows - 1) + HALO
        for k in range(taps - 1):
            back = taps - 2 - k
            line = u[pl.ds(local - back, 1), :]
            keep = jnp.full((1, 128), ends[r] - back, jnp.int32) >= starts[r]
            for j in range(lbs):
                stage[k * lbs + j : k * lbs + j + 1, :] = jnp.where(
                    keep, line[:, j * 128 : (j + 1) * 128], 0.0
                )
            for j in range(2):
                at = (taps - 1) * lbs + 2 * k + j
                stage[at : at + 1, :] = jnp.where(
                    keep, line[:, (2 * lbs + j) * 128 : (2 * lbs + j + 1) * 128], 0.0
                )
        v_all[r] = stage[...].astype(BF16)

    @pl.loop(0, nseq)
    def _(q):
        v_send[q] = v_all[where_ref[2, q]]

    arrive_all(S, D)

    def advance(i, carried):
        h_all[i] = carried
        h_send[i] = carried.astype(BF16)
        return d_buf[i, 0:1, :] * carried + s_buf[i].astype(F32)

    lax.fori_loop(0, nseq, advance, jnp.zeros((piece, 128), F32))
    start_all(H)
    h_buf[seq] = h_send[seq]
    start_all(V)
    v_buf[seq] = v_send[seq]

    arrive_all(AB)

    @pl.loop(0, nseq)
    def _(q):
        kind = where_ref[0, q]
        at = where_ref[1, q]
        value = ab_buf[at, jnp.where(kind == 1, 1, 0)].astype(F32)
        first = value + d_buf[at, 1:2, :] * h_all[at]
        kinds = jnp.full((piece, 128), kind, jnp.int32)
        p_send[q] = jnp.where(kinds == 0, first, jnp.where(kinds == 1, value, 0.0)).astype(BF16)

    start_all(PG)
    page_out[seq] = p_send[seq]

    tile = 64
    low = lax.broadcasted_iota(jnp.int32, (tile, 128), 1) < 64
    lanes128 = lax.broadcasted_iota(jnp.int32, (tile, 128), 1)
    subl = lax.broadcasted_iota(jnp.int32, (tile, 128), 0)
    for g in range(rows // tile):
        ri = pl.ds(g * tile, tile)
        for lb in range(lbs):
            lanes = pl.ds(lb * 128, 128)
            at = heads + 2 * lb
            scores[ri, lanes] = silu(u[pl.ds(HALO + g * tile, tile), pl.ds(inner + lb * 128, 128)])
            spread[ri, lanes] = jnp.where(low, cols[ri, at : at + 1], cols[ri, at + 1 : at + 2])

    arrive_all(H)
    for g in range(rows // 128):
        line = jnp.zeros((1, 128), F32)
        for s in range(128 // tile):
            ri = pl.ds(g * 128 + s * tile, tile)
            total = jnp.zeros((tile, 128), F32)
            for lb in range(lbs):
                lanes = pl.ds(lb * 128, 128)
                hmat = h_buf[pl.ds(lb * per, per)].reshape(state, 128)
                ac = jnp.dot(ccol[ri, :], hmat, preferred_element_type=F32)
                yv = (y_loc[ri, lanes] + ac * spread[ri, lanes]).astype(BF16).astype(F32)
                gv = yv * scores[ri, lanes]
                gated[ri, lanes] = gv
                total = total + gv * gv
            col = jnp.sum(total, axis=1, keepdims=True)
            line = line + jnp.sum(
                jnp.where(lanes128 == subl + s * tile, col, 0.0), axis=0, keepdims=True
            )
        q_send[g : g + 1, :] = line

    q_copies = []
    for k in range(1, nhead):
        one = pltpu.make_async_remote_copy(
            src_ref=q_send, dst_ref=q_buf.at[head], send_sem=qs_sem.at[k], recv_sem=qr_sem.at[k],
            device_id={"head": (head + k) % nhead}, device_id_type=MESH,
        )
        one.start()
        q_copies.append(one)
    q_buf[head] = q_send[...]

    source = jnp.int32(0)
    found = jnp.int32(0)
    for r in range(prompts):
        hit = page_ref[r] == seq
        source = jnp.where(hit, block[r], source)
        found = jnp.where(hit, 1, found)
    source = jnp.clip(source, 0, nseq - 1)
    arrive_all(V)
    v_out[...] = jnp.where(
        jnp.full(v_out.shape, found, jnp.int32) == 1, v_buf[source].astype(F32), 0.0
    )

    arrive_all(PG)

    @pl.loop(0, nseq - 1)
    def _(n):
        for kind in (S, D, AB, V, H, PG):
            in_copy(kind, n).wait_send()

    for k in range(1, nhead):
        frm = (head + nhead - k) % nhead
        pltpu.make_async_remote_copy(
            src_ref=q_send, dst_ref=q_buf.at[frm], send_sem=qs_sem.at[k], recv_sem=qr_sem.at[k],
            device_id={"head": frm}, device_id_type=MESH,
        ).wait_recv()
    squares = q_buf[0]
    for k in range(1, nhead):
        squares = squares + q_buf[k]
    scale_out[...] = lax.rsqrt(squares / (inner * nhead) + EPS)

    for one in q_copies:
        one.wait_send()


def run_block(u, dt_raw, wconv_x, bconv_x, wconv_bc, bconv_bc, step_bias, decay_log, skip,
              lengths, pages, nseq, nhead):
    rows, inner = dt_raw.shape[0], wconv_x.shape[1]
    state = wconv_bc.shape[1] // 2
    lbs = inner // 128
    piece = state * lbs // nseq
    prompts = lengths.shape[0]
    xs = 4
    tiles = (nseq, piece, 128)
    v_rows = 24
    return pl.pallas_call(
        functools.partial(block_kernel, xs, nseq // xs, nhead),
        name="block",
        out_shape=(
            jax.ShapeDtypeStruct((rows, inner), F32),
            jax.ShapeDtypeStruct((rows // 128, 128), F32),
            jax.ShapeDtypeStruct(tiles, BF16),
            jax.ShapeDtypeStruct((v_rows, 128), F32),
            jax.ShapeDtypeStruct((1,), jnp.int32),
        ),
        in_specs=[smem()] * 5 + [vmem()] * 6,
        out_specs=(vmem(),) * 4 + (smem(),),
        scratch_shapes=[
            pltpu.VMEM((rows, inner), BF16),
            pltpu.VMEM((rows, state), F32),
            pltpu.VMEM((state, rows), F32),
            pltpu.VMEM((rows, state), BF16),
            pltpu.VMEM((state, rows), BF16),
            pltpu.VMEM((rows, max(rows, inner)), F32),
            pltpu.VMEM((rows, inner), F32),
            pltpu.VMEM((rows, 128), F32),
            pltpu.VMEM((v_rows, 128), F32),
            pltpu.VMEM((rows, inner), F32),
            pltpu.VMEM(tiles, BF16),
            pltpu.VMEM((lbs, 2, 128), F32),
            pltpu.VMEM((nseq, 2, piece, 128), BF16),
            pltpu.VMEM((prompts + 1, v_rows, 128), BF16),
            pltpu.VMEM((nseq, v_rows, 128), BF16),
            pltpu.VMEM(tiles, BF16),
            pltpu.VMEM((nseq, 2, 128), F32),
            pltpu.VMEM((nseq, 2, piece, 128), BF16),
            pltpu.VMEM((nseq, v_rows, 128), BF16),
            pltpu.VMEM(tiles, F32),
            pltpu.VMEM(tiles, BF16),
            pltpu.VMEM(tiles, BF16),
            pltpu.VMEM(tiles, BF16),
            pltpu.VMEM((rows // 128, 128), F32),
            pltpu.VMEM((nhead, rows // 128, 128), F32),
            pltpu.SMEM((3, nseq), jnp.int32),
            pltpu.SemaphoreType.DMA((6, nseq)),
            pltpu.SemaphoreType.DMA((6, nseq)),
            pltpu.SemaphoreType.DMA((nhead,)),
            pltpu.SemaphoreType.DMA((nhead,)),
        ],
        compiler_params=pltpu.CompilerParams(
            collective_id=1, has_side_effects=True, vmem_limit_bytes=40 << 20
        ),
    )(lengths, pages, step_bias, decay_log, skip, u, dt_raw, wconv_x, bconv_x, wconv_bc,
      bconv_bc)


def write_kernel(gated, scale_rows, pages, v, gain, n_out, page_out, cx_out, cb_out):
    rows, inner = gated.shape
    lbs = inner // 128
    per = pages.shape[0] // lbs
    state = per * pages.shape[1]
    tile = 64
    lanes128 = lax.broadcasted_iota(jnp.int32, (tile, 128), 1)
    subl = lax.broadcasted_iota(jnp.int32, (tile, 128), 0)
    for g in range(rows // 128):
        for s in range(128 // tile):
            ri = pl.ds(g * 128 + s * tile, tile)
            diag = jnp.where(lanes128 == subl + s * tile, scale_rows[g : g + 1, :], 0.0)
            scale = jnp.sum(diag, axis=1, keepdims=True)
            n_out[ri, :] = (gated[ri, :] * scale * gain[...]).astype(BF16)
    for lb in range(lbs):
        mat = pages[pl.ds(lb * per, per)].reshape(state, 128).astype(F32)
        page_out[pl.ds(lb * 128, 128), :] = jnp.transpose(mat)
    kept = cx_out.shape[0]
    for k in range(kept):
        for j in range(lbs):
            cx_out[k, :, j * 128 : (j + 1) * 128] = v[k * lbs + j : k * lbs + j + 1, :]
        for j in range(2):
            at = kept * lbs + 2 * k + j
            cb_out[k, :, j * 128 : (j + 1) * 128] = v[at : at + 1, :]


def write(gated, scale_rows, pages, v, gain, state, kept):
    rows, inner = gated.shape
    return pl.pallas_call(
        write_kernel,
        name="write",
        out_shape=(
            jax.ShapeDtypeStruct((rows, inner), BF16),
            jax.ShapeDtypeStruct((inner, state), F32),
            jax.ShapeDtypeStruct((kept, 1, inner), F32),
            jax.ShapeDtypeStruct((kept, 1, 2 * state), F32),
        ),
        in_specs=[vmem()] * 5,
        out_specs=(vmem(),) * 4,
        compiler_params=pltpu.CompilerParams(vmem_limit_bytes=8 << 20),
    )(gated, scale_rows, pages, v, gain)


def crowded_pages(
    u, dt_raw, wconv_x, bconv_x, wconv_bc, bconv_bc, step_bias, decay_log, lengths, pages
):
    rows = dt_raw.shape[0]
    heads = step_bias.shape[0]
    inner = wconv_x.shape[1]
    state = wconv_bc.shape[1] // 2
    taps = wconv_x.shape[0]
    prompts = lengths.shape[0]
    nseq = lax.axis_size("seq")
    base = lax.axis_index("seq") * rows
    ends = jnp.cumsum(lengths) - 1
    starts = ends - lengths + 1
    pos = base + jnp.arange(rows, dtype=jnp.int32)
    age = pos - jnp.max(jnp.where(starts[None] <= pos[:, None], starts[None], 0), axis=1)
    weight = jnp.concatenate([wconv_x, wconv_bc], axis=1)[:, : inner + state]
    total = jnp.concatenate([bconv_x, bconv_bc])[None, : inner + state]
    joined = jnp.concatenate([u[:, :inner], u[:, 2 * inner : 2 * inner + state]], axis=1)
    for k in range(taps):
        d = taps - 1 - k
        term = joined[HALO - d : HALO - d + rows] * weight[k][None]
        total = total + jnp.where((age >= d)[:, None], term, 0.0)
    conv = jax.nn.silu(total).astype(BF16)
    x, b = conv[:, :inner], conv[:, inner:]
    dt = jax.nn.softplus(dt_raw[:, :heads] + step_bias[None])
    cum = jnp.cumsum(-dt * jnp.exp(decay_log)[None], axis=0)
    block = ends // rows
    before = jnp.concatenate([jnp.full((1,), -1, block.dtype), block[:-1]])
    after = jnp.concatenate([block[1:], jnp.full((1,), -1, block.dtype)])
    mine = (before == block) & (after == block) & (block == lax.axis_index("seq"))
    at_end = cum[jnp.clip(ends - base, 0, rows - 1)]
    keep = mine[:, None] & (pos[None] >= starts[:, None]) & (pos[None] <= ends[:, None])
    scale = jnp.where(
        keep[:, :, None], jnp.exp(jnp.minimum(at_end[:, None] - cum[None], 0.0)) * dt[None], 0.0
    )
    x_heads = x.reshape(rows, heads, -1).astype(F32)
    weighted = (scale[:, :, :, None] * x_heads[None]).astype(BF16).reshape(prompts, rows, inner)
    finals = jnp.einsum("rjc,jn->rcn", weighted, b, preferred_element_type=F32)
    hits = (pages[None, :] == jnp.arange(nseq, dtype=jnp.int32)[:, None]).astype(BF16)
    pool = jnp.einsum("qr,rcn->qcn", hits, finals.astype(BF16), preferred_element_type=F32)
    moved = lax.all_to_all(pool.astype(BF16), "seq", 0, 0, tiled=True)
    return jnp.sum(moved.astype(F32), axis=0)


def body(
    tokens, weight_x, weight_z, weight_bc, weight_dt, conv_x_weight, conv_x_bias,
    conv_bc_weight, conv_bc_bias, step_bias, decay_log, skip_gain, norm_gain, lengths, page_table,
):
    nseq, nhead = lax.axis_size("seq"), lax.axis_size("head")
    heads = weight_dt.shape[0]
    inner = weight_x.shape[1]
    width = inner // heads
    kept = conv_x_weight.shape[0] - 1
    u, dt_raw = project(tokens, weight_x, weight_z, weight_bc, weight_dt, nseq, nhead)
    gated, scale, pages, v, more = run_block(
        u, dt_raw, conv_x_weight, conv_x_bias[None, :], conv_bc_weight,
        conv_bc_bias[None, :], step_bias, decay_log, skip_gain, lengths, page_table, nseq, nhead,
    )
    normed, page, conv_x, conv_bc = write(
        gated, scale, pages, v, norm_gain[None, :], conv_bc_weight.shape[1] // 2, kept
    )
    page = lax.cond(
        more[0] > 0,
        lambda page, *rest: page + crowded_pages(*rest),
        lambda page, *rest: page,
        page, u, dt_raw, conv_x_weight, conv_x_bias, conv_bc_weight, conv_bc_bias, step_bias,
        decay_log, lengths, page_table,
    )
    return (
        normed, page.reshape(1, heads, width, -1), jnp.swapaxes(conv_x, 0, 1), jnp.swapaxes(conv_bc, 0, 1),
    )


def solution(mesh):
    in_specs = (
        P("seq", "head"), P(None, "head"), P(None, "head"), P(), P("head", None),
        P(None, "head"), P("head"), P(), P(), P("head"), P("head"), P("head"), P("head"),
        P(), P(),
    )
    out_specs = (
        P("seq", "head"), P("seq", "head", None, None), P("seq", None, "head"),
        P("seq", None, None),
    )
    return jax.shard_map(body, mesh=mesh, in_specs=in_specs, out_specs=out_specs, check_vma=False)
```
